32 devices in a mesh: space: 8 (over z, y), mem: 4 (over x, core).
Axes of the slice: x: 2, y: 2, z: 4, core: 2. Of those that a mesh axis runs over, the one named last changes fastest.
Arguments:
- prior_ensemble: float32 [512, 32, 128], P('mem', 'space'), may hold values from -70 to 70
- stencil_factors: float32 [4, 32, 128], P(None, 'space'), may hold values from 0.02 to 0.22
- sea_mask: int32 [32, 128], P('space'), may hold values 0 or 1
- measured_site_positions: int32 [8, 128], P('space'), may hold values from 0 to 511
- measured_data: float32 [1024], P('space'), may hold values from -16 to 16
- measurement_precision: float32 [1024], P('space'), may hold values from 0.5 to 2
- cotangent: float32 [512, 32, 128], P('mem', 'space'), may hold values from -6 to 6
Outputs:
- grad_prior: float32 [512, 32, 128], P('mem', 'space')
- grad_coef: float32 [4, 32, 128], P(None, 'space')
The draws below stay inside these ranges and needn't reach their ends.
Inputs may be any that keep to these rules, and one draw needn't show every extreme that they name: `measured_site_positions`: the flat position row * 128 + column, within its strip of 4 rows, of each observed cell; strip s holds rows s * 4 to (s + 1) * 4 - 1. `sea_mask`: 1 marks a sea cell, 0 a land cell.
All inputs are finite; a program needn't handle non-finite values. No bound on the sum of `sea_mask` on one device may be relied on, other than what follows from the above.
Results may differ from the reference program's by a relative error of at most 0.0003.
Values sent between devices are 32-bit elements; how exact they have to be, the bound alone decides.
A program may use at most 64 MiB of HBM per device.

```python
import math
import jax
import jax.numpy as jnp
from jax import lax

SAMPLE_TOTAL = 512
MESH_LONGITUDES = 128
BAND_LATITUDES = 4
K = 128
ITERS = 2
TILES = 8
MESH_LATITUDES = 32
NOBS = 1024


def draw_prior_ensemble(key, part):
    key_scale, key_noise = jax.random.split(key, 2)
    member_pos = (jnp.arange(SAMPLE_TOTAL, dtype=jnp.float32) + jax.random.uniform(key_scale, (SAMPLE_TOTAL,))) / SAMPLE_TOTAL
    row_pos = jnp.arange(MESH_LATITUDES, dtype=jnp.float32) / MESH_LATITUDES
    scales = 0.3 * 10.0 ** member_pos
    strip_ramp = 3.0 ** row_pos
    noise_field = jax.random.truncated_normal(key_noise, -4.0, 4.0, (SAMPLE_TOTAL, MESH_LATITUDES, MESH_LONGITUDES))
    return (scales[:, None, None] * strip_ramp[None, :, None] * noise_field).astype(jnp.float32)


def with_ends(result, stream_key, least, largest):
    longest = result.shape.index(max(result.shape))
    spots = []
    for shift in (0, 1):
        where = [jax.random.randint(jax.random.fold_in(stream_key, axis), (), 0, length) for axis, length in enumerate(result.shape)]
        where[longest] = (where[longest] + shift) % result.shape[longest]
        spots.append(tuple(where))
    return result.at[spots[0]].set(least).at[spots[1]].set(largest)


def block_levels(own_key, dims, cuts, low, high):
    def one(dim, blocks):
        draws = jax.random.uniform(jax.random.fold_in(jax.random.fold_in(own_key, 6), dim), (blocks,), jnp.float32, low / len(cuts), high / len(cuts))
        return jnp.repeat(jnp.exp(draws), dims[dim] // blocks).reshape((-1,) + (1,) * (len(dims) - dim - 1))

    loudness = one(*cuts[0])
    for cut in cuts[1:]:
        loudness = loudness * one(*cut)
    return loudness


def normal_values(own_key, shape, width, most, pieces=(), kind=jnp.bfloat16):
    gain = block_levels(own_key, shape, pieces, -0.22, 0.18) if pieces else 1.0
    drawn = jax.random.normal(own_key, shape, jnp.float32) * width * gain
    return jnp.minimum(jnp.maximum(drawn, -most), most).astype(kind)


def setup_inputs(seed: int = 0) -> dict:
    splits = jax.random.split(jax.random.key(seed), 8)
    return {
        "prior_ensemble": draw_prior_ensemble(jax.random.fold_in(splits[7], 71), 0),
        "stencil_factors": jnp.clip(0.02 + 0.2 * jax.random.uniform(splits[1], (4, MESH_LATITUDES, MESH_LONGITUDES), jnp.float32) ** block_levels(splits[1], (4, MESH_LATITUDES, MESH_LONGITUDES), ((1, 8),), -0.2, 0.2), 0.02, 0.22),
        "sea_mask": with_ends((jax.random.randint(splits[2], (MESH_LATITUDES, MESH_LONGITUDES), 0, 5) < 4).astype(jnp.int32), jax.random.fold_in(splits[2], 1), 0, 1),
        "measured_site_positions": with_ends(jax.random.randint(splits[3], (TILES, K), 0, BAND_LATITUDES * MESH_LONGITUDES), jax.random.fold_in(splits[3], 1), 0, (BAND_LATITUDES * MESH_LONGITUDES) - 1).astype(jnp.int32),
        "measured_data": normal_values(splits[4], (NOBS,), 4.0, 16.0, ((0, 8),), jnp.float32),
        "measurement_precision": jnp.clip(jnp.exp(math.log(2.0) - 1.3862944 * jax.random.uniform(splits[5], (NOBS,), jnp.float32) ** block_levels(splits[5], (NOBS,), ((0, 8),), -0.2, 0.2)), 0.5, 2.0),
        "cotangent": normal_values(splits[6], (SAMPLE_TOTAL, MESH_LATITUDES, MESH_LONGITUDES), 1.0, 6.0, ((0, 4), (1, 8)), jnp.float32),
    }


highest = lax.Precision.HIGHEST

def product(left_side, right_side):
    return jnp.dot(left_side, right_side, precision=highest, preferred_element_type=jnp.float32)

def substep(state_band_piece, stencil_factors, ocean_share):
    padded = jnp.pad(state_band_piece, ((0, 0), (1, 1), (1, 1)))
    northern = padded[:, :-2, 1:-1]
    southern = padded[:, 2:, 1:-1]
    western = padded[:, 1:-1, :-2]
    eastern = padded[:, 1:-1, 2:]
    advanced = state_band_piece + stencil_factors[0] * (northern - state_band_piece) + stencil_factors[1] * (southern - state_band_piece) + stencil_factors[2] * (western - state_band_piece) + stencil_factors[3] * (eastern - state_band_piece)
    return ocean_share * advanced

def predicted_samples(state_band_piece, stencil_factors, ocean_share):
    return substep(substep(state_band_piece, stencil_factors, ocean_share), stencil_factors, ocean_share)

def corrected_state(predict_advance, measured_site_positions, measured_data, measurement_precision):
    covariance_factor_matrix = jnp.sqrt(jnp.float32(SAMPLE_TOTAL - 1))
    sample_average = lax.optimization_barrier(jnp.mean(predict_advance, axis=0))
    sample_deviations = (predict_advance - sample_average) / covariance_factor_matrix
    mesh_bands = predict_advance.reshape(SAMPLE_TOTAL, MESH_LATITUDES // BAND_LATITUDES, BAND_LATITUDES * MESH_LONGITUDES)
    where_seen = jnp.broadcast_to(measured_site_positions[None, :, :], (SAMPLE_TOTAL, MESH_LATITUDES // BAND_LATITUDES, K))
    picked = jnp.take_along_axis(mesh_bands, where_seen, axis=2).reshape(SAMPLE_TOTAL, NOBS)
    observed = picked + 0.5 * jnp.tanh(picked)
    observed_mean = lax.optimization_barrier(jnp.mean(observed, axis=0))
    obs_anom = (observed - observed_mean) * measurement_precision / covariance_factor_matrix
    innovation = measurement_precision * (measured_data - observed_mean)
    identity = jnp.eye(SAMPLE_TOTAL, dtype=jnp.float32)
    system = identity + product(obs_anom, obs_anom.T)
    norm_scale = jnp.sqrt(jnp.sum(system * system))
    obs_pull = product(obs_anom, innovation)
    approach = system / norm_scale
    polar = identity
    for iteration in range(ITERS):
        factor = 1.5 * identity - 0.5 * product(polar, approach)
        approach = product(approach, factor)
        polar = product(factor, polar)
    transform = polar / jnp.sqrt(norm_scale)
    mean_weights = product(transform, product(transform, obs_pull))
    mixing = covariance_factor_matrix * transform + mean_weights[None, :]
    flattened = sample_deviations.reshape(SAMPLE_TOTAL, MESH_LATITUDES * MESH_LONGITUDES)
    return sample_average + product(mixing, flattened).reshape(SAMPLE_TOTAL, MESH_LATITUDES, MESH_LONGITUDES)

def reference(prior_ensemble, stencil_factors, sea_mask, measured_site_positions, measured_data, measurement_precision, cotangent):
    ocean_share = sea_mask.astype(jnp.float32)
    gathered_samples = prior_ensemble.reshape(SAMPLE_TOTAL // 64, 64, MESH_LATITUDES, MESH_LONGITUDES)
    predict_advance = lax.map(lambda sample_band_piece: predicted_samples(sample_band_piece, stencil_factors, ocean_share), gathered_samples).reshape(SAMPLE_TOTAL, MESH_LATITUDES, MESH_LONGITUDES)
    advance_product, cotangent_mapping = jax.vjp(lambda state_argument: corrected_state(state_argument, measured_site_positions, measured_data, measurement_precision), predict_advance)
    field_bar, = cotangent_mapping(cotangent)

    def block_grad(block_pair):
        sample_band_piece, block_bar = block_pair
        overall_answer, reverse_sweep = jax.vjp(lambda state_argument, stencil_argument: predicted_samples(state_argument, stencil_argument, ocean_share), sample_band_piece, stencil_factors)
        return reverse_sweep(block_bar)
    prior_bar, coef_parts = lax.map(block_grad, (gathered_samples, field_bar.reshape(SAMPLE_TOTAL // 64, 64, MESH_LATITUDES, MESH_LONGITUDES)))
    return (prior_bar.reshape(SAMPLE_TOTAL, MESH_LATITUDES, MESH_LONGITUDES), lax.optimization_barrier(jnp.sum(coef_parts, axis=0)) / jnp.sqrt(jnp.float32(SAMPLE_TOTAL)))
```

```python
import functools
import jax
import jax.numpy as jnp
from jax import lax
from jax.experimental import pallas as pl
from jax.experimental.pallas import tpu as pltpu
from jax.sharding import PartitionSpec as P

MESH = pl.DeviceIdType.MESH
F32 = jnp.float32
BF16 = jnp.bfloat16
VMEM_SPEC = pl.BlockSpec(memory_space=pltpu.VMEM)


def remote(src, dst, send, recv, s, m):
    return pltpu.make_async_remote_copy(
        src_ref=src, dst_ref=dst, send_sem=send, recv_sem=recv, device_id=(s, m), device_id_type=MESH
    )


def split(x):
    lead = x.astype(BF16)
    return lead, (x - lead.astype(F32)).astype(BF16)


def split3(x):
    lead = x.astype(BF16)
    rest = x - lead.astype(F32)
    middle = rest.astype(BF16)
    return lead, middle, (rest - middle.astype(F32)).astype(BF16)


def plain(a, b):
    return jnp.dot(a, b, preferred_element_type=F32)


def plain_t(a, b):
    return lax.dot_general(a, b, (((1,), (1,)), ((), ())), preferred_element_type=F32)


def mm3(a, b):
    return plain(a[0], b[0]) + (plain(a[0], b[1]) + plain(a[1], b[0]))


def mm3_t(a, b):
    return plain_t(a[0], b[0]) + (plain_t(a[0], b[1]) + plain_t(a[1], b[0]))


def whole_sum(x):
    return jnp.sum(jnp.sum(x, axis=0, keepdims=True), axis=1, keepdims=True)


def eye(size):
    return lax.broadcasted_iota(jnp.int32, (size, size), 0) == lax.broadcasted_iota(
        jnp.int32, (size, size), 1
    )


class Sizes:
    def __init__(self, n_space, n_mem, prior, sites):
        self.n_space, self.n_mem = n_space, n_mem
        self.members, self.rows, self.cols = prior.shape
        self.total = self.members * n_mem
        self.sites = sites.shape[-1]
        self.height = self.members // n_space
        self.near = 2 if n_space % 2 == 0 else 1
        self.far = n_space // self.near
        self.half = 2 if n_mem % 2 == 0 else 1
        self.wide = n_mem // self.half
        self.group = max(1, self.far // 4)
        self.groups = self.far // self.group


def scratch_of(z):
    dma = pltpu.SemaphoreType.DMA
    ext = z.rows + 4
    v = lambda *shape: pltpu.VMEM(shape, F32)
    b = lambda *shape: pltpu.VMEM(shape, BF16)
    square = (z.total, z.total)
    return dict(
        pext=v(ext, z.members, z.cols),
        aux=v(ext, 8, z.cols),
        cotf=v(z.rows, z.total, z.cols),
        chi=b(z.rows, z.total, z.cols),
        clo=b(z.rows, z.total, z.cols),
        fext=v(z.rows + 2, z.members, z.cols),
        state=v(z.rows, z.members, z.cols),
        hot=b(z.rows, z.cols, z.sites),
        obsf=v(z.total, z.sites),
        tanh=v(z.members, z.sites),
        anom=v(z.total, z.sites),
        innov=v(8, z.sites),
        sums=v(z.n_mem, 8 * pl.cdiv(z.rows, 8), z.cols),
        dmat=v(z.n_mem, z.members, z.members),
        dx=v(z.n_mem, z.members, z.members),
        rsrc=v(z.n_space, z.height, z.total),
        rbuf=v(z.n_space, z.height, z.total),
        vec=v(8, z.members),
        vbuf=v(z.n_space, 8, z.members),
        vout=v(z.n_mem, 8, z.members),
        out=v(z.n_mem, z.far, z.near, z.height, z.total),
        f=v(*square),
        f2=v(*square),
        t=v(*square),
        s=v(*square),
        u=v(*square),
        y=v(*square),
        vcol=v(z.total, 8),
        sbext=v(ext, z.members, z.cols),
        fbar=v(z.rows + 2, z.members, z.cols),
        cbuf=v(z.n_mem, 4 * z.rows, z.cols),
        own=dma((2, z.rows)),
        keep=dma((2,)),
        halo=dma((2, 2)),
        aux_halo=dma((2, 2)),
        bar_halo=dma((2, 2)),
        cot_sem=dma((2, z.half, z.wide)),
        obs_sem=dma((2, z.half, z.wide)),
        sum_sem=dma((2, z.n_mem)),
        d_sem=dma((2, z.n_mem)),
        rs_sem=dma((2, z.n_space)),
        v_sem=dma((2, z.n_space)),
        vg_sem=dma((2, z.n_mem)),
        c_sem=dma((2, z.n_mem)),
        a_sem=dma((2, z.far)),
        b_sem=dma((2, z.near, z.groups)),
        p_sem=dma((2, z.wide, z.near, z.groups)),
        q_sem=dma((2, z.half, z.wide, z.near, z.groups)),
    )


class Step:
    def __init__(self, z, refs):
        self.z = z
        self.__dict__.update(refs)
        self.s_id, self.m_id = lax.axis_index("space"), lax.axis_index("mem")
        self.waits = []

    def finish_sends(self):
        for copy, when in self.waits:
            if when is None:
                copy.wait_send()
            else:
                pl.when(when)(copy.wait_send)

    def barrier(self):
        z, s, m = self.z, self.s_id, self.m_id
        peers = [(lax.rem(s + k, z.n_space), m) for k in range(1, z.n_space)]
        peers += [(s, lax.rem(m + k, z.n_mem)) for k in range(1, z.n_mem)]
        barrier = pltpu.get_barrier_semaphore()
        for peer in peers:
            pl.semaphore_signal(barrier, inc=1, device_id=peer, device_id_type=MESH)
        return lambda: pl.semaphore_wait(barrier, len(peers))

    def halo_send(self, ref, sem):
        z, s, m = self.z, self.s_id, self.m_id
        has_low, has_high = s > 0, s < z.n_space - 1
        r = z.rows
        up = remote(ref.at[pl.ds(r, 2)], ref.at[pl.ds(0, 2)], sem.at[0, 0], sem.at[1, 0], s + 1, m)
        down = remote(
            ref.at[pl.ds(2, 2)], ref.at[pl.ds(r + 2, 2)], sem.at[0, 1], sem.at[1, 1], s - 1, m
        )
        pl.when(has_high)(up.start)
        pl.when(has_low)(down.start)
        self.waits += [(up, has_high), (down, has_low)]

        def wait():
            pl.when(has_low)(up.wait_recv)
            pl.when(has_high)(down.wait_recv)

        return wait

    def pair_gather(self, part, sem):
        z, s, m = self.z, self.s_id, self.m_id
        p, q = m // z.half, lax.rem(m, z.half)
        across = [lax.rem(p + k, z.wide) * z.half + q for k in range(1, z.wide)]
        beside = [p * z.half + lax.rem(q + k, z.half) for k in range(1, z.half)]
        mine = part(m)
        hops, sides = [], []
        for k, to in enumerate(across):
            hops.append(remote(mine, mine, sem.at[0, 0, k + 1], sem.at[1, 0, k + 1], s, to))
            hops[-1].start()
        for k, to in enumerate(beside):
            sides.append(remote(mine, mine, sem.at[0, k + 1, 0], sem.at[1, k + 1, 0], s, to))
            sides[-1].start()

        def forward():
            for kp, hop in enumerate(hops):
                hop.wait_recv()
                piece = part(lax.rem(p + z.wide - kp - 1, z.wide) * z.half + q)
                for k, to in enumerate(beside):
                    copy = remote(
                        piece, piece, sem.at[0, k + 1, kp + 1], sem.at[1, k + 1, kp + 1], s, to
                    )
                    copy.start()
                    sides.append(copy)

        def wait():
            for copy in sides:
                copy.wait_recv()
            self.waits.extend((copy, None) for copy in hops + sides)

        return forward, wait

    def mem_send(self, ref, sem):
        z, s, m = self.z, self.s_id, self.m_id
        copies = []
        for k in range(1, z.n_mem):
            to = lax.rem(m + k, z.n_mem)
            copies.append(remote(ref.at[m], ref.at[m], sem.at[0, k], sem.at[1, k], s, to))
            copies[-1].start()

        def wait():
            for copy in copies:
                copy.wait_recv()
            self.waits.extend((copy, None) for copy in copies)

        return wait


    def coefficients(self, e):
        z = self.z
        c = [self.aux[e, k : k + 1, :] for k in range(4)]
        sea = self.aux[e, 4:5, :]
        lane = lax.broadcasted_iota(jnp.int32, (1, z.cols), 1)
        keep = sea * (1.0 - c[0] - c[1] - c[2] - c[3])
        west = jnp.where(lane == 0, 0.0, c[2])
        east = jnp.where(lane == z.cols - 1, 0.0, c[3])
        return keep, sea * c[0], sea * c[1], sea * west, sea * east

    def chunks(self):
        size = min(32, self.z.members)
        return [pl.ds(k, size) for k in range(0, self.z.members, size)]

    def advance(self, src, first, dst, count):
        z = self.z
        for i in range(count):
            keep, north, south, west, east = self.coefficients(first + i)
            for part in self.chunks():
                v = src[i + 1, part, :]
                dst[i, part, :] = (
                    keep * v
                    + north * src[i, part, :]
                    + south * src[i + 2, part, :]
                    + west * pltpu.roll(v, 1, 1)
                    + east * pltpu.roll(v, z.cols - 1, 1)
                )

    def observe(self):
        z = self.z
        picked = jnp.zeros((z.members, z.sites), F32)
        for r in range(z.rows):
            for piece in split3(self.state[r]):
                picked = picked + plain(piece, self.hot[r])
        tanh = jnp.tanh(picked)
        self.tanh[...] = tanh
        return picked + 0.5 * tanh

    def mark_sites(self):
        z = self.z
        for r in range(z.rows):
            cell = lax.broadcasted_iota(jnp.int32, (z.cols, z.sites), 0) + r * z.cols
            self.hot[r] = jnp.where(cell == self.sites[...], 1.0, 0.0).astype(BF16)


    def reduce_scatter(self):
        z, s, m = self.z, self.s_id, self.m_id
        copies = []
        for k in range(1, z.n_space):
            to = lax.rem(s + k, z.n_space)
            copies.append(
                remote(self.rsrc.at[to], self.rbuf.at[s], self.rs_sem.at[0, k], self.rs_sem.at[1, k], to, m)
            )
            copies[-1].start()
        tiny = []
        for k in range(1, z.n_space):
            to = lax.rem(s + k, z.n_space)
            tiny.append(remote(self.vec, self.vbuf.at[s], self.v_sem.at[0, k], self.v_sem.at[1, k], to, m))
            tiny[-1].start()
        self.rbuf[s] = self.rsrc[s]
        self.vbuf[s] = self.vec[...]
        for copy in copies:
            copy.wait_recv()
        total = self.rbuf[0]
        for k in range(1, z.n_space):
            total = total + self.rbuf[k]
        self.out[m, s // z.near, lax.rem(s, z.near)] = total
        self.waits += [(copy, None) for copy in copies + tiny]

        def small():
            for copy in tiny:
                copy.wait_recv()
            vec = self.vbuf[0]
            for k in range(1, z.n_space):
                vec = vec + self.vbuf[k]
            self.vout[m] = vec
            return self.mem_send(self.vout, self.vg_sem)

        return small

    def flow(self, which_b, start, index, kb, beside_b):
        z, s, m = self.z, self.s_id, self.m_id
        p, q = m // z.half, lax.rem(m, z.half)
        piece = self.out.at[m, pl.ds(start, z.group), which_b]
        to_send = []
        for kp in range(1, z.wide):
            to_send.append((
                self.p_sem.at[0, kp, kb, index], self.p_sem.at[1, kp, kb, index],
                s, lax.rem(p + kp, z.wide) * z.half + q,
            ))
        if beside_b:
            for k in range(1, z.near):
                to = (s // z.near) * z.near + lax.rem(which_b + k, z.near)
                to_send.append((self.b_sem.at[0, k, index], self.b_sem.at[1, k, index], to, m))
        for kq in range(1, z.half):
            to_send.append((
                self.q_sem.at[0, kq, 0, kb, index], self.q_sem.at[1, kq, 0, kb, index],
                s, p * z.half + lax.rem(q + kq, z.half),
            ))
        for item in to_send:
            copy = remote(piece, piece, *item)
            copy.start()
            self.waits.append((copy, None))

    def all_gather(self, small):
        z, s, m = self.z, self.s_id, self.m_id
        a, b = s // z.near, lax.rem(s, z.near)
        p, q = m // z.half, lax.rem(m, z.half)
        out = self.out
        stage_a = []
        for k in range(1, z.far):
            to = lax.rem(a + k, z.far)
            copy = remote(
                out.at[m, a, b], out.at[m, a, b], self.a_sem.at[0, k], self.a_sem.at[1, k],
                to * z.near + b, m,
            )
            copy.start()
            stage_a.append(copy)
        if z.group == 1:
            a_steps = [([], a)] + [
                ([stage_a[k - 1]], lax.rem(a + z.far - k, z.far)) for k in range(1, z.far)
            ]
        else:
            a_steps = [(stage_a if g == 0 else [], g * z.group) for g in range(z.groups)]
        steps_b = []
        small_wait = None
        for index, (needs, start) in enumerate(a_steps):
            for copy in needs:
                copy.wait_recv()
            steps_b.append((start, index))
            self.flow(b, start, index, 0, True)
            if index == 0:
                small_wait = small()
        self.waits += [(copy, None) for copy in stage_a]
        for start, index in steps_b:
            for kb in range(1, z.near):
                from_b = lax.rem(b + z.near - kb, z.near)
                piece = out.at[m, pl.ds(start, z.group), from_b]
                remote(
                    piece, piece, self.b_sem.at[0, kb, index], self.b_sem.at[1, kb, index], s, m
                ).wait_recv()
                self.flow(from_b, start, index, kb, False)
        for start, index in steps_b:
            for kb in range(z.near):
                which_b = lax.rem(b + z.near - kb, z.near)
                for kp in range(1, z.wide):
                    from_p = lax.rem(p + z.wide - kp, z.wide)
                    piece = out.at[from_p * z.half + q, pl.ds(start, z.group), which_b]
                    remote(
                        piece, piece, self.p_sem.at[0, kp, kb, index], self.p_sem.at[1, kp, kb, index], s, m
                    ).wait_recv()
                    for kq in range(1, z.half):
                        copy = remote(
                            piece, piece,
                            self.q_sem.at[0, kq, kp, kb, index], self.q_sem.at[1, kq, kp, kb, index],
                            s, p * z.half + lax.rem(q + kq, z.half),
                        )
                        copy.start()
                        self.waits.append((copy, None))
        for start, index in steps_b:
            for kb in range(z.near):
                which_b = lax.rem(b + z.near - kb, z.near)
                for kp in range(z.wide):
                    from_p = lax.rem(p + z.wide - kp, z.wide)
                    for kq in range(1, z.half):
                        from_q = lax.rem(q + z.half - kq, z.half)
                        piece = out.at[from_p * z.half + from_q, pl.ds(start, z.group), which_b]
                        remote(
                            piece, piece,
                            self.q_sem.at[0, kq, kp, kb, index], self.q_sem.at[1, kq, kp, kb, index], s, m,
                        ).wait_recv()
        small_wait()


    def holds_gram(self, k):
        n = self.z.n_mem
        if 2 * k < n:
            return True
        if 2 * k > n:
            return False
        return None

    def pack(self, scale):
        z, m = self.z, self.m_id
        lane8 = lax.broadcasted_iota(jnp.int32, (z.members, z.members), 1)
        mean = jnp.zeros((1, z.sites), F32)
        for k in range(z.n_mem):
            mean = mean + jnp.sum(self.obsf[k * z.members : (k + 1) * z.members, :], axis=0, keepdims=True)
        mean = mean / z.total
        prec = self.prec[...]
        innov = prec * (self.data[...] - mean)
        self.innov[0:1, :] = innov
        self.anom[...] = (self.obsf[...] - mean) * (prec / scale)
        blocks = [pl.ds(pl.multiple_of(lax.rem(m + k, z.n_mem) * z.members, z.members), z.members) for k in range(z.n_mem)]
        mine = self.anom[blocks[0], :]
        mine_split = split(mine)
        pull = jnp.sum(mine * innov, axis=1, keepdims=True)
        total = self.sums[0]
        for k in range(1, z.n_mem):
            total = total + self.sums[k]
        lacks = [
            (self.sums[k] / z.members - total / z.total) / scale for k in range(z.n_mem)
        ]
        terms = []
        lead = [jnp.concatenate([lacks[k][r : r + 1] for k in range(z.n_mem)] + [jnp.zeros((-z.n_mem % 8, z.cols), F32)] * (z.n_mem % 8 > 0), axis=0) for r in range(z.rows)]
        for r in range(z.rows):
            a = split(lead[r])
            b = (self.chi[r], self.clo[r])
            terms.append(mm3_t(a, b))
        term = terms[0]
        for other in terms[1:]:
            term = term + other
        self.corr[...] = term
        mean_bar = jnp.zeros((z.members, 1), F32)
        diagonal = eye(z.members)
        upper = lax.broadcasted_iota(jnp.int32, (z.members, z.members), 0) <= lane8
        for k in range(z.n_mem):
            b = blocks[k]
            cross = self.dmat[k] + self.pick_row(m, b)
            mean_bar = mean_bar + jnp.sum(cross, axis=1, keepdims=True)
            kind = self.holds_gram(k)
            gram = mm3_t(mine_split, split(self.anom[b, :])) if (k == 0 or kind is not False) else None
            if k == 0:
                sym = 0.5 * (cross + cross.T)
                own = jnp.sum(jnp.where(diagonal, sym, 0.0), axis=1, keepdims=True)
                block = jnp.where(upper, gram, sym)
            elif kind is True:
                block = gram
            else:
                there = lax.rem(m + k, z.n_mem)
                other = self.dx[k] + self.pick_row(there, blocks[0])
                block = 0.5 * (cross + other.T)
                if kind is None:
                    block = jnp.where(m < z.n_mem // 2, gram, block)
            self.rsrc[:, :, b] = block.reshape(z.n_space, z.height, z.members)
        lane = lax.broadcasted_iota(jnp.int32, (z.members, z.members), 1)
        columns = jnp.where(lane == 0, pull, jnp.where(lane == 1, mean_bar, jnp.where(lane == 2, own, 0.0)))
        self.vec[...] = columns.T[:8]

    def pick_row(self, which, cols):
        z = self.z
        rows = lax.broadcasted_iota(jnp.int32, (self.corr.shape[0], z.members), 0)
        return jnp.sum(jnp.where(rows == which, self.corr[:, cols], 0.0), axis=0, keepdims=True)

    def unpack(self, system, cross):
        z = self.z
        n = z.n_mem
        col = lambda k: slice(k * z.members, (k + 1) * z.members)
        lower = lax.broadcasted_iota(jnp.int32, (z.members, z.members), 0) > lax.broadcasted_iota(
            jnp.int32, (z.members, z.members), 1
        )
        diagonal = eye(z.members)
        read = lambda i, j: self.out[i, :, :, :, col(j)].reshape(z.members, z.members)
        for i in range(n):
            block = read(i, i)
            turned = block.T
            system[col(i), col(i)] = jnp.where(lower, turned, block) + diagonal.astype(F32)
            sym = jnp.where(lower, block, turned)
            cross[col(i), col(i)] = jnp.where(diagonal, self.vout[i, 2:3, :], sym)
            for j in range(i + 1, n):
                one, two = read(i, j), read(j, i)
                k = j - i
                gram_first = self.holds_gram(k)
                if gram_first is None:
                    gram_first = i < n // 2
                gram, sym = (one, two.T) if gram_first else (two.T, one)
                system[col(i), col(j)] = gram
                system[col(j), col(i)] = gram.T
                cross[col(i), col(j)] = sym
                cross[col(j), col(i)] = sym.T


    def analyse(self, scale):
        z, m = self.z, self.m_id
        total = z.total
        f_ref, f2_ref, t_ref, s_ref, u_ref, y_ref = self.f, self.f2, self.t, self.s, self.u, self.y
        offset = pl.multiple_of(m * z.members, z.members)
        mine = pl.ds(offset, z.members)
        self.unpack(f_ref, s_ref)
        identity = eye(total).astype(F32)
        norm = jnp.sqrt(whole_sum(f_ref[...] * f_ref[...]))
        root = jnp.sqrt(norm)
        f_ref[...] = 1.5 * identity - (0.5 / norm) * f_ref[...]
        f_split = split(f_ref[...])
        f2_ref[...] = mm3(f_split, f_split)
        f2_split = split(f2_ref[...])
        t_ref[...] = (1.5 * f_ref[...] + mm3(f2_split, split(f2_ref[...] - 1.5 * f_ref[...]))) / root
        t_split = split(t_ref[...])
        rows = jnp.concatenate([self.vout[k] for k in range(z.n_mem)], axis=1)
        rows = jnp.where(lax.broadcasted_iota(jnp.int32, rows.shape, 0) == 3, 1.0, rows)
        first = mm3(split(rows), t_split)
        second = mm3(split(first), t_split)
        turn = lambda x: x.T
        rows_t, first_t = turn(rows), turn(first)
        self.vcol[...] = turn(second)
        pull, mean_bar = rows[0:1], rows[1:2]
        weight = scale * s_ref[...] + 0.5 * (
            rows_t[:, 1:2] * first[0:1]
            + first_t[:, 0:1] * mean_bar
            + first_t[:, 1:2] * pull
            + rows_t[:, 0:1] * first[1:2]
        )
        scale_bar = -0.5 * whole_sum(weight * t_ref[...]) / norm
        s_ref[...] = weight / root
        s_split = split(s_ref[...])
        u_ref[...] = mm3(s_split, f2_split)
        y_ref[...] = mm3(s_split, split(2.0 * f2_ref[...] - 1.5 * f_ref[...]))
        y_ref[...] = 0.5 * (y_ref[...] + y_ref[...].T)
        approach = 1.5 * s_ref[...] - 1.5 * u_ref[...]
        approach = whole_sum(
            approach * (3.0 * identity - 2.0 * f_ref[...])
            + 2.0 * y_ref[...] * (3.0 * f_ref[...] - 2.0 * f2_ref[...])
        )
        scale_bar = scale_bar + 0.5 * approach / norm

        centred = lambda ref: ref[mine, :] - jnp.sum(ref[...], axis=0, keepdims=True) / total
        f_mine = centred(f_ref)
        bar = 1.5 * centred(s_ref) - 0.75 * (centred(u_ref) + mm3(split(centred(f2_ref)), s_split))
        bar = bar + mm3(split(centred(y_ref)), f_split) + mm3(split(f_mine), split(y_ref[...]))
        unit = (
            lax.broadcasted_iota(jnp.int32, (z.members, total), 0) + offset
            == lax.broadcasted_iota(jnp.int32, (z.members, total), 1)
        ).astype(F32) - 1.0 / total
        system_mine = norm * (3.0 * unit - 2.0 * f_mine)
        sym = 2.0 * (-0.5 * bar + scale_bar * system_mine) / norm
        pull_bar = second[1:2]
        sym = sym - (scale / total) * pull_bar
        pull_mine = self.vcol[mine, 1:2] - jnp.sum(pull_bar, axis=1, keepdims=True) / total
        mix = t_ref[mine, :] + self.vcol[mine, 0:1] / scale
        row_weights = first[3:4] + jnp.sum(second[0:1], axis=1, keepdims=True) / scale
        mix = mix + (1.0 - row_weights) / total
        observed = (self.prec[...] / scale) * (
            mm3(split(sym), split(self.anom[...])) + pull_mine * self.innov[0:1, :]
        )
        tanh = self.tanh[...]
        picked = observed * (1.0 + 0.5 * (1.0 - tanh * tanh))
        return split(mix), split(picked)


    def pull_back(self, src, first, dst, count, to_sea):
        z = self.z
        for i in range(count):
            e = first + i
            c = [self.aux[e, k : k + 1, :] for k in range(4)]
            lane = lax.broadcasted_iota(jnp.int32, (1, z.cols), 1)
            keep = 1.0 - c[0] - c[1] - c[2] - c[3]
            from_south, from_north = self.aux[e + 1, 0:1, :], self.aux[e - 1, 1:2, :]
            sea = self.aux[e, 4:5, :]
            east = pltpu.roll(jnp.broadcast_to(jnp.where(lane == 0, 0.0, c[2]), (8, z.cols)), z.cols - 1, 1)[:1]
            west = pltpu.roll(jnp.broadcast_to(jnp.where(lane == z.cols - 1, 0.0, c[3]), (8, z.cols)), 1, 1)[:1]
            if to_sea:
                keep, from_south, from_north = sea * keep, sea * from_south, sea * from_north
                east, west = sea * east, sea * west
            for part in self.chunks():
                v = src[i + 1, part, :]
                dst[i, part, :] = (
                    keep * v
                    + from_south * src[i + 2, part, :]
                    + from_north * src[i, part, :]
                    + east * pltpu.roll(v, z.cols - 1, 1)
                    + west * pltpu.roll(v, 1, 1)
                )

    def coefficient_terms(self, weight, w0, field, f0):
        z = self.z
        lane = lax.broadcasted_iota(jnp.int32, (1, z.cols), 1)
        rows = []
        for r in range(z.rows):
            sums = [0.0] * 5
            for part in self.chunks():
                w = weight[w0 + r, part, :]
                c = field[f0 + r, part, :]
                terms = [
                    w * field[f0 + r - 1, part, :],
                    w * field[f0 + r + 1, part, :],
                    w * pltpu.roll(c, 1, 1),
                    w * pltpu.roll(c, z.cols - 1, 1),
                    w * c,
                ]
                sums = [x + y for x, y in zip(sums, terms)]
            north, south, west, east, own = [jnp.sum(x, axis=0, keepdims=True) for x in sums]
            west = jnp.where(lane == 0, 0.0, west)
            east = jnp.where(lane == z.cols - 1, 0.0, east)
            rows.append([north - own, south - own, west - own, east - own])
        return rows


def kernel(z, *refs):
    names = ["prior", "cot", "stencil", "sea", "sites", "data", "prec", "grad", "coef"]
    names += list(scratch_of(z)) + ["corr"]
    g = Step(z, dict(zip(names, refs)))
    scale = jnp.sqrt(jnp.float32(z.total - 1))
    s, m = g.s_id, g.m_id
    r, ext = z.rows, z.rows + 4
    mine = pl.ds(pl.multiple_of(m * z.members, z.members), z.members)

    loads = []
    for i in range(r):
        loads.append(pltpu.make_async_copy(g.prior.at[i], g.pext.at[2 + i], g.own.at[0, i]))
    for i in range(r):
        loads.append(pltpu.make_async_copy(g.cot.at[i], g.cotf.at[i, mine], g.own.at[1, i]))
    for copy in loads:
        copy.start()
    for e in (0, 1, ext - 2, ext - 1):
        g.pext[e] = jnp.zeros((z.members, z.cols), F32)
        g.sbext[e] = jnp.zeros((z.members, z.cols), F32)
        g.aux[e] = jnp.zeros((8, z.cols), F32)
    for i in range(r):
        g.aux[2 + i, 0:4, :] = g.stencil[:, i, :]
        g.aux[2 + i, 4:5, :] = g.sea[i : i + 1, :].astype(F32)
        g.aux[2 + i, 5:8, :] = jnp.zeros((3, z.cols), F32)
    entered = g.barrier()
    for copy in loads[:r]:
        copy.wait()
    entered()
    halo = g.halo_send(g.pext, g.halo)
    aux_halo = g.halo_send(g.aux, g.aux_halo)
    for copy in loads[r:]:
        copy.wait()
    cot_forward, cot_wait = g.pair_gather(lambda which: g.cotf.at[:, pl.ds(pl.multiple_of(which * z.members, z.members), z.members)], g.cot_sem)
    g.mark_sites()
    aux_halo()
    cot_forward()
    halo()

    g.advance(g.pext, 1, g.fext, r + 2)
    g.advance(g.fext, 2, g.state, r)
    g.obsf[mine, :] = g.observe()
    obs_forward, obs_wait = g.pair_gather(lambda which: g.obsf.at[pl.ds(pl.multiple_of(which * z.members, z.members), z.members)], g.obs_sem)
    own = [jnp.sum(g.state[i], axis=0, keepdims=True) for i in range(r)]
    own += [jnp.zeros((-r % 8, z.cols), F32)] * (r % 8 > 0)
    g.sums[m] = jnp.concatenate(own, axis=0)
    sums_wait = g.mem_send(g.sums, g.sum_sem)

    cot_wait()
    for i in range(r):
        g.chi[i], g.clo[i] = split(g.cotf[i])
    dev = [split((g.state[i] - own[i] / z.members) / scale) for i in range(r)]
    d_copies = []
    order = [k for k in range(1, z.n_mem) if 2 * k <= z.n_mem] + [0] + [k for k in range(1, z.n_mem) if 2 * k > z.n_mem]
    for k in order:
        there = lax.rem(m + k, z.n_mem)
        rows = pl.ds(pl.multiple_of(there * z.members, z.members), z.members)
        part = mm3_t(dev[0], (g.chi[0, rows, :], g.clo[0, rows, :]))
        for i in range(1, r):
            part = part + mm3_t(dev[i], (g.chi[i, rows, :], g.clo[i, rows, :]))
        g.dmat[k] = part
        if 0 < 2 * k <= z.n_mem:
            back = z.n_mem - k
            copy = remote(g.dmat.at[k], g.dx.at[back], g.d_sem.at[0, k], g.d_sem.at[1, k], s, there)
            copy.start()
            d_copies.append(copy)
    obs_forward()
    sums_wait()
    obs_wait()
    for copy in d_copies:
        copy.wait_recv()
    g.waits += [(copy, None) for copy in d_copies]
    g.pack(scale)
    small = g.reduce_scatter()
    g.all_gather(small)

    mix, picked = g.analyse(scale)
    for i in range(r):
        mark = g.hot[i]
        spread = plain_t(picked[0], mark) + plain_t(picked[1], mark)
        g.sbext[2 + i] = g.aux[2 + i, 4:5, :] * (mm3(mix, (g.chi[i], g.clo[i])) + spread)
    bar_halo = g.halo_send(g.sbext, g.bar_halo)
    second = g.coefficient_terms(g.sbext, 2, g.fext, 1)
    bar_halo()
    g.pull_back(g.sbext, 1, g.fbar, r + 2, True)
    firsts = g.coefficient_terms(g.fbar, 1, g.pext, 2)
    g.cbuf[m] = jnp.concatenate(
        [second[i][k] + firsts[i][k] for k in range(4) for i in range(r)], axis=0
    )
    c_wait = g.mem_send(g.cbuf, g.c_sem)
    g.pull_back(g.fbar, 2, g.grad, r, False)
    c_wait()
    both = g.cbuf[0]
    for k in range(1, z.n_mem):
        both = both + g.cbuf[k]
    both = both / jnp.sqrt(jnp.float32(z.total))
    for k in range(4):
        g.coef[k] = both[k * r : (k + 1) * r]
    g.finish_sends()


def local(n_space, n_mem, prior, stencil, sea_mask, sites, data, precision, cotangent):
    z = Sizes(n_space, n_mem, prior, sites)
    any_spec = pl.BlockSpec(memory_space=pl.ANY)
    grad, coef = pl.pallas_call(
        functools.partial(kernel, z),
        out_shape=(
            jax.ShapeDtypeStruct((z.rows, z.members, z.cols), F32),
            jax.ShapeDtypeStruct((4, z.rows, z.cols), F32),
        ),
        in_specs=[any_spec, any_spec] + [VMEM_SPEC] * 5,
        out_specs=(VMEM_SPEC, VMEM_SPEC),
        scratch_shapes=list(scratch_of(z).values()) + [pltpu.VMEM((8 * pl.cdiv(n_mem, 8), z.total), F32)],
        compiler_params=pltpu.CompilerParams(
            collective_id=1, has_side_effects=True, vmem_limit_bytes=60 * 1024 * 1024
        ),
        name="adjoint",
    )(
        jnp.transpose(prior, (1, 0, 2)), jnp.transpose(cotangent, (1, 0, 2)),
        stencil, sea_mask, sites, data[None], precision[None],
    )
    return jnp.transpose(grad, (1, 0, 2)), coef


def solution(mesh):
    placed = (
        P("mem", "space", None),
        P(None, "space", None),
        P("space", None),
        P("space", None),
        P("space"),
        P("space"),
        P("mem", "space", None),
    )
    return jax.shard_map(
        functools.partial(local, mesh.shape["space"], mesh.shape["mem"]),
        mesh=mesh,
        in_specs=placed,
        out_specs=(P("mem", "space", None), P(None, "space", None)),
        check_vma=False,
    )
```

```python
import functools
import jax
import jax.numpy as jnp
from jax import lax
from jax.experimental import pallas as pl
from jax.experimental.pallas import tpu as pltpu
from jax.sharding import PartitionSpec as P

MESH = pl.DeviceIdType.MESH
F32 = jnp.float32
GRANT = 48 * 1024 * 1024
BF16 = jnp.bfloat16
VMEM_SPEC = pl.BlockSpec(memory_space=pltpu.VMEM)


def remote(src, dst, send, recv, s, m):
    return pltpu.make_async_remote_copy(
        src_ref=src, dst_ref=dst, send_sem=send, recv_sem=recv, device_id=(s, m), device_id_type=MESH
    )


def split(x):
    lead = x.astype(BF16)
    return lead, (x - lead.astype(F32)).astype(BF16)


def split3(x):
    lead = x.astype(BF16)
    rest = x - lead.astype(F32)
    middle = rest.astype(BF16)
    return lead, middle, (rest - middle.astype(F32)).astype(BF16)


def plain(a, b):
    return jnp.dot(a, b, preferred_element_type=F32)


def plain_t(a, b):
    return lax.dot_general(a, b, (((1,), (1,)), ((), ())), preferred_element_type=F32)


def mm3(a, b):
    return plain(a[0], b[0]) + (plain(a[0], b[1]) + plain(a[1], b[0]))


def mm3_t(a, b):
    return plain_t(a[0], b[0]) + (plain_t(a[0], b[1]) + plain_t(a[1], b[0]))


def whole_sum(x):
    return jnp.sum(jnp.sum(x, axis=0, keepdims=True), axis=1, keepdims=True)


def eye(size):
    return lax.broadcasted_iota(jnp.int32, (size, size), 0) == lax.broadcasted_iota(
        jnp.int32, (size, size), 1
    )


class Sizes:
    def __init__(self, n_space, n_mem, prior, sites):
        self.n_space, self.n_mem = n_space, n_mem
        self.members, self.rows, self.cols = prior.shape
        self.total = self.members * n_mem
        self.sites = sites.shape[-1]
        self.near = 2 if n_space % 2 == 0 else 1
        self.far = n_space // self.near
        self.half = 2 if n_mem % 2 == 0 else 1
        self.wide = n_mem // self.half
        self.group = max(1, self.far // 4)
        self.groups = self.far // self.group
        self.height = n_mem // 2 * self.members // n_space
        self.lines = 8 * pl.cdiv(4 + n_mem, 8)


def scratch_of(z):
    dma = pltpu.SemaphoreType.DMA
    ext = z.rows + 4
    v = lambda *shape: pltpu.VMEM(shape, F32)
    b = lambda *shape: pltpu.VMEM(shape, BF16)
    square = (z.total, z.total)
    half_square = (z.n_space, z.height, z.members)
    gathered = (z.n_mem, z.far, z.near, z.height, z.members)
    found = dict(
        stencil=v(4, z.rows, z.cols),
        sea=pltpu.VMEM((z.rows, z.cols), jnp.int32),
        sites=pltpu.VMEM((1, z.sites), jnp.int32),
        data=v(1, z.sites),
        prec=v(1, z.sites),
        few=dma((5,)),
        pext=v(ext, z.members, z.cols),
        aux=v(ext, 8, z.cols),
        cotf=v(z.rows, z.total, z.cols),
        chi=b(z.rows, z.total, z.cols),
        clo=b(z.rows, z.total, z.cols),
        fext=v(z.rows + 2, z.members, z.cols),
        state=v(z.rows, z.members, z.cols),
        hot=b(ext, z.cols, z.sites),
        obsf=v(z.n_mem, z.members, z.sites),
        tanh=v(z.members, z.sites),
        ahi=b(z.total, z.sites),
        alo=b(z.total, z.sites),
        innov=v(8, z.sites),
        sums=v(z.n_mem, 8 * pl.cdiv(z.rows, 8), z.cols),
        dmat=v(z.n_mem, z.members, z.members),
        dx=v(z.n_mem, z.members, z.members),
        vec=v(z.lines, z.members),
        vbuf=v(z.n_space, z.lines, z.members),
        vout=v(z.n_mem, z.lines, z.members),
        f=v(*square),
        g=v(*square),
        fg=v(*square),
        s=v(*square),
        weigh=v(*square),
        fh=b(*square), fl=b(*square),
        f2h=b(*square), f2l=b(*square),
        gh=b(*square), gl=b(*square),
        sh=b(*square), sl=b(*square),
        lh=b(3 * z.members, z.total), ll=b(3 * z.members, z.total),
        vcol=v(z.total, z.lines),
        sbext=v(ext, z.members, z.cols),
        mixed=v(ext, z.members, z.cols),
        picked=v(3, z.members, z.sites),
        fbar=v(z.rows + 2, z.members, z.cols),
        cbuf=v(z.n_mem, 4 * z.rows, z.cols),
        own=dma((2, z.rows)),
        halo=dma((2, 2)),
        aux_halo=dma((2, 2)),
        bar_halo=dma((2, 2)),
        pick_sem=dma((2, 2)),
        cot_sem=dma((2, z.half, z.wide)),
        obs_sem=dma((2, z.n_mem)),
        sum_sem=dma((2, z.n_mem)),
        d_sem=dma((2, z.n_mem)),
        v_sem=dma((2, z.n_space)),
        vg_sem=dma((2, z.n_mem)),
        c_sem=dma((2, z.n_mem)),
    )
    for tag in ("gram", "cross"):
        found[tag + "_src"] = v(*half_square)
        found[tag + "_buf"] = v(*half_square)
        found[tag + "_out"] = v(*gathered)
        found[tag + "_rs"] = dma((2, z.n_space))
        found[tag + "_a"] = dma((2, z.far))
        found[tag + "_x"] = dma((2, z.near, z.wide, z.groups))
        found[tag + "_q"] = dma((2, z.half, z.near, z.wide, z.groups))
    return found


class Reduction:
    def __init__(self, g, tag):
        self.g, self.z = g, g.z
        for name in ("src", "buf", "out", "rs", "a", "x", "q"):
            setattr(self, name, getattr(g, tag + "_" + name))
        z = g.z
        self.a_id, self.b_id = g.s_id // z.near, lax.rem(g.s_id, z.near)
        self.p_id, self.q_id = g.m_id // z.half, lax.rem(g.m_id, z.half)

    def scatter(self):
        z, s, m = self.z, self.g.s_id, self.g.m_id
        self.copies = []
        for k in range(1, z.n_space):
            to = lax.rem(s + k, z.n_space)
            self.copies.append(
                remote(self.src.at[to], self.buf.at[s], self.rs.at[0, k], self.rs.at[1, k], to, m)
            )
            self.copies[-1].start()
        self.g.waits += [(copy, None) for copy in self.copies]

    def start(self):
        z, s, m = self.z, self.g.s_id, self.g.m_id
        a, b = self.a_id, self.b_id
        self.buf[s] = self.src[s]
        for copy in self.copies:
            copy.wait_recv()
        total = self.buf[0]
        for k in range(1, z.n_space):
            total = total + self.buf[k]
        self.out[m, a, b] = total
        piece = self.out.at[m, a, b]
        stage = []
        for k in range(1, z.far):
            to = lax.rem(a + k, z.far) * z.near + b
            stage.append(remote(piece, piece, self.a.at[0, k], self.a.at[1, k], to, m))
            stage[-1].start()
        self.g.waits += [(copy, None) for copy in stage]
        if z.group == 1:
            self.steps = [([], a)] + [
                ([stage[k - 1]], lax.rem(a + z.far - k, z.far)) for k in range(1, z.far)
            ]
            self.forward(0)
        else:
            self.steps = [(stage if n == 0 else [], n * z.group) for n in range(z.groups)]

    def forward(self, index):
        z, s, m = self.z, self.g.s_id, self.g.m_id
        needs, start = self.steps[index]
        for copy in needs:
            copy.wait_recv()
        piece = self.out.at[m, pl.ds(start, z.group), self.b_id]
        for kb, kp in self.offsets():
            to_s = self.a_id * z.near + lax.rem(self.b_id + kb, z.near)
            to_m = lax.rem(self.p_id + kp, z.wide) * z.half + self.q_id
            self.send(piece, self.x.at[0, kb, kp, index], self.x.at[1, kb, kp, index], to_s, to_m)
        self.beside(piece, 0, 0, index)

    def forward_all(self):
        for index in range(1 if self.z.group == 1 else 0, self.z.groups):
            self.forward(index)

    def offsets(self):
        z = self.z
        return [(kb, kp) for kb in range(z.near) for kp in range(z.wide) if kb or kp]

    def send(self, piece, *where):
        copy = remote(piece, piece, *where)
        copy.start()
        self.g.waits.append((copy, None))

    def beside(self, piece, kb, kp, index):
        z = self.z
        for kq in range(1, z.half):
            to = self.p_id * z.half + lax.rem(self.q_id + kq, z.half)
            self.send(
                piece, self.q.at[0, kq, kb, kp, index], self.q.at[1, kq, kb, kp, index], self.g.s_id, to
            )

    def piece_of(self, kb, kp, kq, index):
        z = self.z
        which_b = lax.rem(self.b_id + z.near - kb, z.near)
        which_p = lax.rem(self.p_id + z.wide - kp, z.wide)
        which_q = lax.rem(self.q_id + z.half - kq, z.half)
        return self.out.at[which_p * z.half + which_q, pl.ds(self.steps[index][1], z.group), which_b]

    def pass_on(self):
        for index in range(self.z.groups):
            for kb, kp in self.offsets():
                piece = self.piece_of(kb, kp, 0, index)
                self.arrived(piece, self.x.at[0, kb, kp, index], self.x.at[1, kb, kp, index])
                self.beside(piece, kb, kp, index)

    def arrived(self, piece, send, recv):
        remote(piece, piece, send, recv, self.g.s_id, self.g.m_id).wait_recv()

    def finish(self):
        z = self.z
        for index in range(z.groups):
            for kb in range(z.near):
                for kp in range(z.wide):
                    for kq in range(1, z.half):
                        self.arrived(
                            self.piece_of(kb, kp, kq, index),
                            self.q.at[0, kq, kb, kp, index], self.q.at[1, kq, kb, kp, index],
                        )

    def whole(self, i):
        z = self.z
        return self.out[i].reshape(z.n_mem // 2 * z.members, z.members)


class Step:
    def __init__(self, z, refs):
        self.z = z
        self.__dict__.update(refs)
        self.s_id, self.m_id = lax.axis_index("space"), lax.axis_index("mem")
        self.lo = lax.rem(self.m_id, z.n_mem // 2)
        self.hi = self.m_id // (z.n_mem // 2)
        self.waits = []

    def finish_sends(self):
        for copy, when in self.waits:
            if when is None:
                copy.wait_send()
            else:
                pl.when(when)(copy.wait_send)

    def barrier(self):
        z, s, m = self.z, self.s_id, self.m_id
        peers = [(lax.rem(s + k, z.n_space), m) for k in range(1, z.n_space)]
        peers += [(s, lax.rem(m + k, z.n_mem)) for k in range(1, z.n_mem)]
        a, b = s // z.near, lax.rem(s, z.near)
        p, q = m // z.half, lax.rem(m, z.half)
        for kb in range(1, z.near):
            for kp in range(1, z.wide):
                peers.append((
                    a * z.near + lax.rem(b + kb, z.near), lax.rem(p + kp, z.wide) * z.half + q
                ))
        barrier = pltpu.get_barrier_semaphore()
        for peer in peers:
            pl.semaphore_signal(barrier, inc=1, device_id=peer, device_id_type=MESH)
        return lambda: pl.semaphore_wait(barrier, len(peers))

    def between(self, up_src, up_dst, down_src, down_dst, sem):
        z, s, m = self.z, self.s_id, self.m_id
        has_low, has_high = s > 0, s < z.n_space - 1
        up = remote(up_src, up_dst, sem.at[0, 0], sem.at[1, 0], s + 1, m)
        down = remote(down_src, down_dst, sem.at[0, 1], sem.at[1, 1], s - 1, m)
        pl.when(has_high)(up.start)
        pl.when(has_low)(down.start)
        self.waits += [(up, has_high), (down, has_low)]

        def wait():
            pl.when(has_low)(up.wait_recv)
            pl.when(has_high)(down.wait_recv)

        return wait

    def halo_send(self, ref, sem):
        r = self.z.rows
        at = lambda row: ref.at[pl.ds(row, 2)]
        return self.between(at(r), at(0), at(2), at(r + 2), sem)

    def pair_gather(self, part, sem):
        z, s, m = self.z, self.s_id, self.m_id
        p, q = m // z.half, lax.rem(m, z.half)
        across = [lax.rem(p + k, z.wide) * z.half + q for k in range(1, z.wide)]
        beside = [p * z.half + lax.rem(q + k, z.half) for k in range(1, z.half)]
        mine = part(m)
        hops, sides = [], []
        for k, to in enumerate(across):
            hops.append(remote(mine, mine, sem.at[0, 0, k + 1], sem.at[1, 0, k + 1], s, to))
            hops[-1].start()
        for k, to in enumerate(beside):
            sides.append(remote(mine, mine, sem.at[0, k + 1, 0], sem.at[1, k + 1, 0], s, to))
            sides[-1].start()

        def forward():
            for kp, hop in enumerate(hops):
                hop.wait_recv()
                piece = part(lax.rem(p + z.wide - kp - 1, z.wide) * z.half + q)
                for k, to in enumerate(beside):
                    copy = remote(
                        piece, piece, sem.at[0, k + 1, kp + 1], sem.at[1, k + 1, kp + 1], s, to
                    )
                    copy.start()
                    sides.append(copy)

        def wait():
            for copy in sides:
                copy.wait_recv()
            self.waits.extend((copy, None) for copy in hops + sides)

        return forward, wait

    def mem_send(self, ref, sem):
        z, s, m = self.z, self.s_id, self.m_id
        copies = []
        for k in range(1, z.n_mem):
            to = lax.rem(m + k, z.n_mem)
            copies.append(remote(ref.at[m], ref.at[m], sem.at[0, k], sem.at[1, k], s, to))
            copies[-1].start()

        def wait():
            for copy in copies:
                copy.wait_recv()
            self.waits.extend((copy, None) for copy in copies)

        return wait

    def block(self, which):
        size = self.z.members
        return pl.ds(pl.multiple_of(which * size, size), size)


    def coefficients(self, e):
        z = self.z
        c = [self.aux[e, k : k + 1, :] for k in range(4)]
        sea = self.aux[e, 4:5, :]
        lane = lax.broadcasted_iota(jnp.int32, (1, z.cols), 1)
        keep = sea * (1.0 - c[0] - c[1] - c[2] - c[3])
        west = jnp.where(lane == 0, 0.0, c[2])
        east = jnp.where(lane == z.cols - 1, 0.0, c[3])
        return keep, sea * c[0], sea * c[1], sea * west, sea * east

    def chunks(self):
        size = min(32, self.z.members)
        return [pl.ds(k, size) for k in range(0, self.z.members, size)]

    def advance(self, src, first, dst, count):
        z = self.z
        for i in range(count):
            keep, north, south, west, east = self.coefficients(first + i)
            for part in self.chunks():
                v = src[i + 1, part, :]
                dst[i, part, :] = (
                    keep * v
                    + north * src[i, part, :]
                    + south * src[i + 2, part, :]
                    + west * pltpu.roll(v, 1, 1)
                    + east * pltpu.roll(v, z.cols - 1, 1)
                )

    def observe(self):
        z = self.z
        picked = jnp.zeros((z.members, z.sites), F32)
        for r in range(z.rows):
            for piece in split3(self.state[r]):
                picked = picked + plain(piece, self.hot[2 + r])
        tanh = jnp.tanh(picked)
        self.tanh[...] = tanh
        return picked + 0.5 * tanh

    def mark(self, e, row, sites):
        z = self.z
        cell = lax.broadcasted_iota(jnp.int32, (z.cols, z.sites), 0) + row * z.cols
        self.hot[e] = jnp.where(cell == sites, 1.0, 0.0).astype(BF16)

    def mark_sites(self):
        for r in range(self.z.rows):
            self.mark(2 + r, r, self.sites[...])

    def mark_sites_beside(self):
        r = self.z.rows
        low, high = (self.aux[e, 5:6, :].astype(jnp.int32) for e in (1, r + 2))
        for k in range(2):
            self.mark(k, r - 2 + k, low)
            self.mark(r + 2 + k, k, high)

    def spread(self, slot, rows):
        hi, lo = split(self.picked[slot])
        for e in rows:
            field = self.mixed[e] + plain_t(hi, self.hot[e]) + plain_t(lo, self.hot[e])
            self.sbext[e] = self.aux[e, 4:5, :] * field


    def fold(self, block):
        size = self.z.members
        half = size // 2
        bottom = pltpu.roll(block[half:], half, 1)
        lane = lax.broadcasted_iota(jnp.int32, (half, size), 1)
        line = lax.broadcasted_iota(jnp.int32, (half, size), 0)
        return jnp.where(lane < line, bottom, block[:half])

    def unfold(self, folded, diagonal):
        size = self.z.members
        half = size // 2
        wide = jnp.concatenate([folded, pltpu.roll(folded, half, 1)], axis=0)
        lane = lax.broadcasted_iota(jnp.int32, (size, size), 1)
        line = lax.broadcasted_iota(jnp.int32, (size, size), 0)
        above, below = lane - line, lane - half
        straight = ((line < half) & (above >= 0)) | ((line >= half) & (below >= 0) & (above < 0))
        block = jnp.where(straight, wide, wide.T)
        return jnp.where((line >= half) & (above == 0), diagonal, block)

    def cross_rows(self, dev):
        z, s, m = self.z, self.s_id, self.m_id
        n, size = z.n_mem, z.members
        half = size // 2
        self.d_copies = []
        mean_bar = jnp.zeros((size, 1), F32)
        for k in list(range(n - 1, 0, -1)) + [0]:
            there = lax.rem(m + k, n)
            rows = self.block(there)
            part = mm3_t(dev[0], (self.chi[0, rows, :], self.clo[0, rows, :]))
            for i in range(1, z.rows):
                part = part + mm3_t(dev[i], (self.chi[i, rows, :], self.clo[i, rows, :]))
            mean_bar = mean_bar + jnp.sum(part, axis=1, keepdims=True)
            if 2 * k == n:
                part = jnp.where(self.hi == 0, part, part.T)
            self.dmat[k] = part
            copy = None
            if 2 * k > n:
                copy = remote(
                    self.dmat.at[k], self.dx.at[n - k], self.d_sem.at[0, k], self.d_sem.at[1, k], s, there
                )
            elif 2 * k == n:
                theirs = pl.ds(pl.multiple_of((1 - self.hi) * half, half), half)
                copy = remote(
                    self.dmat.at[k, theirs], self.dx.at[k, pl.ds(0, half)],
                    self.d_sem.at[0, k], self.d_sem.at[1, k], s, there,
                )
            if copy is not None:
                copy.start()
                self.d_copies.append(copy)
        self.waits += [(copy, None) for copy in self.d_copies]
        return mean_bar

    def pack_gram(self, scale, mean_bar, own_sums):
        z, m = self.z, self.m_id
        n, size = z.n_mem, z.members
        half = size // 2
        mean = jnp.zeros((1, z.sites), F32)
        for k in range(n):
            mean = mean + jnp.sum(self.obsf[k], axis=0, keepdims=True)
        mean = mean / z.total
        prec = self.prec[...]
        innov = prec * (self.data[...] - mean)
        self.innov[0:1, :] = innov
        for k in range(n):
            rows = slice(k * size, (k + 1) * size)
            self.ahi[rows, :], self.alo[rows, :] = split((self.obsf[k] - mean) * (prec / scale))
        anom = lambda rows: (self.ahi[rows, :], self.alo[rows, :])
        mine = anom(self.block(m))
        diag = mm3_t(mine, mine)
        parts = [self.fold(diag)]
        base = self.lo * size + self.hi * half
        upper = anom(pl.ds(pl.multiple_of(base, half), half))
        parts.append(mm3_t(upper, anom(self.block(self.lo + n // 2))))
        for k in range(1, n // 2):
            parts.append(mm3_t(mine, anom(self.block(lax.rem(m + k, n)))))
        self.gram_src[...] = jnp.concatenate(parts, axis=0).reshape(z.n_space, z.height, size)

        cross = self.dmat[0]
        self.cross_diag = 0.5 * (cross + cross.T)
        exact = (self.obsf[m] - mean) * (prec / scale)
        lane = lax.broadcasted_iota(jnp.int32, (size, size), 1)
        diagonal = lambda x: jnp.sum(jnp.where(eye(size), x, 0.0), axis=1, keepdims=True)
        pull = jnp.sum(exact * innov, axis=1, keepdims=True)
        columns = [pull, mean_bar, diagonal(self.cross_diag), diagonal(diag)]
        stacked = jnp.zeros((size, size), F32)
        for k, column in enumerate(columns):
            stacked = jnp.where(lane == k, column, stacked)
        total = self.sums[0]
        for k in range(1, n):
            total = total + self.sums[k]
        term = None
        for r in range(z.rows):
            lacks = (own_sums[r] / size - total[r : r + 1] / z.total) / scale
            this = mm3_t(split(jnp.broadcast_to(lacks, (8, z.cols))), (self.chi[r], self.clo[r]))
            term = this if term is None else term + this
        lines = [stacked.T[:4]] + [term[:1, k * size : (k + 1) * size] for k in range(n)]
        if z.lines > 4 + n:
            lines.append(jnp.zeros((z.lines - 4 - n, size), F32))
        self.vec[...] = jnp.concatenate(lines, axis=0)

    def pack_cross(self):
        z = self.z
        n, size = z.n_mem, z.members
        half = size // 2
        for copy in self.d_copies:
            copy.wait_recv()
        parts = [self.fold(self.cross_diag)]
        ours = pl.ds(pl.multiple_of(self.hi * half, half), half)
        parts.append(0.5 * (self.dmat[n // 2, ours] + self.dx[n // 2, pl.ds(0, half)]))
        for k in range(1, n // 2):
            parts.append(0.5 * (self.dmat[k] + self.dx[k].T))
        self.cross_src[...] = jnp.concatenate(parts, axis=0).reshape(z.n_space, z.height, size)

    def send_lines(self):
        z, s, m = self.z, self.s_id, self.m_id
        self.tiny = []
        for k in range(1, z.n_space):
            to = lax.rem(s + k, z.n_space)
            self.tiny.append(
                remote(self.vec, self.vbuf.at[s], self.v_sem.at[0, k], self.v_sem.at[1, k], to, m)
            )
            self.tiny[-1].start()
        self.waits += [(copy, None) for copy in self.tiny]

    def sum_lines(self):
        self.vbuf[self.s_id] = self.vec[...]
        for copy in self.tiny:
            copy.wait_recv()
        vec = self.vbuf[0]
        for k in range(1, self.z.n_space):
            vec = vec + self.vbuf[k]
        self.vout[self.m_id] = vec
        return self.mem_send(self.vout, self.vg_sem)

    def blocks_of(self, reduction, line):
        z = self.z
        n, size = z.n_mem, z.members
        half = size // 2
        wholes = [reduction.whole(i) for i in range(n)]
        for i in range(n):
            yield i, i, self.unfold(wholes[i][:half], self.vout[i, line : line + 1, :])
        for i in range(n // 2):
            j = i + n // 2
            yield i, j, jnp.concatenate([wholes[i][half:size], wholes[j][half:size]], axis=0)
        for i in range(n):
            for k in range(1, n // 2):
                yield i, (i + k) % n, wholes[i][k * size : (k + 1) * size]


    def transform(self, scale, gram):
        z, m = self.z, self.m_id
        n, size, total = z.n_mem, z.members, z.total
        mine = self.block(m)
        col = lambda k: slice(k * size, (k + 1) * size)
        squares = jnp.zeros((size, size), F32)
        for i, j, block in self.blocks_of(gram, 3):
            if i == j:
                block = block + eye(size).astype(F32)
                squares = squares + block * block
            else:
                self.f[col(j), col(i)] = block.T
                squares = squares + 2.0 * (block * block)
            self.f[col(i), col(j)] = block
        norm = jnp.sqrt(whole_sum(squares))
        root = jnp.sqrt(norm)
        identity = eye(total).astype(F32)
        f = 1.5 * identity - (0.5 / norm) * self.f[...]
        self.f[...] = f
        self.fh[...], self.fl[...] = split(f)
        f_split = (self.fh[...], self.fl[...])
        f2 = mm3(f_split, f_split)
        self.f2h[...], self.f2l[...] = split(f2)
        g = f2 - 1.5 * self.f[...]
        self.g[...] = g
        self.gh[...], self.gl[...] = split(g)
        g_split = (self.gh[...], self.gl[...])
        yield
        p = 1.5 * self.f[...] + mm3((self.f2h[...], self.f2l[...]), g_split)
        self.s[...] = p
        p_split = split(p)
        kind = lax.broadcasted_iota(jnp.int32, (z.lines, size), 0)
        self.lines = []
        for i in range(n):
            lines = self.vout[i]
            lacks = jnp.sum(jnp.sum(lines[4 : 4 + n], axis=0, keepdims=True), axis=1, keepdims=True)
            self.lines.append(jnp.where(kind == 1, lines + lacks, jnp.where(kind == 3, 1.0, lines)))
        rows = jnp.concatenate(self.lines, axis=1)
        self.first = mm3(split(rows), p_split) / root
        second = mm3(split(self.first), p_split) / root
        self.vcol[...] = second.T
        self.pull_bar = second[1:2]
        self.pull_mine = self.vcol[mine, 1:2] - jnp.sum(self.pull_bar, axis=1, keepdims=True) / total
        mix = self.s[mine, :] / root + self.vcol[mine, 0:1] / scale
        row_weights = self.first[3:4] + jnp.sum(second[0:1], axis=1, keepdims=True) / scale
        mix = split(mix + (1.0 - row_weights) / total)
        for r in range(z.rows):
            self.mixed[2 + r] = mm3(mix, (self.chi[r], self.clo[r]))
        bar_halo = self.halo_send(self.mixed, self.bar_halo)
        self.fg[...] = mm3((self.fh[...], self.fl[...]), g_split)
        self.weigh[...] = 2.25 * identity + 4.5 * (self.fg[...] + self.f[...] - self.s[...])
        self.norm, self.root = norm, root
        for k, ref in enumerate((self.f, self.g, self.fg)):
            rows = slice(k * size, (k + 1) * size)
            self.lh[rows, :], self.ll[rows, :] = split(self.centred(ref))
        yield bar_halo

    def centred(self, ref):
        return ref[self.block(self.m_id), :] - jnp.sum(ref[...], axis=0, keepdims=True) / self.z.total

    def respond(self, scale, cross):
        z, m = self.z, self.m_id
        n, size, total = z.n_mem, z.members, z.total
        col = lambda k: slice(k * size, (k + 1) * size)
        norm, root = self.norm, self.root
        turned = [x.T for x in self.lines]
        first_t = self.first.T
        for i, j, block in self.blocks_of(cross, 2):
            block = (scale / root) * (
                block + 0.5 * (self.lines[i][4 + j : 5 + j] + turned[j][:, 4 + i : 5 + i])
            ) + (0.5 / root) * (
                turned[i][:, 1:2] * self.first[0:1, col(j)]
                + first_t[col(i), 0:1] * self.lines[j][1:2]
                + first_t[col(i), 1:2] * self.lines[j][0:1]
                + turned[i][:, 0:1] * self.first[1:2, col(j)]
            )
            self.s[col(i), col(j)] = block
            if i != j:
                self.s[col(j), col(i)] = block.T
        scale_bar = whole_sum(self.s[...] * self.weigh[...]) / norm
        self.sh[...], self.sl[...] = split(self.s[...])
        s_split = (self.sh[...], self.sl[...])
        s_mine = self.centred(self.s)
        f_split = (self.fh[...], self.fl[...])
        through = mm3((self.lh[...], self.ll[...]), s_split)
        bar = 1.5 * s_mine + through[2 * size :]
        bar = bar + mm3(split(mm3(split(s_mine), f_split)), (self.gh[...], self.gl[...]))
        bar = bar + mm3(split(through[:size]), (self.f2h[...], self.f2l[...]))
        bar = bar + mm3(split(through[size : 2 * size]), f_split)
        unit = (
            lax.broadcasted_iota(jnp.int32, (size, total), 0) + m * size
            == lax.broadcasted_iota(jnp.int32, (size, total), 1)
        ).astype(F32) - 1.0 / total
        sym = 2.0 * scale_bar * (3.0 * unit - 2.0 * self.centred(self.f)) - bar / norm
        sym = sym - (scale / total) * self.pull_bar
        observed = (self.prec[...] / scale) * (
            mm3(split(sym), (self.ahi[...], self.alo[...])) + self.pull_mine * self.innov[0:1, :]
        )
        tanh = self.tanh[...]
        return observed * (1.0 + 0.5 * (1.0 - tanh * tanh))


    def pull_back(self, src, first, dst, rows, to_sea):
        z = self.z
        for i in rows:
            e = first + i
            c = [self.aux[e, k : k + 1, :] for k in range(4)]
            lane = lax.broadcasted_iota(jnp.int32, (1, z.cols), 1)
            keep = 1.0 - c[0] - c[1] - c[2] - c[3]
            from_south, from_north = self.aux[e + 1, 0:1, :], self.aux[e - 1, 1:2, :]
            sea = self.aux[e, 4:5, :]
            east = pltpu.roll(jnp.broadcast_to(jnp.where(lane == 0, 0.0, c[2]), (8, z.cols)), z.cols - 1, 1)[:1]
            west = pltpu.roll(jnp.broadcast_to(jnp.where(lane == z.cols - 1, 0.0, c[3]), (8, z.cols)), 1, 1)[:1]
            if to_sea:
                keep, from_south, from_north = sea * keep, sea * from_south, sea * from_north
                east, west = sea * east, sea * west
            for part in self.chunks():
                v = src[i + 1, part, :]
                dst[i, part, :] = (
                    keep * v
                    + from_south * src[i + 2, part, :]
                    + from_north * src[i, part, :]
                    + east * pltpu.roll(v, z.cols - 1, 1)
                    + west * pltpu.roll(v, 1, 1)
                )

    def coefficient_terms(self, weight, w0, field, f0):
        z = self.z
        lane = lax.broadcasted_iota(jnp.int32, (1, z.cols), 1)
        rows = []
        for r in range(z.rows):
            sums = [0.0] * 5
            for part in self.chunks():
                w = weight[w0 + r, part, :]
                c = field[f0 + r, part, :]
                terms = [
                    w * field[f0 + r - 1, part, :],
                    w * field[f0 + r + 1, part, :],
                    w * pltpu.roll(c, 1, 1),
                    w * pltpu.roll(c, z.cols - 1, 1),
                    w * c,
                ]
                sums = [x + y for x, y in zip(sums, terms)]
            north, south, west, east, own = [jnp.sum(x, axis=0, keepdims=True) for x in sums]
            west = jnp.where(lane == 0, 0.0, west)
            east = jnp.where(lane == z.cols - 1, 0.0, east)
            rows.append([north - own, south - own, west - own, east - own])
        return rows


def kernel(z, *refs):
    small = ["stencil", "sea", "sites", "data", "prec"]
    names = ["prior", "cot"] + [name + "_in" for name in small] + ["grad", "coef"]
    names += list(scratch_of(z))
    g = Step(z, dict(zip(names, refs)))
    scale = jnp.sqrt(jnp.float32(z.total - 1))
    s, m = g.s_id, g.m_id
    r, ext = z.rows, z.rows + 4
    mine = g.block(m)

    entered = g.barrier()
    loads = []
    for i in range(r):
        loads.append(pltpu.make_async_copy(g.prior.at[:, i], g.pext.at[2 + i], g.own.at[0, i]))
    for i in range(r):
        loads.append(pltpu.make_async_copy(g.cot.at[:, i], g.cotf.at[i, mine], g.own.at[1, i]))
    few = [
        pltpu.make_async_copy(getattr(g, name + "_in"), getattr(g, name), g.few.at[i])
        for i, name in enumerate(small)
    ]
    for copy in loads[:r] + few + loads[r:]:
        copy.start()
    for copy in few:
        copy.wait()
    for i in range(r):
        g.aux[2 + i, 0:4, :] = g.stencil[:, i, :]
        g.aux[2 + i, 4:5, :] = g.sea[i : i + 1, :].astype(F32)
        g.aux[2 + i, 5:6, :] = g.sites[...].astype(F32)
        g.aux[2 + i, 6:8, :] = jnp.zeros((2, z.cols), F32)
    for e, edge in ((0, 0), (1, 0), (ext - 2, z.n_space - 1), (ext - 1, z.n_space - 1)):
        @pl.when(s == edge)
        def _():
            g.pext[e] = jnp.zeros((z.members, z.cols), F32)
            g.mixed[e] = jnp.zeros((z.members, z.cols), F32)
            g.aux[e] = jnp.zeros((8, z.cols), F32)
            g.picked[1 if e < 2 else 2] = jnp.zeros((z.members, z.sites), F32)
    for copy in loads[:r]:
        copy.wait()
    entered()
    halo = g.halo_send(g.pext, g.halo)
    for copy in loads[r:]:
        copy.wait()
    cot_forward, cot_wait = g.pair_gather(lambda which: g.cotf.at[:, g.block(which)], g.cot_sem)
    aux_halo = g.halo_send(g.aux, g.aux_halo)
    g.mark_sites()
    aux_halo()
    g.mark_sites_beside()
    cot_forward()
    halo()

    g.advance(g.pext, 1, g.fext, r + 2)
    g.advance(g.fext, 2, g.state, r)
    g.obsf[m] = g.observe()
    obs_wait = g.mem_send(g.obsf, g.obs_sem)
    own_sums = [jnp.sum(g.state[i], axis=0, keepdims=True) for i in range(r)]
    padding = [jnp.zeros((-r % 8, z.cols), F32)] * (r % 8 > 0)
    g.sums[m] = jnp.concatenate(own_sums + padding, axis=0)
    sums_wait = g.mem_send(g.sums, g.sum_sem)
    cot_wait()
    for i in range(r):
        g.chi[i], g.clo[i] = split(g.cotf[i])
    dev = [split((g.state[i] - own_sums[i] / z.members) / scale) for i in range(r)]
    mean_bar = g.cross_rows(dev)
    sums_wait()
    obs_wait()
    g.pack_gram(scale, mean_bar, own_sums)

    gram, cross = Reduction(g, "gram"), Reduction(g, "cross")
    gram.scatter()
    g.send_lines()
    g.pack_cross()
    cross.scatter()
    gram.start()
    lines_wait = g.sum_lines()
    gram.forward_all()
    cross.start()
    gram.pass_on()
    cross.forward_all()
    lines_wait()
    gram.finish()
    parts = g.transform(scale, gram)
    next(parts)
    cross.pass_on()
    bar_halo = next(parts)
    cross.finish()
    g.picked[0] = g.respond(scale, cross)
    pick_wait = g.between(
        g.picked.at[0], g.picked.at[1], g.picked.at[0], g.picked.at[2], g.pick_sem
    )
    g.spread(0, range(2, r + 2))
    second = g.coefficient_terms(g.sbext, 2, g.fext, 1)
    bar_halo()
    g.pull_back(g.sbext, 1, g.fbar, range(2, r), True)
    pick_wait()
    g.spread(1, (0, 1))
    g.spread(2, (r + 2, r + 3))
    g.pull_back(g.sbext, 1, g.fbar, (0, 1, r, r + 1), True)
    firsts = g.coefficient_terms(g.fbar, 1, g.pext, 2)
    g.cbuf[m] = jnp.concatenate(
        [second[i][k] + firsts[i][k] for k in range(4) for i in range(r)], axis=0
    )
    c_wait = g.mem_send(g.cbuf, g.c_sem)
    g.pull_back(g.fbar, 2, g.grad, range(r), False)
    c_wait()
    both = g.cbuf[0]
    for k in range(1, z.n_mem):
        both = both + g.cbuf[k]
    for k in range(4):
        g.coef[k] = both[k * r : (k + 1) * r]
    g.finish_sends()


def place(z, last, sums, grad, coef, scaled, sem):
    stores = [pltpu.make_async_copy(last.at[i], grad.at[:, i], sem.at[i]) for i in range(z.rows)]
    for copy in stores:
        copy.start()
    scaled[...] = sums[...] / jnp.sqrt(jnp.float32(z.total))
    stores.append(pltpu.make_async_copy(scaled, coef, sem.at[z.rows]))
    stores[-1].start()
    for copy in stores:
        copy.wait()


def local(n_space, n_mem, prior, stencil, sea_mask, sites, data, precision, cotangent):
    z = Sizes(n_space, n_mem, prior, sites)
    any_spec = pl.BlockSpec(memory_space=pl.ANY)
    turned = (z.rows, z.members, z.cols)
    factors = (4, z.rows, z.cols)
    inputs = (prior, cotangent, stencil, sea_mask, sites, data[None], precision[None])
    last, sums = pl.pallas_call(
        functools.partial(kernel, z),
        out_shape=(jax.ShapeDtypeStruct(turned, F32), jax.ShapeDtypeStruct(factors, F32)),
        in_specs=[pl.BlockSpec(memory_space=pltpu.HBM)] * 7,
        out_specs=(VMEM_SPEC, VMEM_SPEC),
        scratch_shapes=list(scratch_of(z).values()),
        compiler_params=pltpu.CompilerParams(
            collective_id=1, has_side_effects=True, vmem_limit_bytes=GRANT
        ),
        name="adjoint",
    )(*[pltpu.with_memory_space_constraint(x, pltpu.HBM) for x in inputs])
    return pl.pallas_call(
        functools.partial(place, z),
        out_shape=(jax.ShapeDtypeStruct(prior.shape, F32), jax.ShapeDtypeStruct(factors, F32)),
        in_specs=[VMEM_SPEC, VMEM_SPEC],
        out_specs=(any_spec, any_spec),
        scratch_shapes=[pltpu.VMEM(factors, F32), pltpu.SemaphoreType.DMA((z.rows + 1,))],
        compiler_params=pltpu.CompilerParams(vmem_limit_bytes=4 * 1024 * 1024),
        name="place",
    )(last, sums)


def solution(mesh):
    placed = (
        P("mem", "space", None),
        P(None, "space", None),
        P("space", None),
        P("space", None),
        P("space"),
        P("space"),
        P("mem", "space", None),
    )
    return jax.shard_map(
        functools.partial(local, mesh.shape["space"], mesh.shape["mem"]),
        mesh=mesh,
        in_specs=placed,
        out_specs=(P("mem", "space", None), P(None, "space", None)),
        check_vma=False,
    )
```

```python
import functools
import jax
import jax.numpy as jnp
from jax import lax
from jax.experimental import pallas as pl
from jax.experimental.pallas import tpu as pltpu
from jax.sharding import PartitionSpec as P

MESH = pl.DeviceIdType.MESH
F32 = jnp.float32
GRANT = 48 * 1024 * 1024
BF16 = jnp.bfloat16
VMEM_SPEC = pl.BlockSpec(memory_space=pltpu.VMEM)


def remote(src, dst, send, recv, s, m):
    return pltpu.make_async_remote_copy(
        src_ref=src, dst_ref=dst, send_sem=send, recv_sem=recv, device_id=(s, m), device_id_type=MESH
    )


def split(x):
    lead = x.astype(BF16)
    return lead, (x - lead.astype(F32)).astype(BF16)


def split3(x):
    lead = x.astype(BF16)
    rest = x - lead.astype(F32)
    middle = rest.astype(BF16)
    return lead, middle, (rest - middle.astype(F32)).astype(BF16)


def plain(a, b):
    return jnp.dot(a, b, preferred_element_type=F32)


def plain_t(a, b):
    return lax.dot_general(a, b, (((1,), (1,)), ((), ())), preferred_element_type=F32)


def mm3(a, b):
    return plain(a[0], b[0]) + (plain(a[0], b[1]) + plain(a[1], b[0]))


def mm3_t(a, b):
    return plain_t(a[0], b[0]) + (plain_t(a[0], b[1]) + plain_t(a[1], b[0]))


def whole_sum(x):
    return jnp.sum(jnp.sum(x, axis=0, keepdims=True), axis=1, keepdims=True)


def eye(size):
    return lax.broadcasted_iota(jnp.int32, (size, size), 0) == lax.broadcasted_iota(
        jnp.int32, (size, size), 1
    )


class Sizes:
    def __init__(self, n_space, n_mem, prior, sites):
        self.n_space, self.n_mem = n_space, n_mem
        self.members, self.rows, self.cols = prior.shape
        self.total = self.members * n_mem
        self.sites = sites.shape[-1]
        self.near = 2 if n_space % 2 == 0 else 1
        self.far = n_space // self.near
        self.half = 2 if n_mem % 2 == 0 else 1
        self.wide = n_mem // self.half
        self.group = max(1, self.far // 4)
        self.groups = self.far // self.group
        self.height = n_mem // 2 * self.members // n_space
        self.lines = 8 * pl.cdiv(4 + n_mem, 8)
        self.rounds = max(0, (n_space - 1).bit_length() - 1)


def scratch_of(z):
    dma = pltpu.SemaphoreType.DMA
    ext = z.rows + 4
    v = lambda *shape: pltpu.VMEM(shape, F32)
    b = lambda *shape: pltpu.VMEM(shape, BF16)
    square = (z.total, z.total)
    half_square = (z.n_space, z.height, z.members)
    gathered = (z.n_mem, z.far, z.near, z.height, z.members)
    found = dict(
        stencil=v(4, z.rows, z.cols),
        sea=pltpu.VMEM((z.rows, z.cols), jnp.int32),
        sites=pltpu.VMEM((1, z.sites), jnp.int32),
        data=v(1, z.sites),
        prec=v(1, z.sites),
        few=dma((5,)),
        token=pltpu.SemaphoreType.REGULAR((max(1, z.rounds), 2)),
        pext=v(ext, z.members, z.cols),
        aux=v(ext, 8, z.cols),
        cotf=v(z.rows, z.total, z.cols),
        chi=b(z.rows, z.total, z.cols),
        clo=b(z.rows, z.total, z.cols),
        fext=v(z.rows + 2, z.members, z.cols),
        state=v(z.rows, z.members, z.cols),
        hot=b(ext, z.cols, z.sites),
        obsf=v(z.n_mem, z.members, z.sites),
        tanh=v(z.members, z.sites),
        ahi=b(z.total, z.sites),
        alo=b(z.total, z.sites),
        innov=v(8, z.sites),
        sums=v(z.n_mem, 8 * pl.cdiv(z.rows, 8), z.cols),
        dmat=v(z.n_mem, z.members, z.members),
        dx=v(z.n_mem, z.members, z.members),
        vec=v(z.lines, z.members),
        vbuf=v(z.n_space, z.lines, z.members),
        vout=v(z.n_mem, z.lines, z.members),
        f=v(*square),
        g=v(*square),
        fg=v(*square),
        s=v(*square),
        weigh=v(*square),
        fh=b(*square), fl=b(*square),
        f2h=b(*square), f2l=b(*square),
        gh=b(*square), gl=b(*square),
        sh=b(*square), sl=b(*square),
        lh=b(3 * z.members, z.total), ll=b(3 * z.members, z.total),
        vcol=v(z.total, z.lines),
        sbext=v(ext, z.members, z.cols),
        mixed=v(ext, z.members, z.cols),
        picked=v(3, z.members, z.sites),
        fbar=v(z.rows + 2, z.members, z.cols),
        cbuf=v(z.n_mem, 4 * z.rows, z.cols),
        own=dma((2, z.rows)),
        halo=dma((2, 2)),
        aux_halo=dma((2, 2)),
        bar_halo=dma((2, 2)),
        pick_sem=dma((2, 2)),
        cot_sem=dma((2, z.half, z.wide)),
        obs_sem=dma((2, z.n_mem)),
        sum_sem=dma((2, z.n_mem)),
        d_sem=dma((2, z.n_mem)),
        v_sem=dma((2, z.n_space)),
        vg_sem=dma((2, z.n_mem)),
        c_sem=dma((2, z.n_mem)),
    )
    for tag in ("gram", "cross"):
        found[tag + "_src"] = v(*half_square)
        found[tag + "_buf"] = v(*half_square)
        found[tag + "_out"] = v(*gathered)
        found[tag + "_rs"] = dma((2, z.n_space))
        found[tag + "_a"] = dma((2, z.far))
        found[tag + "_x"] = dma((2, z.near, z.wide, z.groups))
        found[tag + "_q"] = dma((2, z.half, z.near, z.wide, z.groups))
    return found


class Reduction:
    def __init__(self, g, tag):
        self.g, self.z = g, g.z
        for name in ("src", "buf", "out", "rs", "a", "x", "q"):
            setattr(self, name, getattr(g, tag + "_" + name))
        z = g.z
        self.a_id, self.b_id = g.s_id // z.near, lax.rem(g.s_id, z.near)
        self.p_id, self.q_id = g.m_id // z.half, lax.rem(g.m_id, z.half)

    def scatter(self):
        z, s, m = self.z, self.g.s_id, self.g.m_id
        self.copies = []
        for k in range(1, z.n_space):
            to = lax.rem(s + k, z.n_space)
            self.copies.append(
                remote(self.src.at[to], self.buf.at[s], self.rs.at[0, k], self.rs.at[1, k], to, m)
            )
            self.copies[-1].start()
        self.g.waits += [(copy, None) for copy in self.copies]

    def start(self):
        z, s, m = self.z, self.g.s_id, self.g.m_id
        a, b = self.a_id, self.b_id
        self.buf[s] = self.src[s]
        for copy in self.copies:
            copy.wait_recv()
        total = self.buf[0]
        for k in range(1, z.n_space):
            total = total + self.buf[k]
        self.out[m, a, b] = total
        piece = self.out.at[m, a, b]
        stage = []
        for k in range(1, z.far):
            to = lax.rem(a + k, z.far) * z.near + b
            stage.append(remote(piece, piece, self.a.at[0, k], self.a.at[1, k], to, m))
            stage[-1].start()
        self.g.waits += [(copy, None) for copy in stage]
        if z.group == 1:
            self.steps = [([], a)] + [
                ([stage[k - 1]], lax.rem(a + z.far - k, z.far)) for k in range(1, z.far)
            ]
            self.forward(0)
        else:
            self.steps = [(stage if n == 0 else [], n * z.group) for n in range(z.groups)]

    def forward(self, index):
        z, s, m = self.z, self.g.s_id, self.g.m_id
        needs, start = self.steps[index]
        for copy in needs:
            copy.wait_recv()
        piece = self.out.at[m, pl.ds(start, z.group), self.b_id]
        for kb, kp in self.offsets():
            to_s = self.a_id * z.near + lax.rem(self.b_id + kb, z.near)
            to_m = lax.rem(self.p_id + kp, z.wide) * z.half + self.q_id
            self.send(piece, self.x.at[0, kb, kp, index], self.x.at[1, kb, kp, index], to_s, to_m)
        self.beside(piece, 0, 0, index)

    def forward_all(self):
        for index in range(1 if self.z.group == 1 else 0, self.z.groups):
            self.forward(index)

    def offsets(self):
        z = self.z
        return [(kb, kp) for kb in range(z.near) for kp in range(z.wide) if kb or kp]

    def send(self, piece, *where):
        copy = remote(piece, piece, *where)
        copy.start()
        self.g.waits.append((copy, None))

    def beside(self, piece, kb, kp, index):
        z = self.z
        for kq in range(1, z.half):
            to = self.p_id * z.half + lax.rem(self.q_id + kq, z.half)
            self.send(
                piece, self.q.at[0, kq, kb, kp, index], self.q.at[1, kq, kb, kp, index], self.g.s_id, to
            )

    def piece_of(self, kb, kp, kq, index):
        z = self.z
        which_b = lax.rem(self.b_id + z.near - kb, z.near)
        which_p = lax.rem(self.p_id + z.wide - kp, z.wide)
        which_q = lax.rem(self.q_id + z.half - kq, z.half)
        return self.out.at[which_p * z.half + which_q, pl.ds(self.steps[index][1], z.group), which_b]

    def pass_on(self):
        for index in range(self.z.groups):
            for kb, kp in self.offsets():
                piece = self.piece_of(kb, kp, 0, index)
                self.arrived(piece, self.x.at[0, kb, kp, index], self.x.at[1, kb, kp, index])
                self.beside(piece, kb, kp, index)

    def arrived(self, piece, send, recv):
        remote(piece, piece, send, recv, self.g.s_id, self.g.m_id).wait_recv()

    def finish(self):
        z = self.z
        for index in range(z.groups):
            for kb in range(z.near):
                for kp in range(z.wide):
                    for kq in range(1, z.half):
                        self.arrived(
                            self.piece_of(kb, kp, kq, index),
                            self.q.at[0, kq, kb, kp, index], self.q.at[1, kq, kb, kp, index],
                        )

    def whole(self, i):
        z = self.z
        return self.out[i].reshape(z.n_mem // 2 * z.members, z.members)


class Step:
    def __init__(self, z, refs):
        self.z = z
        self.__dict__.update(refs)
        self.s_id, self.m_id = lax.axis_index("space"), lax.axis_index("mem")
        self.lo = lax.rem(self.m_id, z.n_mem // 2)
        self.hi = self.m_id // (z.n_mem // 2)
        self.waits = []

    def finish_sends(self):
        for copy, when in self.waits:
            if when is None:
                copy.wait_send()
            else:
                pl.when(when)(copy.wait_send)

    def barrier(self):
        z, s, m = self.z, self.s_id, self.m_id
        peers = [(s, lax.rem(m + k, z.n_mem)) for k in range(1, z.n_mem)]
        a, b = s // z.near, lax.rem(s, z.near)
        p, q = m // z.half, lax.rem(m, z.half)
        for kb in range(1, z.near):
            for kp in range(1, z.wide):
                peers.append((
                    a * z.near + lax.rem(b + kb, z.near), lax.rem(p + kp, z.wide) * z.half + q
                ))
        barrier = pltpu.get_barrier_semaphore()
        count = len(peers)
        for peer in peers:
            pl.semaphore_signal(barrier, inc=1, device_id=peer, device_id_type=MESH)
        for step in (1, -1, 2, -2):
            there = self.exists(step)
            count = count + there.astype(jnp.int32)

            @pl.when(there)
            def _():
                pl.semaphore_signal(barrier, inc=1, device_id=(s + step, m), device_id_type=MESH)

        return lambda: pl.semaphore_wait(barrier, count)

    def exists(self, step):
        to = self.s_id + step
        return (to >= 0) & (to < self.z.n_space)

    def vouch(self, round_):
        for side, step in ((0, 2**round_), (1, -(2**round_))):
            @pl.when(self.exists(step))
            def _():
                pl.semaphore_signal(
                    self.token.at[round_ - 1, side], inc=1,
                    device_id=(self.s_id + step, self.m_id), device_id_type=MESH,
                )

    def hear(self, round_):
        for side, step in ((0, -(2**round_)), (1, 2**round_)):
            @pl.when(self.exists(step))
            def _():
                pl.semaphore_wait(self.token.at[round_ - 1, side], 1)

    def between(self, up_src, up_dst, down_src, down_dst, sem):
        z, s, m = self.z, self.s_id, self.m_id
        has_low, has_high = s > 0, s < z.n_space - 1
        up = remote(up_src, up_dst, sem.at[0, 0], sem.at[1, 0], s + 1, m)
        down = remote(down_src, down_dst, sem.at[0, 1], sem.at[1, 1], s - 1, m)
        pl.when(has_high)(up.start)
        pl.when(has_low)(down.start)
        self.waits += [(up, has_high), (down, has_low)]

        def wait():
            pl.when(has_low)(up.wait_recv)
            pl.when(has_high)(down.wait_recv)

        return wait

    def halo_send(self, ref, sem):
        r = self.z.rows
        at = lambda row: ref.at[pl.ds(row, 2)]
        return self.between(at(r), at(0), at(2), at(r + 2), sem)

    def pair_gather(self, part, sem):
        z, s, m = self.z, self.s_id, self.m_id
        p, q = m // z.half, lax.rem(m, z.half)
        across = [lax.rem(p + k, z.wide) * z.half + q for k in range(1, z.wide)]
        beside = [p * z.half + lax.rem(q + k, z.half) for k in range(1, z.half)]
        mine = part(m)
        hops, sides = [], []
        for k, to in enumerate(across):
            hops.append(remote(mine, mine, sem.at[0, 0, k + 1], sem.at[1, 0, k + 1], s, to))
            hops[-1].start()
        for k, to in enumerate(beside):
            sides.append(remote(mine, mine, sem.at[0, k + 1, 0], sem.at[1, k + 1, 0], s, to))
            sides[-1].start()

        def forward():
            for kp, hop in enumerate(hops):
                hop.wait_recv()
                piece = part(lax.rem(p + z.wide - kp - 1, z.wide) * z.half + q)
                for k, to in enumerate(beside):
                    copy = remote(
                        piece, piece, sem.at[0, k + 1, kp + 1], sem.at[1, k + 1, kp + 1], s, to
                    )
                    copy.start()
                    sides.append(copy)

        def wait():
            for copy in sides:
                copy.wait_recv()
            self.waits.extend((copy, None) for copy in hops + sides)

        return forward, wait

    def mem_send(self, ref, sem):
        z, s, m = self.z, self.s_id, self.m_id
        copies = []
        for k in range(1, z.n_mem):
            to = lax.rem(m + k, z.n_mem)
            copies.append(remote(ref.at[m], ref.at[m], sem.at[0, k], sem.at[1, k], s, to))
            copies[-1].start()

        def wait():
            for copy in copies:
                copy.wait_recv()
            self.waits.extend((copy, None) for copy in copies)

        return wait

    def block(self, which):
        size = self.z.members
        return pl.ds(pl.multiple_of(which * size, size), size)


    def coefficients(self, e):
        z = self.z
        c = [self.aux[e, k : k + 1, :] for k in range(4)]
        sea = self.aux[e, 4:5, :]
        lane = lax.broadcasted_iota(jnp.int32, (1, z.cols), 1)
        keep = sea * (1.0 - c[0] - c[1] - c[2] - c[3])
        west = jnp.where(lane == 0, 0.0, c[2])
        east = jnp.where(lane == z.cols - 1, 0.0, c[3])
        return keep, sea * c[0], sea * c[1], sea * west, sea * east

    def chunks(self):
        size = min(32, self.z.members)
        return [pl.ds(k, size) for k in range(0, self.z.members, size)]

    def advance(self, src, first, dst, count):
        z = self.z
        for i in range(count):
            keep, north, south, west, east = self.coefficients(first + i)
            for part in self.chunks():
                v = src[i + 1, part, :]
                dst[i, part, :] = (
                    keep * v
                    + north * src[i, part, :]
                    + south * src[i + 2, part, :]
                    + west * pltpu.roll(v, 1, 1)
                    + east * pltpu.roll(v, z.cols - 1, 1)
                )

    def observe(self):
        z = self.z
        picked = jnp.zeros((z.members, z.sites), F32)
        for r in range(z.rows):
            for piece in split3(self.state[r]):
                picked = picked + plain(piece, self.hot[2 + r])
        tanh = jnp.tanh(picked)
        self.tanh[...] = tanh
        return picked + 0.5 * tanh

    def mark(self, e, row, sites):
        z = self.z
        cell = lax.broadcasted_iota(jnp.int32, (z.cols, z.sites), 0) + row * z.cols
        self.hot[e] = jnp.where(cell == sites, 1.0, 0.0).astype(BF16)

    def mark_sites(self):
        for r in range(self.z.rows):
            self.mark(2 + r, r, self.sites[...])

    def mark_sites_beside(self):
        r = self.z.rows
        low, high = (self.aux[e, 5:6, :].astype(jnp.int32) for e in (1, r + 2))
        for k in range(2):
            self.mark(k, r - 2 + k, low)
            self.mark(r + 2 + k, k, high)

    def spread(self, slot, rows):
        hi, lo = split(self.picked[slot])
        for e in rows:
            field = self.mixed[e] + plain_t(hi, self.hot[e]) + plain_t(lo, self.hot[e])
            self.sbext[e] = self.aux[e, 4:5, :] * field


    def fold(self, block):
        size = self.z.members
        half = size // 2
        bottom = pltpu.roll(block[half:], half, 1)
        lane = lax.broadcasted_iota(jnp.int32, (half, size), 1)
        line = lax.broadcasted_iota(jnp.int32, (half, size), 0)
        return jnp.where(lane < line, bottom, block[:half])

    def unfold(self, folded, diagonal):
        size = self.z.members
        half = size // 2
        wide = jnp.concatenate([folded, pltpu.roll(folded, half, 1)], axis=0)
        lane = lax.broadcasted_iota(jnp.int32, (size, size), 1)
        line = lax.broadcasted_iota(jnp.int32, (size, size), 0)
        above, below = lane - line, lane - half
        straight = ((line < half) & (above >= 0)) | ((line >= half) & (below >= 0) & (above < 0))
        block = jnp.where(straight, wide, wide.T)
        return jnp.where((line >= half) & (above == 0), diagonal, block)

    def cross_rows(self, dev):
        z, s, m = self.z, self.s_id, self.m_id
        n, size = z.n_mem, z.members
        half = size // 2
        self.d_copies = []
        mean_bar = jnp.zeros((size, 1), F32)
        for k in list(range(n - 1, 0, -1)) + [0]:
            there = lax.rem(m + k, n)
            rows = self.block(there)
            part = mm3_t(dev[0], (self.chi[0, rows, :], self.clo[0, rows, :]))
            for i in range(1, z.rows):
                part = part + mm3_t(dev[i], (self.chi[i, rows, :], self.clo[i, rows, :]))
            mean_bar = mean_bar + jnp.sum(part, axis=1, keepdims=True)
            if 2 * k == n:
                part = jnp.where(self.hi == 0, part, part.T)
            self.dmat[k] = part
            copy = None
            if 2 * k > n:
                copy = remote(
                    self.dmat.at[k], self.dx.at[n - k], self.d_sem.at[0, k], self.d_sem.at[1, k], s, there
                )
            elif 2 * k == n:
                theirs = pl.ds(pl.multiple_of((1 - self.hi) * half, half), half)
                copy = remote(
                    self.dmat.at[k, theirs], self.dx.at[k, pl.ds(0, half)],
                    self.d_sem.at[0, k], self.d_sem.at[1, k], s, there,
                )
            if copy is not None:
                copy.start()
                self.d_copies.append(copy)
        self.waits += [(copy, None) for copy in self.d_copies]
        return mean_bar

    def pack_gram(self, scale):
        z, m = self.z, self.m_id
        n, size = z.n_mem, z.members
        half = size // 2
        mean = jnp.zeros((1, z.sites), F32)
        for k in range(n):
            mean = mean + jnp.sum(self.obsf[k], axis=0, keepdims=True)
        mean = mean / z.total
        prec = self.prec[...]
        for k in range(n):
            rows = slice(k * size, (k + 1) * size)
            self.ahi[rows, :], self.alo[rows, :] = split((self.obsf[k] - mean) * (prec / scale))
        anom = lambda rows: (self.ahi[rows, :], self.alo[rows, :])
        mine = anom(self.block(m))
        diag = mm3_t(mine, mine)
        parts = [self.fold(diag)]
        base = self.lo * size + self.hi * half
        upper = anom(pl.ds(pl.multiple_of(base, half), half))
        parts.append(mm3_t(upper, anom(self.block(self.lo + n // 2))))
        for k in range(1, n // 2):
            parts.append(mm3_t(mine, anom(self.block(lax.rem(m + k, n)))))
        self.gram_src[...] = jnp.concatenate(parts, axis=0).reshape(z.n_space, z.height, size)
        return mean, diag

    def pack_lines(self, scale, mean_bar, own_sums, mean, diag):
        z, m = self.z, self.m_id
        n, size = z.n_mem, z.members
        prec = self.prec[...]
        innov = prec * (self.data[...] - mean)
        self.innov[0:1, :] = innov
        cross = self.dmat[0]
        self.cross_diag = 0.5 * (cross + cross.T)
        exact = (self.obsf[m] - mean) * (prec / scale)
        lane = lax.broadcasted_iota(jnp.int32, (size, size), 1)
        diagonal = lambda x: jnp.sum(jnp.where(eye(size), x, 0.0), axis=1, keepdims=True)
        pull = jnp.sum(exact * innov, axis=1, keepdims=True)
        columns = [pull, mean_bar, diagonal(self.cross_diag), diagonal(diag)]
        stacked = jnp.zeros((size, size), F32)
        for k, column in enumerate(columns):
            stacked = jnp.where(lane == k, column, stacked)
        total = self.sums[0]
        for k in range(1, n):
            total = total + self.sums[k]
        term = None
        for r in range(z.rows):
            lacks = (own_sums[r] / size - total[r : r + 1] / z.total) / scale
            this = mm3_t(split(jnp.broadcast_to(lacks, (8, z.cols))), (self.chi[r], self.clo[r]))
            term = this if term is None else term + this
        lines = [stacked.T[:4]] + [term[:1, k * size : (k + 1) * size] for k in range(n)]
        if z.lines > 4 + n:
            lines.append(jnp.zeros((z.lines - 4 - n, size), F32))
        self.vec[...] = jnp.concatenate(lines, axis=0)

    def pack_cross(self):
        z = self.z
        n, size = z.n_mem, z.members
        half = size // 2
        for copy in self.d_copies:
            copy.wait_recv()
        parts = [self.fold(self.cross_diag)]
        ours = pl.ds(pl.multiple_of(self.hi * half, half), half)
        parts.append(0.5 * (self.dmat[n // 2, ours] + self.dx[n // 2, pl.ds(0, half)]))
        for k in range(1, n // 2):
            parts.append(0.5 * (self.dmat[k] + self.dx[k].T))
        self.cross_src[...] = jnp.concatenate(parts, axis=0).reshape(z.n_space, z.height, size)

    def send_lines(self):
        z, s, m = self.z, self.s_id, self.m_id
        self.tiny = []
        for k in range(1, z.n_space):
            to = lax.rem(s + k, z.n_space)
            self.tiny.append(
                remote(self.vec, self.vbuf.at[s], self.v_sem.at[0, k], self.v_sem.at[1, k], to, m)
            )
            self.tiny[-1].start()
        self.waits += [(copy, None) for copy in self.tiny]

    def sum_lines(self):
        self.vbuf[self.s_id] = self.vec[...]
        for copy in self.tiny:
            copy.wait_recv()
        vec = self.vbuf[0]
        for k in range(1, self.z.n_space):
            vec = vec + self.vbuf[k]
        self.vout[self.m_id] = vec
        return self.mem_send(self.vout, self.vg_sem)

    def blocks_of(self, reduction, line):
        z = self.z
        n, size = z.n_mem, z.members
        half = size // 2
        wholes = [reduction.whole(i) for i in range(n)]
        for i in range(n):
            yield i, i, self.unfold(wholes[i][:half], self.vout[i, line : line + 1, :])
        for i in range(n // 2):
            j = i + n // 2
            yield i, j, jnp.concatenate([wholes[i][half:size], wholes[j][half:size]], axis=0)
        for i in range(n):
            for k in range(1, n // 2):
                yield i, (i + k) % n, wholes[i][k * size : (k + 1) * size]


    def transform(self, scale, gram):
        z, m = self.z, self.m_id
        n, size, total = z.n_mem, z.members, z.total
        mine = self.block(m)
        col = lambda k: slice(k * size, (k + 1) * size)
        squares = jnp.zeros((size, size), F32)
        for i, j, block in self.blocks_of(gram, 3):
            if i == j:
                block = block + eye(size).astype(F32)
                squares = squares + block * block
            else:
                self.f[col(j), col(i)] = block.T
                squares = squares + 2.0 * (block * block)
            self.f[col(i), col(j)] = block
        norm = jnp.sqrt(whole_sum(squares))
        root = jnp.sqrt(norm)
        identity = eye(total).astype(F32)
        f = 1.5 * identity - (0.5 / norm) * self.f[...]
        self.f[...] = f
        self.fh[...], self.fl[...] = split(f)
        f_split = (self.fh[...], self.fl[...])
        f2 = mm3(f_split, f_split)
        self.f2h[...], self.f2l[...] = split(f2)
        g = f2 - 1.5 * self.f[...]
        self.g[...] = g
        self.gh[...], self.gl[...] = split(g)
        g_split = (self.gh[...], self.gl[...])
        yield
        p = 1.5 * self.f[...] + mm3((self.f2h[...], self.f2l[...]), g_split)
        self.s[...] = p
        p_split = split(p)
        kind = lax.broadcasted_iota(jnp.int32, (z.lines, size), 0)
        self.lines = []
        for i in range(n):
            lines = self.vout[i]
            lacks = jnp.sum(jnp.sum(lines[4 : 4 + n], axis=0, keepdims=True), axis=1, keepdims=True)
            self.lines.append(jnp.where(kind == 1, lines + lacks, jnp.where(kind == 3, 1.0, lines)))
        rows = jnp.concatenate(self.lines, axis=1)
        self.first = mm3(split(rows), p_split) / root
        second = mm3(split(self.first), p_split) / root
        self.vcol[...] = second.T
        self.pull_bar = second[1:2]
        self.pull_mine = self.vcol[mine, 1:2] - jnp.sum(self.pull_bar, axis=1, keepdims=True) / total
        mix = self.s[mine, :] / root + self.vcol[mine, 0:1] / scale
        row_weights = self.first[3:4] + jnp.sum(second[0:1], axis=1, keepdims=True) / scale
        mix = split(mix + (1.0 - row_weights) / total)
        for r in range(z.rows):
            self.mixed[2 + r] = mm3(mix, (self.chi[r], self.clo[r]))
        bar_halo = self.halo_send(self.mixed, self.bar_halo)
        self.fg[...] = mm3((self.fh[...], self.fl[...]), g_split)
        self.weigh[...] = 2.25 * identity + 4.5 * (self.fg[...] + self.f[...] - self.s[...])
        self.norm, self.root = norm, root
        for k, ref in enumerate((self.f, self.g, self.fg)):
            rows = slice(k * size, (k + 1) * size)
            self.lh[rows, :], self.ll[rows, :] = split(self.centred(ref))
        yield bar_halo

    def centred(self, ref):
        return ref[self.block(self.m_id), :] - jnp.sum(ref[...], axis=0, keepdims=True) / self.z.total

    def respond(self, scale, cross):
        z, m = self.z, self.m_id
        n, size, total = z.n_mem, z.members, z.total
        col = lambda k: slice(k * size, (k + 1) * size)
        norm, root = self.norm, self.root
        turned = [x.T for x in self.lines]
        first_t = self.first.T
        for i, j, block in self.blocks_of(cross, 2):
            block = (scale / root) * (
                block + 0.5 * (self.lines[i][4 + j : 5 + j] + turned[j][:, 4 + i : 5 + i])
            ) + (0.5 / root) * (
                turned[i][:, 1:2] * self.first[0:1, col(j)]
                + first_t[col(i), 0:1] * self.lines[j][1:2]
                + first_t[col(i), 1:2] * self.lines[j][0:1]
                + turned[i][:, 0:1] * self.first[1:2, col(j)]
            )
            self.s[col(i), col(j)] = block
            if i != j:
                self.s[col(j), col(i)] = block.T
        scale_bar = whole_sum(self.s[...] * self.weigh[...]) / norm
        self.sh[...], self.sl[...] = split(self.s[...])
        s_split = (self.sh[...], self.sl[...])
        s_mine = self.centred(self.s)
        f_split = (self.fh[...], self.fl[...])
        through = mm3((self.lh[...], self.ll[...]), s_split)
        bar = 1.5 * s_mine + through[2 * size :]
        bar = bar + mm3(split(mm3(split(s_mine), f_split)), (self.gh[...], self.gl[...]))
        bar = bar + mm3(split(through[:size]), (self.f2h[...], self.f2l[...]))
        bar = bar + mm3(split(through[size : 2 * size]), f_split)
        unit = (
            lax.broadcasted_iota(jnp.int32, (size, total), 0) + m * size
            == lax.broadcasted_iota(jnp.int32, (size, total), 1)
        ).astype(F32) - 1.0 / total
        sym = 2.0 * scale_bar * (3.0 * unit - 2.0 * self.centred(self.f)) - bar / norm
        sym = sym - (scale / total) * self.pull_bar
        observed = (self.prec[...] / scale) * (
            mm3(split(sym), (self.ahi[...], self.alo[...])) + self.pull_mine * self.innov[0:1, :]
        )
        tanh = self.tanh[...]
        return observed * (1.0 + 0.5 * (1.0 - tanh * tanh))


    def pull_back(self, src, first, dst, rows, to_sea):
        z = self.z
        for i in rows:
            e = first + i
            c = [self.aux[e, k : k + 1, :] for k in range(4)]
            lane = lax.broadcasted_iota(jnp.int32, (1, z.cols), 1)
            keep = 1.0 - c[0] - c[1] - c[2] - c[3]
            from_south, from_north = self.aux[e + 1, 0:1, :], self.aux[e - 1, 1:2, :]
            sea = self.aux[e, 4:5, :]
            east = pltpu.roll(jnp.broadcast_to(jnp.where(lane == 0, 0.0, c[2]), (8, z.cols)), z.cols - 1, 1)[:1]
            west = pltpu.roll(jnp.broadcast_to(jnp.where(lane == z.cols - 1, 0.0, c[3]), (8, z.cols)), 1, 1)[:1]
            if to_sea:
                keep, from_south, from_north = sea * keep, sea * from_south, sea * from_north
                east, west = sea * east, sea * west
            for part in self.chunks():
                v = src[i + 1, part, :]
                dst[i, part, :] = (
                    keep * v
                    + from_south * src[i + 2, part, :]
                    + from_north * src[i, part, :]
                    + east * pltpu.roll(v, z.cols - 1, 1)
                    + west * pltpu.roll(v, 1, 1)
                )

    def coefficient_terms(self, weight, w0, field, f0):
        z = self.z
        lane = lax.broadcasted_iota(jnp.int32, (1, z.cols), 1)
        rows = []
        for r in range(z.rows):
            sums = [0.0] * 5
            for part in self.chunks():
                w = weight[w0 + r, part, :]
                c = field[f0 + r, part, :]
                terms = [
                    w * field[f0 + r - 1, part, :],
                    w * field[f0 + r + 1, part, :],
                    w * pltpu.roll(c, 1, 1),
                    w * pltpu.roll(c, z.cols - 1, 1),
                    w * c,
                ]
                sums = [x + y for x, y in zip(sums, terms)]
            north, south, west, east, own = [jnp.sum(x, axis=0, keepdims=True) for x in sums]
            west = jnp.where(lane == 0, 0.0, west)
            east = jnp.where(lane == z.cols - 1, 0.0, east)
            rows.append([north - own, south - own, west - own, east - own])
        return rows


def kernel(z, *refs):
    small = ["stencil", "sea", "sites", "data", "prec"]
    names = ["prior", "cot"] + [name + "_in" for name in small] + ["grad", "coef"]
    names += list(scratch_of(z))
    g = Step(z, dict(zip(names, refs)))
    scale = jnp.sqrt(jnp.float32(z.total - 1))
    s, m = g.s_id, g.m_id
    r, ext = z.rows, z.rows + 4
    mine = g.block(m)

    entered = g.barrier()
    loads = []
    for i in range(r):
        loads.append(pltpu.make_async_copy(g.prior.at[:, i], g.pext.at[2 + i], g.own.at[0, i]))
    for i in range(r):
        loads.append(pltpu.make_async_copy(g.cot.at[:, i], g.cotf.at[i, mine], g.own.at[1, i]))
    few = [
        pltpu.make_async_copy(getattr(g, name + "_in"), getattr(g, name), g.few.at[i])
        for i, name in enumerate(small)
    ]
    for copy in loads[:r] + few + loads[r:]:
        copy.start()
    for copy in few:
        copy.wait()
    for i in range(r):
        g.aux[2 + i, 0:4, :] = g.stencil[:, i, :]
        g.aux[2 + i, 4:5, :] = g.sea[i : i + 1, :].astype(F32)
        g.aux[2 + i, 5:6, :] = g.sites[...].astype(F32)
        g.aux[2 + i, 6:8, :] = jnp.zeros((2, z.cols), F32)
    for e, edge in ((0, 0), (1, 0), (ext - 2, z.n_space - 1), (ext - 1, z.n_space - 1)):
        @pl.when(s == edge)
        def _():
            g.pext[e] = jnp.zeros((z.members, z.cols), F32)
            g.mixed[e] = jnp.zeros((z.members, z.cols), F32)
            g.aux[e] = jnp.zeros((8, z.cols), F32)
            g.picked[1 if e < 2 else 2] = jnp.zeros((z.members, z.sites), F32)
    for copy in loads[:r]:
        copy.wait()
    entered()
    halo = g.halo_send(g.pext, g.halo)
    if z.rounds:
        g.vouch(1)
    for copy in loads[r:]:
        copy.wait()
    cot_forward, cot_wait = g.pair_gather(lambda which: g.cotf.at[:, g.block(which)], g.cot_sem)
    aux_halo = g.halo_send(g.aux, g.aux_halo)
    g.mark_sites()
    aux_halo()
    g.mark_sites_beside()
    cot_forward()
    for k in range(1, z.rounds):
        g.hear(k)
        g.vouch(k + 1)
    halo()

    g.advance(g.pext, 1, g.fext, r + 2)
    g.advance(g.fext, 2, g.state, r)
    g.obsf[m] = g.observe()
    obs_wait = g.mem_send(g.obsf, g.obs_sem)
    own_sums = [jnp.sum(g.state[i], axis=0, keepdims=True) for i in range(r)]
    padding = [jnp.zeros((-r % 8, z.cols), F32)] * (r % 8 > 0)
    g.sums[m] = jnp.concatenate(own_sums + padding, axis=0)
    sums_wait = g.mem_send(g.sums, g.sum_sem)
    cot_wait()
    for i in range(r):
        g.chi[i], g.clo[i] = split(g.cotf[i])
    dev = [split((g.state[i] - own_sums[i] / z.members) / scale) for i in range(r)]
    mean_bar = g.cross_rows(dev)
    obs_wait()
    mean, diag = g.pack_gram(scale)
    if z.rounds:
        g.hear(z.rounds)
    gram, cross = Reduction(g, "gram"), Reduction(g, "cross")
    gram.scatter()
    sums_wait()
    g.pack_lines(scale, mean_bar, own_sums, mean, diag)
    g.send_lines()
    g.pack_cross()
    cross.scatter()
    gram.start()
    lines_wait = g.sum_lines()
    gram.forward_all()
    cross.start()
    gram.pass_on()
    cross.forward_all()
    lines_wait()
    gram.finish()
    parts = g.transform(scale, gram)
    next(parts)
    cross.pass_on()
    bar_halo = next(parts)
    cross.finish()
    g.picked[0] = g.respond(scale, cross)
    pick_wait = g.between(
        g.picked.at[0], g.picked.at[1], g.picked.at[0], g.picked.at[2], g.pick_sem
    )
    g.spread(0, range(2, r + 2))
    second = g.coefficient_terms(g.sbext, 2, g.fext, 1)
    bar_halo()
    g.pull_back(g.sbext, 1, g.fbar, range(2, r), True)
    pick_wait()
    g.spread(1, (0, 1))
    g.spread(2, (r + 2, r + 3))
    g.pull_back(g.sbext, 1, g.fbar, (0, 1, r, r + 1), True)
    firsts = g.coefficient_terms(g.fbar, 1, g.pext, 2)
    g.cbuf[m] = jnp.concatenate(
        [second[i][k] + firsts[i][k] for k in range(4) for i in range(r)], axis=0
    )
    c_wait = g.mem_send(g.cbuf, g.c_sem)
    g.pull_back(g.fbar, 2, g.grad, range(r), False)
    c_wait()
    both = g.cbuf[0]
    for k in range(1, z.n_mem):
        both = both + g.cbuf[k]
    for k in range(4):
        g.coef[k] = both[k * r : (k + 1) * r]
    g.finish_sends()


def place(z, last, sums, grad, coef, scaled, sem):
    stores = [pltpu.make_async_copy(last.at[i], grad.at[:, i], sem.at[i]) for i in range(z.rows)]
    for copy in stores:
        copy.start()
    scaled[...] = sums[...] / jnp.sqrt(jnp.float32(z.total))
    stores.append(pltpu.make_async_copy(scaled, coef, sem.at[z.rows]))
    stores[-1].start()
    for copy in stores:
        copy.wait()


def local(n_space, n_mem, prior, stencil, sea_mask, sites, data, precision, cotangent):
    z = Sizes(n_space, n_mem, prior, sites)
    any_spec = pl.BlockSpec(memory_space=pl.ANY)
    turned = (z.rows, z.members, z.cols)
    factors = (4, z.rows, z.cols)
    inputs = (prior, cotangent, stencil, sea_mask, sites, data[None], precision[None])
    last, sums = pl.pallas_call(
        functools.partial(kernel, z),
        out_shape=(jax.ShapeDtypeStruct(turned, F32), jax.ShapeDtypeStruct(factors, F32)),
        in_specs=[pl.BlockSpec(memory_space=pltpu.HBM)] * 7,
        out_specs=(VMEM_SPEC, VMEM_SPEC),
        scratch_shapes=list(scratch_of(z).values()),
        compiler_params=pltpu.CompilerParams(
            collective_id=1, has_side_effects=True, vmem_limit_bytes=GRANT
        ),
        name="adjoint",
    )(*[pltpu.with_memory_space_constraint(x, pltpu.HBM) for x in inputs])
    return pl.pallas_call(
        functools.partial(place, z),
        out_shape=(jax.ShapeDtypeStruct(prior.shape, F32), jax.ShapeDtypeStruct(factors, F32)),
        in_specs=[VMEM_SPEC, VMEM_SPEC],
        out_specs=(any_spec, any_spec),
        scratch_shapes=[pltpu.VMEM(factors, F32), pltpu.SemaphoreType.DMA((z.rows + 1,))],
        compiler_params=pltpu.CompilerParams(vmem_limit_bytes=4 * 1024 * 1024),
        name="place",
    )(last, sums)


def solution(mesh):
    placed = (
        P("mem", "space", None),
        P(None, "space", None),
        P("space", None),
        P("space", None),
        P("space"),
        P("space"),
        P("mem", "space", None),
    )
    return jax.shard_map(
        functools.partial(local, mesh.shape["space"], mesh.shape["mem"]),
        mesh=mesh,
        in_specs=placed,
        out_specs=(P("mem", "space", None), P(None, "space", None)),
        check_vma=False,
    )
```

```python
import functools
import jax
import jax.numpy as jnp
from jax import lax
from jax.experimental import pallas as pl
from jax.experimental.pallas import tpu as pltpu
from jax.sharding import PartitionSpec as P

MESH = pl.DeviceIdType.MESH
F32 = jnp.float32
GRANT = 48 * 1024 * 1024
BF16 = jnp.bfloat16
VMEM_SPEC = pl.BlockSpec(memory_space=pltpu.VMEM)


def remote(src, dst, send, recv, s, m):
    return pltpu.make_async_remote_copy(
        src_ref=src, dst_ref=dst, send_sem=send, recv_sem=recv, device_id=(s, m), device_id_type=MESH
    )


def split(x):
    lead = x.astype(BF16)
    return lead, (x - lead.astype(F32)).astype(BF16)


def split3(x):
    lead = x.astype(BF16)
    rest = x - lead.astype(F32)
    middle = rest.astype(BF16)
    return lead, middle, (rest - middle.astype(F32)).astype(BF16)


def plain(a, b):
    return jnp.dot(a, b, preferred_element_type=F32)


def plain_t(a, b):
    return lax.dot_general(a, b, (((1,), (1,)), ((), ())), preferred_element_type=F32)


def mm3(a, b):
    return plain(a[0], b[0]) + (plain(a[0], b[1]) + plain(a[1], b[0]))


def mm3_t(a, b):
    return plain_t(a[0], b[0]) + (plain_t(a[0], b[1]) + plain_t(a[1], b[0]))


def whole_sum(x):
    return jnp.sum(jnp.sum(x, axis=0, keepdims=True), axis=1, keepdims=True)


def eye(size):
    return lax.broadcasted_iota(jnp.int32, (size, size), 0) == lax.broadcasted_iota(
        jnp.int32, (size, size), 1
    )


class Sizes:
    def __init__(self, n_space, n_mem, prior, sites):
        self.n_space, self.n_mem = n_space, n_mem
        self.members, self.rows, self.cols = prior.shape
        self.total = self.members * n_mem
        self.sites = sites.shape[-1]
        self.near = 2 if n_space % 2 == 0 else 1
        self.far = n_space // self.near
        self.half = 2 if n_mem % 2 == 0 else 1
        self.wide = n_mem // self.half
        self.group = max(1, self.far // 4)
        self.groups = self.far // self.group
        self.height = n_mem // 2 * self.members // n_space
        self.lines = 8 * pl.cdiv(4 + n_mem, 8)
        self.rounds = max(0, (n_space - 1).bit_length() - 1)


def scratch_of(z):
    dma = pltpu.SemaphoreType.DMA
    ext = z.rows + 4
    v = lambda *shape: pltpu.VMEM(shape, F32)
    b = lambda *shape: pltpu.VMEM(shape, BF16)
    square = (z.total, z.total)
    half_square = (z.n_space, z.height, z.members)
    gathered = (z.n_mem, z.far, z.near, z.height, z.members)
    found = dict(
        stencil=v(4, z.rows, z.cols),
        sea=pltpu.VMEM((z.rows, z.cols), jnp.int32),
        sites=pltpu.VMEM((1, z.sites), jnp.int32),
        data=v(1, z.sites),
        prec=v(1, z.sites),
        few=dma((5,)),
        token=pltpu.SemaphoreType.REGULAR((max(1, z.rounds), 2)),
        pext=v(ext, z.members, z.cols),
        aux=v(ext, 8, z.cols),
        cotf=v(ext, z.total, z.cols),
        chi=b(ext, z.total, z.cols),
        clo=b(ext, z.total, z.cols),
        seen=v(z.members, z.sites),
        beside_seen=v(2, z.n_mem, z.members, z.sites),
        slope=v(z.members, 3 * z.sites),
        fext=v(z.rows + 2, z.members, z.cols),
        state=v(z.rows, z.members, z.cols),
        hot=b(ext, z.cols, z.sites),
        obsf=v(z.n_mem, z.members, z.sites),
        ahi=b(z.total, 3 * z.sites),
        alo=b(z.total, 3 * z.sites),
        innov=v(8, 3 * z.sites),
        sums=v(z.n_mem, 8 * pl.cdiv(z.rows, 8), z.cols),
        dmat=v(z.n_mem, z.members, z.members),
        dx=v(z.n_mem, z.members, z.members),
        vec=v(z.lines, z.members),
        vbuf=v(z.n_space, z.lines, z.members),
        vout=v(z.n_mem, z.lines, z.members),
        f=v(*square),
        g=v(*square),
        fg=v(*square),
        s=v(*square),
        weigh=v(*square),
        fh=b(*square), fl=b(*square),
        f2h=b(*square), f2l=b(*square),
        gh=b(*square), gl=b(*square),
        sh=b(*square), sl=b(*square),
        lh=b(3 * z.members, z.total), ll=b(3 * z.members, z.total),
        vcol=v(z.total, z.lines),
        sbext=v(ext, z.members, z.cols),
        mixed=v(ext, z.members, z.cols),
        picked=v(z.members, 3 * z.sites),
        fbar=v(z.rows + 2, z.members, z.cols),
        cbuf=v(z.n_mem, 4 * z.rows, z.cols),
        own=dma((2, z.rows)),
        halo=dma((2, 2)),
        aux_halo=dma((2, 2)),
        bar_halo=dma((2, 2)),
        seen_halo=dma((2, 2)),
        cot_sem=dma((2, z.half, z.wide)),
        seen_sem=dma((2, z.half, z.wide)),
        obs_sem=dma((2, z.n_mem)),
        sum_sem=dma((2, z.n_mem)),
        d_sem=dma((2, z.n_mem)),
        v_sem=dma((2, z.n_space)),
        vg_sem=dma((2, z.n_mem)),
        c_sem=dma((2, z.n_mem)),
    )
    for tag in ("gram", "cross"):
        found[tag + "_src"] = v(*half_square)
        found[tag + "_buf"] = v(*half_square)
        found[tag + "_out"] = v(*gathered)
        found[tag + "_rs"] = dma((2, z.n_space))
        found[tag + "_a"] = dma((2, z.far))
        found[tag + "_x"] = dma((2, z.near, z.wide, z.groups))
        found[tag + "_q"] = dma((2, z.half, z.near, z.wide, z.groups))
    return found


class Reduction:
    def __init__(self, g, tag):
        self.g, self.z = g, g.z
        for name in ("src", "buf", "out", "rs", "a", "x", "q"):
            setattr(self, name, getattr(g, tag + "_" + name))
        z = g.z
        self.a_id, self.b_id = g.s_id // z.near, lax.rem(g.s_id, z.near)
        self.p_id, self.q_id = g.m_id // z.half, lax.rem(g.m_id, z.half)

    def scatter(self):
        z, s, m = self.z, self.g.s_id, self.g.m_id
        self.copies = []
        for k in range(1, z.n_space):
            to = lax.rem(s + k, z.n_space)
            self.copies.append(
                remote(self.src.at[to], self.buf.at[s], self.rs.at[0, k], self.rs.at[1, k], to, m)
            )
            self.copies[-1].start()
        self.g.waits += [(copy, None) for copy in self.copies]

    def start(self):
        z, s, m = self.z, self.g.s_id, self.g.m_id
        a, b = self.a_id, self.b_id
        self.buf[s] = self.src[s]
        for copy in self.copies:
            copy.wait_recv()
        total = self.buf[0]
        for k in range(1, z.n_space):
            total = total + self.buf[k]
        self.out[m, a, b] = total
        piece = self.out.at[m, a, b]
        stage = []
        for k in range(1, z.far):
            to = lax.rem(a + k, z.far) * z.near + b
            stage.append(remote(piece, piece, self.a.at[0, k], self.a.at[1, k], to, m))
            stage[-1].start()
        self.g.waits += [(copy, None) for copy in stage]
        if z.group == 1:
            self.steps = [([], a)] + [
                ([stage[k - 1]], lax.rem(a + z.far - k, z.far)) for k in range(1, z.far)
            ]
            self.forward(0)
        else:
            self.steps = [(stage if n == 0 else [], n * z.group) for n in range(z.groups)]

    def forward(self, index):
        z, s, m = self.z, self.g.s_id, self.g.m_id
        needs, start = self.steps[index]
        for copy in needs:
            copy.wait_recv()
        piece = self.out.at[m, pl.ds(start, z.group), self.b_id]
        for kb, kp in self.offsets():
            to_s = self.a_id * z.near + lax.rem(self.b_id + kb, z.near)
            to_m = lax.rem(self.p_id + kp, z.wide) * z.half + self.q_id
            self.send(piece, self.x.at[0, kb, kp, index], self.x.at[1, kb, kp, index], to_s, to_m)
        self.beside(piece, 0, 0, index)

    def forward_all(self):
        for index in range(1 if self.z.group == 1 else 0, self.z.groups):
            self.forward(index)

    def offsets(self):
        z = self.z
        return [(kb, kp) for kb in range(z.near) for kp in range(z.wide) if kb or kp]

    def send(self, piece, *where):
        copy = remote(piece, piece, *where)
        copy.start()
        self.g.waits.append((copy, None))

    def beside(self, piece, kb, kp, index):
        z = self.z
        for kq in range(1, z.half):
            to = self.p_id * z.half + lax.rem(self.q_id + kq, z.half)
            self.send(
                piece, self.q.at[0, kq, kb, kp, index], self.q.at[1, kq, kb, kp, index], self.g.s_id, to
            )

    def piece_of(self, kb, kp, kq, index):
        z = self.z
        which_b = lax.rem(self.b_id + z.near - kb, z.near)
        which_p = lax.rem(self.p_id + z.wide - kp, z.wide)
        which_q = lax.rem(self.q_id + z.half - kq, z.half)
        return self.out.at[which_p * z.half + which_q, pl.ds(self.steps[index][1], z.group), which_b]

    def pass_on(self):
        for index in range(self.z.groups):
            for kb, kp in self.offsets():
                piece = self.piece_of(kb, kp, 0, index)
                self.arrived(piece, self.x.at[0, kb, kp, index], self.x.at[1, kb, kp, index])
                self.beside(piece, kb, kp, index)

    def arrived(self, piece, send, recv):
        remote(piece, piece, send, recv, self.g.s_id, self.g.m_id).wait_recv()

    def finish(self):
        z = self.z
        for index in range(z.groups):
            for kb in range(z.near):
                for kp in range(z.wide):
                    for kq in range(1, z.half):
                        self.arrived(
                            self.piece_of(kb, kp, kq, index),
                            self.q.at[0, kq, kb, kp, index], self.q.at[1, kq, kb, kp, index],
                        )

    def whole(self, i):
        z = self.z
        return self.out[i].reshape(z.n_mem // 2 * z.members, z.members)


class Step:
    def __init__(self, z, refs):
        self.z = z
        self.__dict__.update(refs)
        self.s_id, self.m_id = lax.axis_index("space"), lax.axis_index("mem")
        self.lo = lax.rem(self.m_id, z.n_mem // 2)
        self.hi = self.m_id // (z.n_mem // 2)
        self.waits = []

    def finish_sends(self):
        for copy, when in self.waits:
            if when is None:
                copy.wait_send()
            else:
                pl.when(when)(copy.wait_send)

    def barrier(self):
        z, s, m = self.z, self.s_id, self.m_id
        peers = [(s, lax.rem(m + k, z.n_mem)) for k in range(1, z.n_mem)]
        a, b = s // z.near, lax.rem(s, z.near)
        p, q = m // z.half, lax.rem(m, z.half)
        for kb in range(1, z.near):
            for kp in range(1, z.wide):
                peers.append((
                    a * z.near + lax.rem(b + kb, z.near), lax.rem(p + kp, z.wide) * z.half + q
                ))
        barrier = pltpu.get_barrier_semaphore()
        count = len(peers)
        for peer in peers:
            pl.semaphore_signal(barrier, inc=1, device_id=peer, device_id_type=MESH)
        for step in (1, -1, 2, -2):
            there = self.exists(step)
            count = count + there.astype(jnp.int32)

            @pl.when(there)
            def _():
                pl.semaphore_signal(barrier, inc=1, device_id=(s + step, m), device_id_type=MESH)

        return lambda: pl.semaphore_wait(barrier, count)

    def exists(self, step):
        to = self.s_id + step
        return (to >= 0) & (to < self.z.n_space)

    def vouch(self, round_):
        for side, step in ((0, 2**round_), (1, -(2**round_))):
            @pl.when(self.exists(step))
            def _():
                pl.semaphore_signal(
                    self.token.at[round_ - 1, side], inc=1,
                    device_id=(self.s_id + step, self.m_id), device_id_type=MESH,
                )

    def hear(self, round_):
        for side, step in ((0, -(2**round_)), (1, 2**round_)):
            @pl.when(self.exists(step))
            def _():
                pl.semaphore_wait(self.token.at[round_ - 1, side], 1)

    def between(self, up_src, up_dst, down_src, down_dst, sem):
        z, s, m = self.z, self.s_id, self.m_id
        has_low, has_high = s > 0, s < z.n_space - 1
        up = remote(up_src, up_dst, sem.at[0, 0], sem.at[1, 0], s + 1, m)
        down = remote(down_src, down_dst, sem.at[0, 1], sem.at[1, 1], s - 1, m)
        pl.when(has_high)(up.start)
        pl.when(has_low)(down.start)
        self.waits += [(up, has_high), (down, has_low)]

        def wait():
            pl.when(has_low)(up.wait_recv)
            pl.when(has_high)(down.wait_recv)

        return wait

    def halo_send(self, ref, sem):
        r = self.z.rows
        at = lambda row: ref.at[pl.ds(row, 2)]
        return self.between(at(r), at(0), at(2), at(r + 2), sem)

    def pair_gather(self, part, sem):
        z, s, m = self.z, self.s_id, self.m_id
        p, q = m // z.half, lax.rem(m, z.half)
        across = [lax.rem(p + k, z.wide) * z.half + q for k in range(1, z.wide)]
        beside = [p * z.half + lax.rem(q + k, z.half) for k in range(1, z.half)]
        mine = part(m)
        hops, sides = [], []
        for k, to in enumerate(across):
            hops.append(remote(mine, mine, sem.at[0, 0, k + 1], sem.at[1, 0, k + 1], s, to))
            hops[-1].start()
        for k, to in enumerate(beside):
            sides.append(remote(mine, mine, sem.at[0, k + 1, 0], sem.at[1, k + 1, 0], s, to))
            sides[-1].start()

        def forward():
            for kp, hop in enumerate(hops):
                hop.wait_recv()
                piece = part(lax.rem(p + z.wide - kp - 1, z.wide) * z.half + q)
                for k, to in enumerate(beside):
                    copy = remote(
                        piece, piece, sem.at[0, k + 1, kp + 1], sem.at[1, k + 1, kp + 1], s, to
                    )
                    copy.start()
                    sides.append(copy)

        def wait():
            for copy in sides:
                copy.wait_recv()
            self.waits.extend((copy, None) for copy in hops + sides)

        return forward, wait

    def mem_send(self, ref, sem):
        z, s, m = self.z, self.s_id, self.m_id
        copies = []
        for k in range(1, z.n_mem):
            to = lax.rem(m + k, z.n_mem)
            copies.append(remote(ref.at[m], ref.at[m], sem.at[0, k], sem.at[1, k], s, to))
            copies[-1].start()

        def wait():
            for copy in copies:
                copy.wait_recv()
            self.waits.extend((copy, None) for copy in copies)

        return wait

    def block(self, which):
        size = self.z.members
        return pl.ds(pl.multiple_of(which * size, size), size)


    def coefficients(self, e):
        z = self.z
        c = [self.aux[e, k : k + 1, :] for k in range(4)]
        sea = self.aux[e, 4:5, :]
        lane = lax.broadcasted_iota(jnp.int32, (1, z.cols), 1)
        keep = sea * (1.0 - c[0] - c[1] - c[2] - c[3])
        west = jnp.where(lane == 0, 0.0, c[2])
        east = jnp.where(lane == z.cols - 1, 0.0, c[3])
        return keep, sea * c[0], sea * c[1], sea * west, sea * east

    def chunks(self):
        size = min(32, self.z.members)
        return [pl.ds(k, size) for k in range(0, self.z.members, size)]

    def advance(self, src, first, dst, count):
        z = self.z
        for i in range(count):
            keep, north, south, west, east = self.coefficients(first + i)
            for part in self.chunks():
                v = src[i + 1, part, :]
                dst[i, part, :] = (
                    keep * v
                    + north * src[i, part, :]
                    + south * src[i + 2, part, :]
                    + west * pltpu.roll(v, 1, 1)
                    + east * pltpu.roll(v, z.cols - 1, 1)
                )

    def observe(self):
        z = self.z
        picked = jnp.zeros((z.members, z.sites), F32)
        for r in range(z.rows):
            for piece in split3(self.state[r]):
                picked = picked + plain(piece, self.hot[2 + r])
        self.seen[...] = picked
        tanh = jnp.tanh(picked)
        self.slope[:, : z.sites] = 1.0 + 0.5 * (1.0 - tanh * tanh)
        return picked + 0.5 * tanh

    def observe_beside(self):
        z = self.z
        scale = jnp.sqrt(jnp.float32(z.total - 1))
        for side, e in ((0, 1), (1, z.rows + 2)):
            cols = slice((1 + side) * z.sites, (2 + side) * z.sites)
            prec, data = self.aux[e, 6:7, :], self.aux[e, 7:8, :]
            found, mean = [], jnp.zeros((1, z.sites), F32)
            for k in range(z.n_mem):
                picked = self.beside_seen[side, k]
                found.append(picked + 0.5 * jnp.tanh(picked))
                mean = mean + jnp.sum(found[-1], axis=0, keepdims=True)
            mean = mean / z.total
            for k in range(z.n_mem):
                rows = slice(k * z.members, (k + 1) * z.members)
                self.ahi[rows, cols], self.alo[rows, cols] = split((found[k] - mean) * (prec / scale))
            tanh = jnp.tanh(self.beside_seen[side, self.m_id])
            self.slope[:, cols] = 1.0 + 0.5 * (1.0 - tanh * tanh)
            self.innov[0:1, cols] = prec * (data - mean)

    def mark(self, e, row, sites):
        z = self.z
        cell = lax.broadcasted_iota(jnp.int32, (z.cols, z.sites), 0) + row * z.cols
        self.hot[e] = jnp.where(cell == sites, 1.0, 0.0).astype(BF16)

    def mark_sites(self):
        for r in range(self.z.rows):
            self.mark(2 + r, r, self.sites[...])

    def mark_sites_beside(self):
        r = self.z.rows
        low, high = (self.aux[e, 5:6, :].astype(jnp.int32) for e in (1, r + 2))
        for k in range(2):
            self.mark(k, r - 2 + k, low)
            self.mark(r + 2 + k, k, high)

    def spread(self, slot, rows):
        z = self.z
        hi, lo = split(self.picked[:, slot * z.sites : (slot + 1) * z.sites])
        for e in rows:
            field = self.mixed[e] + plain_t(hi, self.hot[e]) + plain_t(lo, self.hot[e])
            self.sbext[e] = self.aux[e, 4:5, :] * field


    def fold(self, block):
        size = self.z.members
        half = size // 2
        bottom = pltpu.roll(block[half:], half, 1)
        lane = lax.broadcasted_iota(jnp.int32, (half, size), 1)
        line = lax.broadcasted_iota(jnp.int32, (half, size), 0)
        return jnp.where(lane < line, bottom, block[:half])

    def unfold(self, folded, diagonal):
        size = self.z.members
        half = size // 2
        wide = jnp.concatenate([folded, pltpu.roll(folded, half, 1)], axis=0)
        lane = lax.broadcasted_iota(jnp.int32, (size, size), 1)
        line = lax.broadcasted_iota(jnp.int32, (size, size), 0)
        above, below = lane - line, lane - half
        straight = ((line < half) & (above >= 0)) | ((line >= half) & (below >= 0) & (above < 0))
        block = jnp.where(straight, wide, wide.T)
        return jnp.where((line >= half) & (above == 0), diagonal, block)

    def cross_rows(self, dev):
        z, s, m = self.z, self.s_id, self.m_id
        n, size = z.n_mem, z.members
        half = size // 2
        self.d_copies = []
        mean_bar = jnp.zeros((size, 1), F32)
        for k in list(range(n - 1, 0, -1)) + [0]:
            there = lax.rem(m + k, n)
            rows = self.block(there)
            part = mm3_t(dev[0], (self.chi[2, rows, :], self.clo[2, rows, :]))
            for i in range(1, z.rows):
                part = part + mm3_t(dev[i], (self.chi[2 + i, rows, :], self.clo[2 + i, rows, :]))
            mean_bar = mean_bar + jnp.sum(part, axis=1, keepdims=True)
            if 2 * k == n:
                part = jnp.where(self.hi == 0, part, part.T)
            self.dmat[k] = part
            copy = None
            if 2 * k > n:
                copy = remote(
                    self.dmat.at[k], self.dx.at[n - k], self.d_sem.at[0, k], self.d_sem.at[1, k], s, there
                )
            elif 2 * k == n:
                theirs = pl.ds(pl.multiple_of((1 - self.hi) * half, half), half)
                copy = remote(
                    self.dmat.at[k, theirs], self.dx.at[k, pl.ds(0, half)],
                    self.d_sem.at[0, k], self.d_sem.at[1, k], s, there,
                )
            if copy is not None:
                copy.start()
                self.d_copies.append(copy)
        self.waits += [(copy, None) for copy in self.d_copies]
        return mean_bar

    def pack_gram(self, scale):
        z, m = self.z, self.m_id
        n, size = z.n_mem, z.members
        half = size // 2
        mean = jnp.zeros((1, z.sites), F32)
        for k in range(n):
            mean = mean + jnp.sum(self.obsf[k], axis=0, keepdims=True)
        mean = mean / z.total
        prec = self.prec[...]
        for k in range(n):
            rows = slice(k * size, (k + 1) * size)
            self.ahi[rows, : z.sites], self.alo[rows, : z.sites] = split((self.obsf[k] - mean) * (prec / scale))
        anom = lambda rows: (self.ahi[rows, : z.sites], self.alo[rows, : z.sites])
        mine = anom(self.block(m))
        diag = mm3_t(mine, mine)
        parts = [self.fold(diag)]
        base = self.lo * size + self.hi * half
        upper = anom(pl.ds(pl.multiple_of(base, half), half))
        parts.append(mm3_t(upper, anom(self.block(self.lo + n // 2))))
        for k in range(1, n // 2):
            parts.append(mm3_t(mine, anom(self.block(lax.rem(m + k, n)))))
        self.gram_src[...] = jnp.concatenate(parts, axis=0).reshape(z.n_space, z.height, size)
        return mean, diag

    def pack_lines(self, scale, mean_bar, own_sums, mean, diag):
        z, m = self.z, self.m_id
        n, size = z.n_mem, z.members
        prec = self.prec[...]
        innov = prec * (self.data[...] - mean)
        self.innov[0:1, : z.sites] = innov
        cross = self.dmat[0]
        self.cross_diag = 0.5 * (cross + cross.T)
        exact = (self.obsf[m] - mean) * (prec / scale)
        lane = lax.broadcasted_iota(jnp.int32, (size, size), 1)
        diagonal = lambda x: jnp.sum(jnp.where(eye(size), x, 0.0), axis=1, keepdims=True)
        pull = jnp.sum(exact * innov, axis=1, keepdims=True)
        columns = [pull, mean_bar, diagonal(self.cross_diag), diagonal(diag)]
        stacked = jnp.zeros((size, size), F32)
        for k, column in enumerate(columns):
            stacked = jnp.where(lane == k, column, stacked)
        total = self.sums[0]
        for k in range(1, n):
            total = total + self.sums[k]
        term = None
        for r in range(z.rows):
            lacks = (own_sums[r] / size - total[r : r + 1] / z.total) / scale
            this = mm3_t(split(jnp.broadcast_to(lacks, (8, z.cols))), (self.chi[2 + r], self.clo[2 + r]))
            term = this if term is None else term + this
        lines = [stacked.T[:4]] + [term[:1, k * size : (k + 1) * size] for k in range(n)]
        if z.lines > 4 + n:
            lines.append(jnp.zeros((z.lines - 4 - n, size), F32))
        self.vec[...] = jnp.concatenate(lines, axis=0)

    def pack_cross(self):
        z = self.z
        n, size = z.n_mem, z.members
        half = size // 2
        for copy in self.d_copies:
            copy.wait_recv()
        parts = [self.fold(self.cross_diag)]
        ours = pl.ds(pl.multiple_of(self.hi * half, half), half)
        parts.append(0.5 * (self.dmat[n // 2, ours] + self.dx[n // 2, pl.ds(0, half)]))
        for k in range(1, n // 2):
            parts.append(0.5 * (self.dmat[k] + self.dx[k].T))
        self.cross_src[...] = jnp.concatenate(parts, axis=0).reshape(z.n_space, z.height, size)

    def send_lines(self):
        z, s, m = self.z, self.s_id, self.m_id
        self.tiny = []
        for k in range(1, z.n_space):
            to = lax.rem(s + k, z.n_space)
            self.tiny.append(
                remote(self.vec, self.vbuf.at[s], self.v_sem.at[0, k], self.v_sem.at[1, k], to, m)
            )
            self.tiny[-1].start()
        self.waits += [(copy, None) for copy in self.tiny]

    def sum_lines(self):
        self.vbuf[self.s_id] = self.vec[...]
        for copy in self.tiny:
            copy.wait_recv()
        vec = self.vbuf[0]
        for k in range(1, self.z.n_space):
            vec = vec + self.vbuf[k]
        self.vout[self.m_id] = vec
        return self.mem_send(self.vout, self.vg_sem)

    def blocks_of(self, reduction, line):
        z = self.z
        n, size = z.n_mem, z.members
        half = size // 2
        wholes = [reduction.whole(i) for i in range(n)]
        for i in range(n):
            yield i, i, self.unfold(wholes[i][:half], self.vout[i, line : line + 1, :])
        for i in range(n // 2):
            j = i + n // 2
            yield i, j, jnp.concatenate([wholes[i][half:size], wholes[j][half:size]], axis=0)
        for i in range(n):
            for k in range(1, n // 2):
                yield i, (i + k) % n, wholes[i][k * size : (k + 1) * size]


    def transform(self, scale, gram):
        z, m = self.z, self.m_id
        n, size, total = z.n_mem, z.members, z.total
        mine = self.block(m)
        col = lambda k: slice(k * size, (k + 1) * size)
        squares = jnp.zeros((size, size), F32)
        for i, j, block in self.blocks_of(gram, 3):
            if i == j:
                block = block + eye(size).astype(F32)
                squares = squares + block * block
            else:
                self.f[col(j), col(i)] = block.T
                squares = squares + 2.0 * (block * block)
            self.f[col(i), col(j)] = block
        norm = jnp.sqrt(whole_sum(squares))
        root = jnp.sqrt(norm)
        identity = eye(total).astype(F32)
        f = 1.5 * identity - (0.5 / norm) * self.f[...]
        self.f[...] = f
        self.fh[...], self.fl[...] = split(f)
        f_split = (self.fh[...], self.fl[...])
        f2 = mm3(f_split, f_split)
        self.f2h[...], self.f2l[...] = split(f2)
        g = f2 - 1.5 * self.f[...]
        self.g[...] = g
        self.gh[...], self.gl[...] = split(g)
        g_split = (self.gh[...], self.gl[...])
        yield
        p = 1.5 * self.f[...] + mm3((self.f2h[...], self.f2l[...]), g_split)
        self.s[...] = p
        p_split = split(p)
        kind = lax.broadcasted_iota(jnp.int32, (z.lines, size), 0)
        self.lines = []
        for i in range(n):
            lines = self.vout[i]
            lacks = jnp.sum(jnp.sum(lines[4 : 4 + n], axis=0, keepdims=True), axis=1, keepdims=True)
            self.lines.append(jnp.where(kind == 1, lines + lacks, jnp.where(kind == 3, 1.0, lines)))
        rows = jnp.concatenate(self.lines, axis=1)
        self.first = mm3(split(rows), p_split) / root
        second = mm3(split(self.first), p_split) / root
        self.vcol[...] = second.T
        self.pull_bar = second[1:2]
        self.pull_mine = self.vcol[mine, 1:2] - jnp.sum(self.pull_bar, axis=1, keepdims=True) / total
        mix = self.s[mine, :] / root + self.vcol[mine, 0:1] / scale
        row_weights = self.first[3:4] + jnp.sum(second[0:1], axis=1, keepdims=True) / scale
        mix = split(mix + (1.0 - row_weights) / total)
        for e in range(2, z.rows + 2):
            self.mixed[e] = mm3(mix, (self.chi[e], self.clo[e]))
        bar_halo = self.halo_send(self.mixed, self.bar_halo)
        self.fg[...] = mm3((self.fh[...], self.fl[...]), g_split)
        self.weigh[...] = 2.25 * identity + 4.5 * (self.fg[...] + self.f[...] - self.s[...])
        self.norm, self.root = norm, root
        for k, ref in enumerate((self.f, self.g, self.fg)):
            rows = slice(k * size, (k + 1) * size)
            self.lh[rows, :], self.ll[rows, :] = split(self.centred(ref))
        yield bar_halo

    def centred(self, ref):
        return ref[self.block(self.m_id), :] - jnp.sum(ref[...], axis=0, keepdims=True) / self.z.total

    def respond(self, scale, cross):
        z, m = self.z, self.m_id
        n, size, total = z.n_mem, z.members, z.total
        col = lambda k: slice(k * size, (k + 1) * size)
        norm, root = self.norm, self.root
        turned = [x.T for x in self.lines]
        first_t = self.first.T
        for i, j, block in self.blocks_of(cross, 2):
            block = (scale / root) * (
                block + 0.5 * (self.lines[i][4 + j : 5 + j] + turned[j][:, 4 + i : 5 + i])
            ) + (0.5 / root) * (
                turned[i][:, 1:2] * self.first[0:1, col(j)]
                + first_t[col(i), 0:1] * self.lines[j][1:2]
                + first_t[col(i), 1:2] * self.lines[j][0:1]
                + turned[i][:, 0:1] * self.first[1:2, col(j)]
            )
            self.s[col(i), col(j)] = block
            if i != j:
                self.s[col(j), col(i)] = block.T
        scale_bar = whole_sum(self.s[...] * self.weigh[...]) / norm
        self.sh[...], self.sl[...] = split(self.s[...])
        s_split = (self.sh[...], self.sl[...])
        s_mine = self.centred(self.s)
        f_split = (self.fh[...], self.fl[...])
        through = mm3((self.lh[...], self.ll[...]), s_split)
        bar = 1.5 * s_mine + through[2 * size :]
        bar = bar + mm3(split(mm3(split(s_mine), f_split)), (self.gh[...], self.gl[...]))
        bar = bar + mm3(split(through[:size]), (self.f2h[...], self.f2l[...]))
        bar = bar + mm3(split(through[size : 2 * size]), f_split)
        unit = (
            lax.broadcasted_iota(jnp.int32, (size, total), 0) + m * size
            == lax.broadcasted_iota(jnp.int32, (size, total), 1)
        ).astype(F32) - 1.0 / total
        sym = 2.0 * scale_bar * (3.0 * unit - 2.0 * self.centred(self.f)) - bar / norm
        sym = sym - (scale / total) * self.pull_bar
        prec = [self.prec[...], self.aux[1, 6:7, :], self.aux[z.rows + 2, 6:7, :]]
        observed = (jnp.concatenate(prec, axis=1) / scale) * (
            mm3(split(sym), (self.ahi[...], self.alo[...])) + self.pull_mine * self.innov[0:1, :]
        )
        return observed * self.slope[...]


    def pull_back(self, src, first, dst, rows, to_sea):
        z = self.z
        for i in rows:
            e = first + i
            c = [self.aux[e, k : k + 1, :] for k in range(4)]
            lane = lax.broadcasted_iota(jnp.int32, (1, z.cols), 1)
            keep = 1.0 - c[0] - c[1] - c[2] - c[3]
            from_south, from_north = self.aux[e + 1, 0:1, :], self.aux[e - 1, 1:2, :]
            sea = self.aux[e, 4:5, :]
            east = pltpu.roll(jnp.broadcast_to(jnp.where(lane == 0, 0.0, c[2]), (8, z.cols)), z.cols - 1, 1)[:1]
            west = pltpu.roll(jnp.broadcast_to(jnp.where(lane == z.cols - 1, 0.0, c[3]), (8, z.cols)), 1, 1)[:1]
            if to_sea:
                keep, from_south, from_north = sea * keep, sea * from_south, sea * from_north
                east, west = sea * east, sea * west
            for part in self.chunks():
                v = src[i + 1, part, :]
                dst[i, part, :] = (
                    keep * v
                    + from_south * src[i + 2, part, :]
                    + from_north * src[i, part, :]
                    + east * pltpu.roll(v, z.cols - 1, 1)
                    + west * pltpu.roll(v, 1, 1)
                )

    def coefficient_terms(self, weight, w0, field, f0):
        z = self.z
        lane = lax.broadcasted_iota(jnp.int32, (1, z.cols), 1)
        rows = []
        for r in range(z.rows):
            sums = [0.0] * 5
            for part in self.chunks():
                w = weight[w0 + r, part, :]
                c = field[f0 + r, part, :]
                terms = [
                    w * field[f0 + r - 1, part, :],
                    w * field[f0 + r + 1, part, :],
                    w * pltpu.roll(c, 1, 1),
                    w * pltpu.roll(c, z.cols - 1, 1),
                    w * c,
                ]
                sums = [x + y for x, y in zip(sums, terms)]
            north, south, west, east, own = [jnp.sum(x, axis=0, keepdims=True) for x in sums]
            west = jnp.where(lane == 0, 0.0, west)
            east = jnp.where(lane == z.cols - 1, 0.0, east)
            rows.append([north - own, south - own, west - own, east - own])
        return rows


def kernel(z, *refs):
    small = ["stencil", "sea", "sites", "data", "prec"]
    names = ["prior", "cot"] + [name + "_in" for name in small] + ["grad", "coef"]
    names += list(scratch_of(z))
    g = Step(z, dict(zip(names, refs)))
    scale = jnp.sqrt(jnp.float32(z.total - 1))
    s, m = g.s_id, g.m_id
    r, ext = z.rows, z.rows + 4
    mine = g.block(m)

    entered = g.barrier()
    loads = []
    for i in range(r):
        loads.append(pltpu.make_async_copy(g.prior.at[:, i], g.pext.at[2 + i], g.own.at[0, i]))
    for i in range(r):
        loads.append(pltpu.make_async_copy(g.cot.at[:, i], g.cotf.at[2 + i, mine], g.own.at[1, i]))
    few = [
        pltpu.make_async_copy(getattr(g, name + "_in"), getattr(g, name), g.few.at[i])
        for i, name in enumerate(small)
    ]
    for copy in loads[:r] + few + loads[r:]:
        copy.start()
    for copy in few:
        copy.wait()
    for i in range(r):
        g.aux[2 + i, 0:4, :] = g.stencil[:, i, :]
        g.aux[2 + i, 4:5, :] = g.sea[i : i + 1, :].astype(F32)
        g.aux[2 + i, 5:6, :] = g.sites[...].astype(F32)
        g.aux[2 + i, 6:7, :] = g.prec[...]
        g.aux[2 + i, 7:8, :] = g.data[...]
    for e, edge in ((0, 0), (1, 0), (ext - 2, z.n_space - 1), (ext - 1, z.n_space - 1)):
        @pl.when(s == edge)
        def _():
            g.pext[e] = jnp.zeros((z.members, z.cols), F32)
            g.mixed[e] = jnp.zeros((z.members, z.cols), F32)
            g.aux[e] = jnp.zeros((8, z.cols), F32)
            g.beside_seen[0 if e < 2 else 1, m] = jnp.zeros((z.members, z.sites), F32)
    for copy in loads[:r]:
        copy.wait()
    entered()
    halo = g.halo_send(g.pext, g.halo)
    if z.rounds:
        g.vouch(1)
    for copy in loads[r:]:
        copy.wait()
    cot_forward, cot_wait = g.pair_gather(lambda which: g.cotf.at[pl.ds(2, r), g.block(which)], g.cot_sem)
    aux_halo = g.halo_send(g.aux, g.aux_halo)
    g.mark_sites()
    aux_halo()
    g.mark_sites_beside()
    cot_forward()
    for k in range(1, z.rounds):
        g.hear(k)
        g.vouch(k + 1)
    halo()

    g.advance(g.pext, 1, g.fext, r + 2)
    g.advance(g.fext, 2, g.state, r)
    g.obsf[m] = g.observe()
    obs_wait = g.mem_send(g.obsf, g.obs_sem)
    own_sums = [jnp.sum(g.state[i], axis=0, keepdims=True) for i in range(r)]
    padding = [jnp.zeros((-r % 8, z.cols), F32)] * (r % 8 > 0)
    g.sums[m] = jnp.concatenate(own_sums + padding, axis=0)
    sums_wait = g.mem_send(g.sums, g.sum_sem)
    seen_halo = g.between(
        g.seen, g.beside_seen.at[0, m], g.seen, g.beside_seen.at[1, m], g.seen_halo
    )
    cot_wait()
    for e in range(2, r + 2):
        g.chi[e], g.clo[e] = split(g.cotf[e])
    dev = [split((g.state[i] - own_sums[i] / z.members) / scale) for i in range(r)]
    mean_bar = g.cross_rows(dev)
    obs_wait()
    mean, diag = g.pack_gram(scale)
    if z.rounds:
        g.hear(z.rounds)
    gram, cross = Reduction(g, "gram"), Reduction(g, "cross")
    gram.scatter()
    sums_wait()
    g.pack_lines(scale, mean_bar, own_sums, mean, diag)
    g.send_lines()
    g.pack_cross()
    cross.scatter()
    seen_halo()
    extras = [
        g.pair_gather(lambda which: g.beside_seen.at[:, which], g.seen_sem),
    ]
    gram.start()
    lines_wait = g.sum_lines()
    for forward, _ in extras:
        forward()
    gram.forward_all()
    cross.start()
    for _, wait in extras:
        wait()
    g.observe_beside()
    gram.pass_on()
    cross.forward_all()
    lines_wait()
    gram.finish()
    parts = g.transform(scale, gram)
    next(parts)
    cross.pass_on()
    bar_halo = next(parts)
    cross.finish()
    g.picked[...] = g.respond(scale, cross)
    g.spread(0, range(2, r + 2))
    second = g.coefficient_terms(g.sbext, 2, g.fext, 1)
    g.pull_back(g.sbext, 1, g.fbar, range(2, r), True)
    bar_halo()
    g.spread(1, (0, 1))
    g.spread(2, (r + 2, r + 3))
    g.pull_back(g.sbext, 1, g.fbar, (0, 1, r, r + 1), True)
    firsts = g.coefficient_terms(g.fbar, 1, g.pext, 2)
    g.cbuf[m] = jnp.concatenate(
        [second[i][k] + firsts[i][k] for k in range(4) for i in range(r)], axis=0
    )
    c_wait = g.mem_send(g.cbuf, g.c_sem)
    g.pull_back(g.fbar, 2, g.grad, range(r), False)
    c_wait()
    both = g.cbuf[0]
    for k in range(1, z.n_mem):
        both = both + g.cbuf[k]
    for k in range(4):
        g.coef[k] = both[k * r : (k + 1) * r]
    g.finish_sends()


def place(z, last, sums, grad, coef, scaled, sem):
    stores = [pltpu.make_async_copy(last.at[i], grad.at[:, i], sem.at[i]) for i in range(z.rows)]
    for copy in stores:
        copy.start()
    scaled[...] = sums[...] / jnp.sqrt(jnp.float32(z.total))
    stores.append(pltpu.make_async_copy(scaled, coef, sem.at[z.rows]))
    stores[-1].start()
    for copy in stores:
        copy.wait()


def local(n_space, n_mem, prior, stencil, sea_mask, sites, data, precision, cotangent):
    z = Sizes(n_space, n_mem, prior, sites)
    any_spec = pl.BlockSpec(memory_space=pl.ANY)
    turned = (z.rows, z.members, z.cols)
    factors = (4, z.rows, z.cols)
    inputs = (prior, cotangent, stencil, sea_mask, sites, data[None], precision[None])
    last, sums = pl.pallas_call(
        functools.partial(kernel, z),
        out_shape=(jax.ShapeDtypeStruct(turned, F32), jax.ShapeDtypeStruct(factors, F32)),
        in_specs=[pl.BlockSpec(memory_space=pltpu.HBM)] * 7,
        out_specs=(VMEM_SPEC, VMEM_SPEC),
        scratch_shapes=list(scratch_of(z).values()),
        compiler_params=pltpu.CompilerParams(
            collective_id=1, has_side_effects=True, vmem_limit_bytes=GRANT
        ),
        name="adjoint",
    )(*[pltpu.with_memory_space_constraint(x, pltpu.HBM) for x in inputs])
    return pl.pallas_call(
        functools.partial(place, z),
        out_shape=(jax.ShapeDtypeStruct(prior.shape, F32), jax.ShapeDtypeStruct(factors, F32)),
        in_specs=[VMEM_SPEC, VMEM_SPEC],
        out_specs=(any_spec, any_spec),
        scratch_shapes=[pltpu.VMEM(factors, F32), pltpu.SemaphoreType.DMA((z.rows + 1,))],
        compiler_params=pltpu.CompilerParams(vmem_limit_bytes=4 * 1024 * 1024),
        name="place",
    )(last, sums)


def solution(mesh):
    placed = (
        P("mem", "space", None),
        P(None, "space", None),
        P("space", None),
        P("space", None),
        P("space"),
        P("space"),
        P("mem", "space", None),
    )
    return jax.shard_map(
        functools.partial(local, mesh.shape["space"], mesh.shape["mem"]),
        mesh=mesh,
        in_specs=placed,
        out_specs=(P("mem", "space", None), P(None, "space", None)),
        check_vma=False,
    )
```

```python
import functools
import jax
import jax.numpy as jnp
from jax import lax
from jax.experimental import pallas as pl
from jax.experimental.pallas import tpu as pltpu
from jax.sharding import PartitionSpec as P

MESH = pl.DeviceIdType.MESH
F32 = jnp.float32
GRANT = 48 * 1024 * 1024
BF16 = jnp.bfloat16
VMEM_SPEC = pl.BlockSpec(memory_space=pltpu.VMEM)


def remote(src, dst, send, recv, s, m):
    return pltpu.make_async_remote_copy(
        src_ref=src, dst_ref=dst, send_sem=send, recv_sem=recv, device_id=(s, m), device_id_type=MESH
    )


def split(x):
    lead = x.astype(BF16)
    return lead, (x - lead.astype(F32)).astype(BF16)


def split3(x):
    lead = x.astype(BF16)
    rest = x - lead.astype(F32)
    middle = rest.astype(BF16)
    return lead, middle, (rest - middle.astype(F32)).astype(BF16)


def plain(a, b):
    return jnp.dot(a, b, preferred_element_type=F32)


def plain_t(a, b):
    return lax.dot_general(a, b, (((1,), (1,)), ((), ())), preferred_element_type=F32)


def mm3(a, b):
    return plain(a[0], b[0]) + (plain(a[0], b[1]) + plain(a[1], b[0]))


def mm3_t(a, b):
    return plain_t(a[0], b[0]) + (plain_t(a[0], b[1]) + plain_t(a[1], b[0]))


def whole_sum(x):
    return jnp.sum(jnp.sum(x, axis=0, keepdims=True), axis=1, keepdims=True)


def eye(size):
    return lax.broadcasted_iota(jnp.int32, (size, size), 0) == lax.broadcasted_iota(
        jnp.int32, (size, size), 1
    )


class Sizes:
    def __init__(self, n_space, n_mem, prior, sites):
        self.n_space, self.n_mem = n_space, n_mem
        self.members, self.rows, self.cols = prior.shape
        self.total = self.members * n_mem
        self.sites = sites.shape[-1]
        self.near = 2 if n_space % 2 == 0 else 1
        self.far = n_space // self.near
        self.half = 2 if n_mem % 2 == 0 else 1
        self.wide = n_mem // self.half
        self.group = max(1, self.far // 4)
        self.groups = self.far // self.group
        self.height = n_mem // 2 * self.members // n_space
        self.lines = 8 * pl.cdiv(4 + n_mem, 8)
        self.rounds = max(0, (n_space - 1).bit_length() - 1)


def scratch_of(z):
    dma = pltpu.SemaphoreType.DMA
    ext = z.rows + 4
    v = lambda *shape: pltpu.VMEM(shape, F32)
    b = lambda *shape: pltpu.VMEM(shape, BF16)
    square = (z.total, z.total)
    half_square = (z.n_space, z.height, z.members)
    gathered = (z.n_mem, z.far, z.near, z.height, z.members)
    found = dict(
        stencil=v(4, z.rows, z.cols),
        sea=pltpu.VMEM((z.rows, z.cols), jnp.int32),
        sites=pltpu.VMEM((1, z.sites), jnp.int32),
        data=v(1, z.sites),
        prec=v(1, z.sites),
        few=dma((5,)),
        token=pltpu.SemaphoreType.REGULAR((max(1, z.rounds), 2)),
        pext=v(ext, z.members, z.cols),
        aux=v(ext, 8, z.cols),
        cotf=v(ext, z.total, z.cols),
        chi=b(ext, z.total, z.cols),
        clo=b(ext, z.total, z.cols),
        seen=v(z.members, z.sites),
        beside_seen=v(2, z.n_mem, z.members, z.sites),
        slope=v(z.members, 3 * z.sites),
        fext=v(z.rows + 2, z.members, z.cols),
        state=v(z.rows, z.members, z.cols),
        hot=b(ext, z.cols, z.sites),
        obsf=v(z.n_mem, z.members, z.sites),
        ahi=b(z.total, 3 * z.sites),
        alo=b(z.total, 3 * z.sites),
        innov=v(8, 3 * z.sites),
        sums=v(z.n_mem, 8 * pl.cdiv(z.rows, 8), z.cols),
        dmat=v(z.n_mem, z.members, z.members),
        dx=v(z.n_mem, z.members, z.members),
        vec=v(z.lines, z.members),
        vbuf=v(z.n_space, z.lines, z.members),
        vout=v(z.n_mem, z.lines, z.members),
        f=v(*square),
        g=v(*square),
        fg=v(*square),
        s=v(*square),
        weigh=v(*square),
        fh=b(*square), fl=b(*square),
        f2h=b(*square), f2l=b(*square),
        gh=b(*square), gl=b(*square),
        sh=b(*square), sl=b(*square),
        lh=b(3 * z.members, z.total), ll=b(3 * z.members, z.total),
        vcol=v(z.total, z.lines),
        sbext=v(ext, z.members, z.cols),
        mixed=v(ext, z.members, z.cols),
        picked=v(z.members, 3 * z.sites),
        fbar=v(z.rows + 2, z.members, z.cols),
        cbuf=v(z.n_mem, 4 * z.rows, z.cols),
        own=dma((2, z.rows)),
        halo=dma((2, 2)),
        aux_halo=dma((2, 2)),
        bar_halo=dma((2, 2)),
        far_halo=dma((2, 2)),
        seen_halo=dma((2, 2)),
        cot_sem=dma((2, z.half, z.wide)),
        seen_sem=dma((2, z.half, z.wide)),
        obs_sem=dma((2, z.n_mem)),
        sum_sem=dma((2, z.n_mem)),
        d_sem=dma((2, z.n_mem)),
        v_sem=dma((2, z.n_space)),
        vg_sem=dma((2, z.n_mem)),
        c_sem=dma((2, z.n_mem)),
    )
    for tag in ("gram", "cross"):
        found[tag + "_src"] = v(*half_square)
        found[tag + "_buf"] = v(*half_square)
        found[tag + "_out"] = v(*gathered)
        found[tag + "_rs"] = dma((2, z.n_space))
        found[tag + "_a"] = dma((2, z.far))
        found[tag + "_x"] = dma((2, z.near, z.wide, z.groups))
        found[tag + "_q"] = dma((2, z.half, z.near, z.wide, z.groups))
    return found


class Reduction:
    def __init__(self, g, tag):
        self.g, self.z = g, g.z
        for name in ("src", "buf", "out", "rs", "a", "x", "q"):
            setattr(self, name, getattr(g, tag + "_" + name))
        z = g.z
        self.a_id, self.b_id = g.s_id // z.near, lax.rem(g.s_id, z.near)
        self.p_id, self.q_id = g.m_id // z.half, lax.rem(g.m_id, z.half)

    def scatter(self):
        z, s, m = self.z, self.g.s_id, self.g.m_id
        self.copies = []
        for k in range(1, z.n_space):
            to = lax.rem(s + k, z.n_space)
            self.copies.append(
                remote(self.src.at[to], self.buf.at[s], self.rs.at[0, k], self.rs.at[1, k], to, m)
            )
            self.copies[-1].start()
        self.g.waits += [(copy, None) for copy in self.copies]

    def start(self):
        z, s, m = self.z, self.g.s_id, self.g.m_id
        a, b = self.a_id, self.b_id
        self.buf[s] = self.src[s]
        for copy in self.copies:
            copy.wait_recv()
        total = self.buf[0]
        for k in range(1, z.n_space):
            total = total + self.buf[k]
        self.out[m, a, b] = total
        piece = self.out.at[m, a, b]
        stage = []
        for k in range(1, z.far):
            to = lax.rem(a + k, z.far) * z.near + b
            stage.append(remote(piece, piece, self.a.at[0, k], self.a.at[1, k], to, m))
            stage[-1].start()
        self.g.waits += [(copy, None) for copy in stage]
        if z.group == 1:
            self.steps = [([], a)] + [
                ([stage[k - 1]], lax.rem(a + z.far - k, z.far)) for k in range(1, z.far)
            ]
            self.forward(0)
        else:
            self.steps = [(stage if n == 0 else [], n * z.group) for n in range(z.groups)]

    def forward(self, index):
        z, s, m = self.z, self.g.s_id, self.g.m_id
        needs, start = self.steps[index]
        for copy in needs:
            copy.wait_recv()
        piece = self.out.at[m, pl.ds(start, z.group), self.b_id]
        for kb, kp in self.offsets():
            to_s = self.a_id * z.near + lax.rem(self.b_id + kb, z.near)
            to_m = lax.rem(self.p_id + kp, z.wide) * z.half + self.q_id
            self.send(piece, self.x.at[0, kb, kp, index], self.x.at[1, kb, kp, index], to_s, to_m)
        self.beside(piece, 0, 0, index)

    def forward_all(self):
        for index in range(1 if self.z.group == 1 else 0, self.z.groups):
            self.forward(index)

    def offsets(self):
        z = self.z
        return [(kb, kp) for kb in range(z.near) for kp in range(z.wide) if kb or kp]

    def send(self, piece, *where):
        copy = remote(piece, piece, *where)
        copy.start()
        self.g.waits.append((copy, None))

    def beside(self, piece, kb, kp, index):
        z = self.z
        for kq in range(1, z.half):
            to = self.p_id * z.half + lax.rem(self.q_id + kq, z.half)
            self.send(
                piece, self.q.at[0, kq, kb, kp, index], self.q.at[1, kq, kb, kp, index], self.g.s_id, to
            )

    def piece_of(self, kb, kp, kq, index):
        z = self.z
        which_b = lax.rem(self.b_id + z.near - kb, z.near)
        which_p = lax.rem(self.p_id + z.wide - kp, z.wide)
        which_q = lax.rem(self.q_id + z.half - kq, z.half)
        return self.out.at[which_p * z.half + which_q, pl.ds(self.steps[index][1], z.group), which_b]

    def pass_on(self):
        for index in range(self.z.groups):
            for kb, kp in self.offsets():
                piece = self.piece_of(kb, kp, 0, index)
                self.arrived(piece, self.x.at[0, kb, kp, index], self.x.at[1, kb, kp, index])
                self.beside(piece, kb, kp, index)

    def arrived(self, piece, send, recv):
        remote(piece, piece, send, recv, self.g.s_id, self.g.m_id).wait_recv()

    def finish(self):
        z = self.z
        for index in range(z.groups):
            for kb in range(z.near):
                for kp in range(z.wide):
                    for kq in range(1, z.half):
                        self.arrived(
                            self.piece_of(kb, kp, kq, index),
                            self.q.at[0, kq, kb, kp, index], self.q.at[1, kq, kb, kp, index],
                        )

    def whole(self, i):
        z = self.z
        return self.out[i].reshape(z.n_mem // 2 * z.members, z.members)


class Step:
    def __init__(self, z, refs):
        self.z = z
        self.__dict__.update(refs)
        self.s_id, self.m_id = lax.axis_index("space"), lax.axis_index("mem")
        self.lo = lax.rem(self.m_id, z.n_mem // 2)
        self.hi = self.m_id // (z.n_mem // 2)
        self.waits = []

    def finish_sends(self):
        for copy, when in self.waits:
            if when is None:
                copy.wait_send()
            else:
                pl.when(when)(copy.wait_send)

    def barrier(self):
        z, s, m = self.z, self.s_id, self.m_id
        peers = [(s, lax.rem(m + k, z.n_mem)) for k in range(1, z.n_mem)]
        a, b = s // z.near, lax.rem(s, z.near)
        p, q = m // z.half, lax.rem(m, z.half)
        for kb in range(1, z.near):
            for kp in range(1, z.wide):
                peers.append((
                    a * z.near + lax.rem(b + kb, z.near), lax.rem(p + kp, z.wide) * z.half + q
                ))
        barrier = pltpu.get_barrier_semaphore()
        count = len(peers)
        for peer in peers:
            pl.semaphore_signal(barrier, inc=1, device_id=peer, device_id_type=MESH)
        for step in (1, -1, 2, -2):
            there = self.exists(step)
            count = count + there.astype(jnp.int32)

            @pl.when(there)
            def _():
                pl.semaphore_signal(barrier, inc=1, device_id=(s + step, m), device_id_type=MESH)

        return lambda: pl.semaphore_wait(barrier, count)

    def exists(self, step):
        to = self.s_id + step
        return (to >= 0) & (to < self.z.n_space)

    def vouch(self, round_):
        for side, step in ((0, 2**round_), (1, -(2**round_))):
            @pl.when(self.exists(step))
            def _():
                pl.semaphore_signal(
                    self.token.at[round_ - 1, side], inc=1,
                    device_id=(self.s_id + step, self.m_id), device_id_type=MESH,
                )

    def hear(self, round_):
        for side, step in ((0, -(2**round_)), (1, 2**round_)):
            @pl.when(self.exists(step))
            def _():
                pl.semaphore_wait(self.token.at[round_ - 1, side], 1)

    def between(self, up_src, up_dst, down_src, down_dst, sem):
        z, s, m = self.z, self.s_id, self.m_id
        has_low, has_high = s > 0, s < z.n_space - 1
        up = remote(up_src, up_dst, sem.at[0, 0], sem.at[1, 0], s + 1, m)
        down = remote(down_src, down_dst, sem.at[0, 1], sem.at[1, 1], s - 1, m)
        pl.when(has_high)(up.start)
        pl.when(has_low)(down.start)
        self.waits += [(up, has_high), (down, has_low)]

        def wait():
            pl.when(has_low)(up.wait_recv)
            pl.when(has_high)(down.wait_recv)

        return wait

    def halo_send(self, ref, sem):
        r = self.z.rows
        at = lambda row: ref.at[pl.ds(row, 2)]
        return self.between(at(r), at(0), at(2), at(r + 2), sem)

    def pair_gather(self, part, sem):
        z, s, m = self.z, self.s_id, self.m_id
        p, q = m // z.half, lax.rem(m, z.half)
        across = [lax.rem(p + k, z.wide) * z.half + q for k in range(1, z.wide)]
        beside = [p * z.half + lax.rem(q + k, z.half) for k in range(1, z.half)]
        mine = part(m)
        hops, sides = [], []
        for k, to in enumerate(across):
            hops.append(remote(mine, mine, sem.at[0, 0, k + 1], sem.at[1, 0, k + 1], s, to))
            hops[-1].start()
        for k, to in enumerate(beside):
            sides.append(remote(mine, mine, sem.at[0, k + 1, 0], sem.at[1, k + 1, 0], s, to))
            sides[-1].start()

        def forward():
            for kp, hop in enumerate(hops):
                hop.wait_recv()
                piece = part(lax.rem(p + z.wide - kp - 1, z.wide) * z.half + q)
                for k, to in enumerate(beside):
                    copy = remote(
                        piece, piece, sem.at[0, k + 1, kp + 1], sem.at[1, k + 1, kp + 1], s, to
                    )
                    copy.start()
                    sides.append(copy)

        def wait():
            for copy in sides:
                copy.wait_recv()
            self.waits.extend((copy, None) for copy in hops + sides)

        return forward, wait

    def mem_send(self, ref, sem):
        z, s, m = self.z, self.s_id, self.m_id
        copies = []
        for k in range(1, z.n_mem):
            to = lax.rem(m + k, z.n_mem)
            copies.append(remote(ref.at[m], ref.at[m], sem.at[0, k], sem.at[1, k], s, to))
            copies[-1].start()

        def wait():
            for copy in copies:
                copy.wait_recv()
            self.waits.extend((copy, None) for copy in copies)

        return wait

    def block(self, which):
        size = self.z.members
        return pl.ds(pl.multiple_of(which * size, size), size)


    def coefficients(self, e):
        z = self.z
        c = [self.aux[e, k : k + 1, :] for k in range(4)]
        sea = self.aux[e, 4:5, :]
        lane = lax.broadcasted_iota(jnp.int32, (1, z.cols), 1)
        keep = sea * (1.0 - c[0] - c[1] - c[2] - c[3])
        west = jnp.where(lane == 0, 0.0, c[2])
        east = jnp.where(lane == z.cols - 1, 0.0, c[3])
        return keep, sea * c[0], sea * c[1], sea * west, sea * east

    def chunks(self):
        size = min(32, self.z.members)
        return [pl.ds(k, size) for k in range(0, self.z.members, size)]

    def advance(self, src, first, dst, count):
        z = self.z
        for i in range(count):
            keep, north, south, west, east = self.coefficients(first + i)
            for part in self.chunks():
                v = src[i + 1, part, :]
                dst[i, part, :] = (
                    keep * v
                    + north * src[i, part, :]
                    + south * src[i + 2, part, :]
                    + west * pltpu.roll(v, 1, 1)
                    + east * pltpu.roll(v, z.cols - 1, 1)
                )

    def observe(self):
        z = self.z
        picked = jnp.zeros((z.members, z.sites), F32)
        for r in range(z.rows):
            for piece in split3(self.state[r]):
                picked = picked + plain(piece, self.hot[2 + r])
        self.seen[...] = picked
        tanh = jnp.tanh(picked)
        self.slope[:, : z.sites] = 1.0 + 0.5 * (1.0 - tanh * tanh)
        return picked + 0.5 * tanh

    def observe_beside(self):
        z = self.z
        scale = jnp.sqrt(jnp.float32(z.total - 1))
        for side, e in ((0, 1), (1, z.rows + 2)):
            cols = slice((1 + side) * z.sites, (2 + side) * z.sites)
            prec, data = self.aux[e, 6:7, :], self.aux[e, 7:8, :]
            found, mean = [], jnp.zeros((1, z.sites), F32)
            for k in range(z.n_mem):
                picked = self.beside_seen[side, k]
                found.append(picked + 0.5 * jnp.tanh(picked))
                mean = mean + jnp.sum(found[-1], axis=0, keepdims=True)
            mean = mean / z.total
            for k in range(z.n_mem):
                rows = slice(k * z.members, (k + 1) * z.members)
                self.ahi[rows, cols], self.alo[rows, cols] = split((found[k] - mean) * (prec / scale))
            tanh = jnp.tanh(self.beside_seen[side, self.m_id])
            self.slope[:, cols] = 1.0 + 0.5 * (1.0 - tanh * tanh)
            self.innov[0:1, cols] = prec * (data - mean)

    def mark(self, e, row, sites):
        z = self.z
        cell = lax.broadcasted_iota(jnp.int32, (z.cols, z.sites), 0) + row * z.cols
        self.hot[e] = jnp.where(cell == sites, 1.0, 0.0).astype(BF16)

    def mark_sites(self):
        for r in range(self.z.rows):
            self.mark(2 + r, r, self.sites[...])

    def mark_sites_beside(self):
        r = self.z.rows
        low, high = (self.aux[e, 5:6, :].astype(jnp.int32) for e in (1, r + 2))
        for k in range(2):
            self.mark(k, r - 2 + k, low)
            self.mark(r + 2 + k, k, high)

    def spread(self, slot, rows):
        z = self.z
        hi, lo = split(self.picked[:, slot * z.sites : (slot + 1) * z.sites])
        for e in rows:
            field = self.mixed[e] + plain_t(hi, self.hot[e]) + plain_t(lo, self.hot[e])
            self.sbext[e] = self.aux[e, 4:5, :] * field


    def fold(self, block):
        size = self.z.members
        half = size // 2
        bottom = pltpu.roll(block[half:], half, 1)
        lane = lax.broadcasted_iota(jnp.int32, (half, size), 1)
        line = lax.broadcasted_iota(jnp.int32, (half, size), 0)
        return jnp.where(lane < line, bottom, block[:half])

    def unfold(self, folded, diagonal):
        size = self.z.members
        half = size // 2
        wide = jnp.concatenate([folded, pltpu.roll(folded, half, 1)], axis=0)
        lane = lax.broadcasted_iota(jnp.int32, (size, size), 1)
        line = lax.broadcasted_iota(jnp.int32, (size, size), 0)
        above, below = lane - line, lane - half
        straight = ((line < half) & (above >= 0)) | ((line >= half) & (below >= 0) & (above < 0))
        block = jnp.where(straight, wide, wide.T)
        return jnp.where((line >= half) & (above == 0), diagonal, block)

    def cross_rows(self, dev):
        z, s, m = self.z, self.s_id, self.m_id
        n, size = z.n_mem, z.members
        half = size // 2
        self.d_copies = []
        mean_bar = jnp.zeros((size, 1), F32)
        for k in list(range(n - 1, 0, -1)) + [0]:
            there = lax.rem(m + k, n)
            rows = self.block(there)
            part = mm3_t(dev[0], (self.chi[2, rows, :], self.clo[2, rows, :]))
            for i in range(1, z.rows):
                part = part + mm3_t(dev[i], (self.chi[2 + i, rows, :], self.clo[2 + i, rows, :]))
            mean_bar = mean_bar + jnp.sum(part, axis=1, keepdims=True)
            if 2 * k == n:
                part = jnp.where(self.hi == 0, part, part.T)
            self.dmat[k] = part
            copy = None
            if 2 * k > n:
                copy = remote(
                    self.dmat.at[k], self.dx.at[n - k], self.d_sem.at[0, k], self.d_sem.at[1, k], s, there
                )
            elif 2 * k == n:
                theirs = pl.ds(pl.multiple_of((1 - self.hi) * half, half), half)
                copy = remote(
                    self.dmat.at[k, theirs], self.dx.at[k, pl.ds(0, half)],
                    self.d_sem.at[0, k], self.d_sem.at[1, k], s, there,
                )
            if copy is not None:
                copy.start()
                self.d_copies.append(copy)
        self.waits += [(copy, None) for copy in self.d_copies]
        return mean_bar

    def pack_gram(self, scale):
        z, m = self.z, self.m_id
        n, size = z.n_mem, z.members
        half = size // 2
        mean = jnp.zeros((1, z.sites), F32)
        for k in range(n):
            mean = mean + jnp.sum(self.obsf[k], axis=0, keepdims=True)
        mean = mean / z.total
        prec = self.prec[...]
        for k in range(n):
            rows = slice(k * size, (k + 1) * size)
            self.ahi[rows, : z.sites], self.alo[rows, : z.sites] = split((self.obsf[k] - mean) * (prec / scale))
        anom = lambda rows: (self.ahi[rows, : z.sites], self.alo[rows, : z.sites])
        mine = anom(self.block(m))
        diag = mm3_t(mine, mine)
        parts = [self.fold(diag)]
        base = self.lo * size + self.hi * half
        upper = anom(pl.ds(pl.multiple_of(base, half), half))
        parts.append(mm3_t(upper, anom(self.block(self.lo + n // 2))))
        for k in range(1, n // 2):
            parts.append(mm3_t(mine, anom(self.block(lax.rem(m + k, n)))))
        self.gram_src[...] = jnp.concatenate(parts, axis=0).reshape(z.n_space, z.height, size)
        return mean, diag

    def pack_lines(self, scale, mean_bar, own_sums, mean, diag):
        z, m = self.z, self.m_id
        n, size = z.n_mem, z.members
        prec = self.prec[...]
        innov = prec * (self.data[...] - mean)
        self.innov[0:1, : z.sites] = innov
        exact = (self.obsf[m] - mean) * (prec / scale)
        lane = lax.broadcasted_iota(jnp.int32, (size, size), 1)
        diagonal = lambda x: jnp.sum(jnp.where(eye(size), x, 0.0), axis=1, keepdims=True)
        pull = jnp.sum(exact * innov, axis=1, keepdims=True)
        columns = [pull, mean_bar, diagonal(self.cross_diag), diagonal(diag)]
        stacked = jnp.zeros((size, size), F32)
        for k, column in enumerate(columns):
            stacked = jnp.where(lane == k, column, stacked)
        total = self.sums[0]
        for k in range(1, n):
            total = total + self.sums[k]
        term = None
        for r in range(z.rows):
            lacks = (own_sums[r] / size - total[r : r + 1] / z.total) / scale
            this = mm3_t(split(jnp.broadcast_to(lacks, (8, z.cols))), (self.chi[2 + r], self.clo[2 + r]))
            term = this if term is None else term + this
        lines = [stacked.T[:4]] + [term[:1, k * size : (k + 1) * size] for k in range(n)]
        if z.lines > 4 + n:
            lines.append(jnp.zeros((z.lines - 4 - n, size), F32))
        self.vec[...] = jnp.concatenate(lines, axis=0)

    def pack_cross(self):
        z = self.z
        n, size = z.n_mem, z.members
        half = size // 2
        for copy in self.d_copies:
            copy.wait_recv()
        cross = self.dmat[0]
        self.cross_diag = 0.5 * (cross + cross.T)
        parts = [self.fold(self.cross_diag)]
        ours = pl.ds(pl.multiple_of(self.hi * half, half), half)
        parts.append(0.5 * (self.dmat[n // 2, ours] + self.dx[n // 2, pl.ds(0, half)]))
        for k in range(1, n // 2):
            parts.append(0.5 * (self.dmat[k] + self.dx[k].T))
        self.cross_src[...] = jnp.concatenate(parts, axis=0).reshape(z.n_space, z.height, size)

    def send_lines(self):
        z, s, m = self.z, self.s_id, self.m_id
        self.tiny = []
        for k in range(1, z.n_space):
            to = lax.rem(s + k, z.n_space)
            self.tiny.append(
                remote(self.vec, self.vbuf.at[s], self.v_sem.at[0, k], self.v_sem.at[1, k], to, m)
            )
            self.tiny[-1].start()
        self.waits += [(copy, None) for copy in self.tiny]

    def sum_lines(self):
        self.vbuf[self.s_id] = self.vec[...]
        for copy in self.tiny:
            copy.wait_recv()
        vec = self.vbuf[0]
        for k in range(1, self.z.n_space):
            vec = vec + self.vbuf[k]
        self.vout[self.m_id] = vec
        return self.mem_send(self.vout, self.vg_sem)

    def blocks_of(self, reduction, line):
        z = self.z
        n, size = z.n_mem, z.members
        half = size // 2
        wholes = [reduction.whole(i) for i in range(n)]
        for i in range(n):
            yield i, i, self.unfold(wholes[i][:half], self.vout[i, line : line + 1, :])
        for i in range(n // 2):
            j = i + n // 2
            yield i, j, jnp.concatenate([wholes[i][half:size], wholes[j][half:size]], axis=0)
        for i in range(n):
            for k in range(1, n // 2):
                yield i, (i + k) % n, wholes[i][k * size : (k + 1) * size]


    def transform(self, scale, gram):
        z, m = self.z, self.m_id
        n, size, total = z.n_mem, z.members, z.total
        mine = self.block(m)
        col = lambda k: slice(k * size, (k + 1) * size)
        squares = jnp.zeros((size, size), F32)
        for i, j, block in self.blocks_of(gram, 3):
            if i == j:
                block = block + eye(size).astype(F32)
                squares = squares + block * block
            else:
                self.f[col(j), col(i)] = block.T
                squares = squares + 2.0 * (block * block)
            self.f[col(i), col(j)] = block
        norm = jnp.sqrt(whole_sum(squares))
        root = jnp.sqrt(norm)
        identity = eye(total).astype(F32)
        f = 1.5 * identity - (0.5 / norm) * self.f[...]
        self.f[...] = f
        self.fh[...], self.fl[...] = split(f)
        f_split = (self.fh[...], self.fl[...])
        f2 = mm3(f_split, f_split)
        self.f2h[...], self.f2l[...] = split(f2)
        g = f2 - 1.5 * self.f[...]
        self.g[...] = g
        self.gh[...], self.gl[...] = split(g)
        g_split = (self.gh[...], self.gl[...])
        yield
        p = 1.5 * self.f[...] + mm3((self.f2h[...], self.f2l[...]), g_split)
        self.s[...] = p
        p_split = split(p)
        kind = lax.broadcasted_iota(jnp.int32, (z.lines, size), 0)
        self.lines = []
        for i in range(n):
            lines = self.vout[i]
            lacks = jnp.sum(jnp.sum(lines[4 : 4 + n], axis=0, keepdims=True), axis=1, keepdims=True)
            self.lines.append(jnp.where(kind == 1, lines + lacks, jnp.where(kind == 3, 1.0, lines)))
        rows = jnp.concatenate(self.lines, axis=1)
        self.first = mm3(split(rows), p_split) / root
        second = mm3(split(self.first), p_split) / root
        self.vcol[...] = second.T
        self.pull_bar = second[1:2]
        self.pull_mine = self.vcol[mine, 1:2] - jnp.sum(self.pull_bar, axis=1, keepdims=True) / total
        mix = self.s[mine, :] / root + self.vcol[mine, 0:1] / scale
        row_weights = self.first[3:4] + jnp.sum(second[0:1], axis=1, keepdims=True) / scale
        mix = split(mix + (1.0 - row_weights) / total)
        for e in range(2, z.rows + 2):
            self.mixed[e] = mm3(mix, (self.chi[e], self.clo[e]))
        r = z.rows
        row = lambda e: self.mixed.at[e]
        bar_halo = (
            self.between(row(r + 1), row(1), row(2), row(r + 2), self.bar_halo),
            self.between(row(r), row(0), row(3), row(r + 3), self.far_halo),
        )
        self.fg[...] = mm3((self.fh[...], self.fl[...]), g_split)
        self.weigh[...] = 2.25 * identity + 4.5 * (self.fg[...] + self.f[...] - self.s[...])
        self.norm, self.root = norm, root
        for k, ref in enumerate((self.f, self.g, self.fg)):
            rows = slice(k * size, (k + 1) * size)
            self.lh[rows, :], self.ll[rows, :] = split(self.centred(ref))
        yield bar_halo

    def centred(self, ref):
        return ref[self.block(self.m_id), :] - jnp.sum(ref[...], axis=0, keepdims=True) / self.z.total

    def respond(self, scale, cross):
        z, m = self.z, self.m_id
        n, size, total = z.n_mem, z.members, z.total
        col = lambda k: slice(k * size, (k + 1) * size)
        norm, root = self.norm, self.root
        turned = [x.T for x in self.lines]
        first_t = self.first.T
        for i, j, block in self.blocks_of(cross, 2):
            block = (scale / root) * (
                block + 0.5 * (self.lines[i][4 + j : 5 + j] + turned[j][:, 4 + i : 5 + i])
            ) + (0.5 / root) * (
                turned[i][:, 1:2] * self.first[0:1, col(j)]
                + first_t[col(i), 0:1] * self.lines[j][1:2]
                + first_t[col(i), 1:2] * self.lines[j][0:1]
                + turned[i][:, 0:1] * self.first[1:2, col(j)]
            )
            self.s[col(i), col(j)] = block
            if i != j:
                self.s[col(j), col(i)] = block.T
        scale_bar = whole_sum(self.s[...] * self.weigh[...]) / norm
        self.sh[...], self.sl[...] = split(self.s[...])
        s_split = (self.sh[...], self.sl[...])
        s_mine = self.centred(self.s)
        f_split = (self.fh[...], self.fl[...])
        through = mm3((self.lh[...], self.ll[...]), s_split)
        bar = 1.5 * s_mine + through[2 * size :]
        bar = bar + mm3(split(mm3(split(s_mine), f_split)), (self.gh[...], self.gl[...]))
        bar = bar + mm3(split(through[:size]), (self.f2h[...], self.f2l[...]))
        bar = bar + mm3(split(through[size : 2 * size]), f_split)
        unit = (
            lax.broadcasted_iota(jnp.int32, (size, total), 0) + m * size
            == lax.broadcasted_iota(jnp.int32, (size, total), 1)
        ).astype(F32) - 1.0 / total
        sym = 2.0 * scale_bar * (3.0 * unit - 2.0 * self.centred(self.f)) - bar / norm
        sym = sym - (scale / total) * self.pull_bar
        prec = [self.prec[...], self.aux[1, 6:7, :], self.aux[z.rows + 2, 6:7, :]]
        observed = (jnp.concatenate(prec, axis=1) / scale) * (
            mm3(split(sym), (self.ahi[...], self.alo[...])) + self.pull_mine * self.innov[0:1, :]
        )
        return observed * self.slope[...]


    def pull_back(self, src, first, dst, rows, to_sea):
        z = self.z
        for i in rows:
            e = first + i
            c = [self.aux[e, k : k + 1, :] for k in range(4)]
            lane = lax.broadcasted_iota(jnp.int32, (1, z.cols), 1)
            keep = 1.0 - c[0] - c[1] - c[2] - c[3]
            from_south, from_north = self.aux[e + 1, 0:1, :], self.aux[e - 1, 1:2, :]
            sea = self.aux[e, 4:5, :]
            east = pltpu.roll(jnp.broadcast_to(jnp.where(lane == 0, 0.0, c[2]), (8, z.cols)), z.cols - 1, 1)[:1]
            west = pltpu.roll(jnp.broadcast_to(jnp.where(lane == z.cols - 1, 0.0, c[3]), (8, z.cols)), 1, 1)[:1]
            if to_sea:
                keep, from_south, from_north = sea * keep, sea * from_south, sea * from_north
                east, west = sea * east, sea * west
            for part in self.chunks():
                v = src[i + 1, part, :]
                dst[i, part, :] = (
                    keep * v
                    + from_south * src[i + 2, part, :]
                    + from_north * src[i, part, :]
                    + east * pltpu.roll(v, z.cols - 1, 1)
                    + west * pltpu.roll(v, 1, 1)
                )

    def coefficient_terms(self, weight, w0, field, f0, which):
        z = self.z
        lane = lax.broadcasted_iota(jnp.int32, (1, z.cols), 1)
        rows = {}
        for r in which:
            sums = [0.0] * 5
            for part in self.chunks():
                w = weight[w0 + r, part, :]
                c = field[f0 + r, part, :]
                terms = [
                    w * field[f0 + r - 1, part, :],
                    w * field[f0 + r + 1, part, :],
                    w * pltpu.roll(c, 1, 1),
                    w * pltpu.roll(c, z.cols - 1, 1),
                    w * c,
                ]
                sums = [x + y for x, y in zip(sums, terms)]
            north, south, west, east, own = [jnp.sum(x, axis=0, keepdims=True) for x in sums]
            west = jnp.where(lane == 0, 0.0, west)
            east = jnp.where(lane == z.cols - 1, 0.0, east)
            rows[r] = [north - own, south - own, west - own, east - own]
        return rows


def kernel(z, *refs):
    small = ["stencil", "sea", "sites", "data", "prec"]
    names = ["prior", "cot"] + [name + "_in" for name in small] + ["grad", "coef"]
    names += list(scratch_of(z))
    g = Step(z, dict(zip(names, refs)))
    scale = jnp.sqrt(jnp.float32(z.total - 1))
    s, m = g.s_id, g.m_id
    r, ext = z.rows, z.rows + 4
    mine = g.block(m)

    entered = g.barrier()
    loads = []
    for i in range(r):
        loads.append(pltpu.make_async_copy(g.prior.at[:, i], g.pext.at[2 + i], g.own.at[0, i]))
    for i in range(r):
        loads.append(pltpu.make_async_copy(g.cot.at[:, i], g.cotf.at[2 + i, mine], g.own.at[1, i]))
    few = [
        pltpu.make_async_copy(getattr(g, name + "_in"), getattr(g, name), g.few.at[i])
        for i, name in enumerate(small)
    ]
    for copy in loads[:r] + few + loads[r:]:
        copy.start()
    for copy in few:
        copy.wait()
    for i in range(r):
        g.aux[2 + i, 0:4, :] = g.stencil[:, i, :]
        g.aux[2 + i, 4:5, :] = g.sea[i : i + 1, :].astype(F32)
        g.aux[2 + i, 5:6, :] = g.sites[...].astype(F32)
        g.aux[2 + i, 6:7, :] = g.prec[...]
        g.aux[2 + i, 7:8, :] = g.data[...]
    for e, edge in ((0, 0), (1, 0), (ext - 2, z.n_space - 1), (ext - 1, z.n_space - 1)):
        @pl.when(s == edge)
        def _():
            g.pext[e] = jnp.zeros((z.members, z.cols), F32)
            g.mixed[e] = jnp.zeros((z.members, z.cols), F32)
            g.aux[e] = jnp.zeros((8, z.cols), F32)
            g.beside_seen[0 if e < 2 else 1, m] = jnp.zeros((z.members, z.sites), F32)
    for copy in loads[:r]:
        copy.wait()
    entered()
    halo = g.halo_send(g.pext, g.halo)
    if z.rounds:
        g.vouch(1)
    for copy in loads[r:]:
        copy.wait()
    cot_forward, cot_wait = g.pair_gather(lambda which: g.cotf.at[pl.ds(2, r), g.block(which)], g.cot_sem)
    aux_halo = g.halo_send(g.aux, g.aux_halo)
    g.mark_sites()
    aux_halo()
    g.mark_sites_beside()
    cot_forward()
    for k in range(1, z.rounds):
        g.hear(k)
        g.vouch(k + 1)
    halo()

    g.advance(g.pext, 1, g.fext, r + 2)
    g.advance(g.fext, 2, g.state, r)
    g.obsf[m] = g.observe()
    obs_wait = g.mem_send(g.obsf, g.obs_sem)
    own_sums = [jnp.sum(g.state[i], axis=0, keepdims=True) for i in range(r)]
    padding = [jnp.zeros((-r % 8, z.cols), F32)] * (r % 8 > 0)
    g.sums[m] = jnp.concatenate(own_sums + padding, axis=0)
    sums_wait = g.mem_send(g.sums, g.sum_sem)
    seen_halo = g.between(
        g.seen, g.beside_seen.at[0, m], g.seen, g.beside_seen.at[1, m], g.seen_halo
    )
    cot_wait()
    for e in range(2, r + 2):
        g.chi[e], g.clo[e] = split(g.cotf[e])
    dev = [split((g.state[i] - own_sums[i] / z.members) / scale) for i in range(r)]
    mean_bar = g.cross_rows(dev)
    obs_wait()
    mean, diag = g.pack_gram(scale)
    if z.rounds:
        g.hear(z.rounds)
    gram, cross = Reduction(g, "gram"), Reduction(g, "cross")
    gram.scatter()
    g.pack_cross()
    cross.scatter()
    sums_wait()
    g.pack_lines(scale, mean_bar, own_sums, mean, diag)
    g.send_lines()
    seen_halo()
    extras = [
        g.pair_gather(lambda which: g.beside_seen.at[:, which], g.seen_sem),
    ]
    gram.start()
    cross.start()
    lines_wait = g.sum_lines()
    for forward, _ in extras:
        forward()
    gram.forward_all()
    cross.forward_all()
    for _, wait in extras:
        wait()
    g.observe_beside()
    gram.pass_on()
    lines_wait()
    gram.finish()
    parts = g.transform(scale, gram)
    next(parts)
    cross.pass_on()
    bar_halo = next(parts)
    cross.finish()
    g.picked[...] = g.respond(scale, cross)
    g.spread(0, range(2, r + 2))
    second = g.coefficient_terms(g.sbext, 2, g.fext, 1, range(r))
    g.pull_back(g.sbext, 1, g.fbar, range(2, r), True)
    firsts = g.coefficient_terms(g.fbar, 1, g.pext, 2, range(1, r - 1))
    bar_halo[0]()
    g.spread(1, (1,))
    g.spread(2, (r + 2,))
    outer = (0, r - 1) if r > 1 else (0,)
    g.pull_back(g.sbext, 1, g.fbar, [i + 1 for i in outer], True)
    firsts.update(g.coefficient_terms(g.fbar, 1, g.pext, 2, outer))
    g.cbuf[m] = jnp.concatenate(
        [second[i][k] + firsts[i][k] for k in range(4) for i in range(r)], axis=0
    )
    c_wait = g.mem_send(g.cbuf, g.c_sem)
    bar_halo[1]()
    g.spread(1, (0,))
    g.spread(2, (r + 3,))
    g.pull_back(g.sbext, 1, g.fbar, (0, r + 1), True)
    g.pull_back(g.fbar, 2, g.grad, range(r), False)
    c_wait()
    both = g.cbuf[0]
    for k in range(1, z.n_mem):
        both = both + g.cbuf[k]
    for k in range(4):
        g.coef[k] = both[k * r : (k + 1) * r]
    g.finish_sends()


def place(z, last, sums, grad, coef, scaled, sem):
    stores = [pltpu.make_async_copy(last.at[i], grad.at[:, i], sem.at[i]) for i in range(z.rows)]
    for copy in stores:
        copy.start()
    scaled[...] = sums[...] / jnp.sqrt(jnp.float32(z.total))
    stores.append(pltpu.make_async_copy(scaled, coef, sem.at[z.rows]))
    stores[-1].start()
    for copy in stores:
        copy.wait()


def local(n_space, n_mem, prior, stencil, sea_mask, sites, data, precision, cotangent):
    z = Sizes(n_space, n_mem, prior, sites)
    any_spec = pl.BlockSpec(memory_space=pl.ANY)
    turned = (z.rows, z.members, z.cols)
    factors = (4, z.rows, z.cols)
    inputs = (prior, cotangent, stencil, sea_mask, sites, data[None], precision[None])
    last, sums = pl.pallas_call(
        functools.partial(kernel, z),
        out_shape=(jax.ShapeDtypeStruct(turned, F32), jax.ShapeDtypeStruct(factors, F32)),
        in_specs=[pl.BlockSpec(memory_space=pltpu.HBM)] * 7,
        out_specs=(VMEM_SPEC, VMEM_SPEC),
        scratch_shapes=list(scratch_of(z).values()),
        compiler_params=pltpu.CompilerParams(
            collective_id=1, has_side_effects=True, vmem_limit_bytes=GRANT
        ),
        name="adjoint",
    )(*[pltpu.with_memory_space_constraint(x, pltpu.HBM) for x in inputs])
    return pl.pallas_call(
        functools.partial(place, z),
        out_shape=(jax.ShapeDtypeStruct(prior.shape, F32), jax.ShapeDtypeStruct(factors, F32)),
        in_specs=[VMEM_SPEC, VMEM_SPEC],
        out_specs=(any_spec, any_spec),
        scratch_shapes=[pltpu.VMEM(factors, F32), pltpu.SemaphoreType.DMA((z.rows + 1,))],
        compiler_params=pltpu.CompilerParams(vmem_limit_bytes=4 * 1024 * 1024),
        name="place",
    )(last, sums)


def solution(mesh):
    placed = (
        P("mem", "space", None),
        P(None, "space", None),
        P("space", None),
        P("space", None),
        P("space"),
        P("space"),
        P("mem", "space", None),
    )
    return jax.shard_map(
        functools.partial(local, mesh.shape["space"], mesh.shape["mem"]),
        mesh=mesh,
        in_specs=placed,
        out_specs=(P("mem", "space", None), P(None, "space", None)),
        check_vma=False,
    )
```

```python
import functools
import jax
import jax.numpy as jnp
from jax import lax
from jax.experimental import pallas as pl
from jax.experimental.pallas import tpu as pltpu
from jax.sharding import PartitionSpec as P

MESH = pl.DeviceIdType.MESH
F32 = jnp.float32
GRANT = 48 * 1024 * 1024
BF16 = jnp.bfloat16
VMEM_SPEC = pl.BlockSpec(memory_space=pltpu.VMEM)


def remote(src, dst, send, recv, s, m):
    return pltpu.make_async_remote_copy(
        src_ref=src, dst_ref=dst, send_sem=send, recv_sem=recv, device_id=(s, m), device_id_type=MESH
    )


def split(x):
    lead = x.astype(BF16)
    return lead, (x - lead.astype(F32)).astype(BF16)


def split3(x):
    lead = x.astype(BF16)
    rest = x - lead.astype(F32)
    middle = rest.astype(BF16)
    return lead, middle, (rest - middle.astype(F32)).astype(BF16)


def plain(a, b):
    return jnp.dot(a, b, preferred_element_type=F32)


def plain_t(a, b):
    return lax.dot_general(a, b, (((1,), (1,)), ((), ())), preferred_element_type=F32)


def mm3(a, b):
    left = jnp.concatenate([a[0], a[0], a[1]], axis=1)
    return plain(left, jnp.concatenate([b[0], b[1], b[0]], axis=0))


def mm3_t(a, b):
    left = jnp.concatenate([a[0], a[0], a[1]], axis=1)
    return plain_t(left, jnp.concatenate([b[0], b[1], b[0]], axis=1))


def whole_sum(x):
    return jnp.sum(jnp.sum(x, axis=0, keepdims=True), axis=1, keepdims=True)


def eye(size):
    return lax.broadcasted_iota(jnp.int32, (size, size), 0) == lax.broadcasted_iota(
        jnp.int32, (size, size), 1
    )


class Sizes:
    def __init__(self, n_space, n_mem, prior, sites):
        self.n_space, self.n_mem = n_space, n_mem
        self.members, self.rows, self.cols = prior.shape
        self.total = self.members * n_mem
        self.sites = sites.shape[-1]
        self.near = 2 if n_space % 2 == 0 else 1
        self.far = n_space // self.near
        self.half = 2 if n_mem % 2 == 0 else 1
        self.wide = n_mem // self.half
        self.group = max(1, self.far // 4)
        self.groups = self.far // self.group
        self.height = n_mem // 2 * self.members // n_space
        self.lines = 8 * pl.cdiv(4 + n_mem, 8)
        self.rounds = max(0, (n_space - 1).bit_length() - 1)


def scratch_of(z):
    dma = pltpu.SemaphoreType.DMA
    ext = z.rows + 4
    v = lambda *shape: pltpu.VMEM(shape, F32)
    b = lambda *shape: pltpu.VMEM(shape, BF16)
    square = (z.total, z.total)
    half_square = (z.n_space, z.height, z.members)
    gathered = (z.n_mem, z.far, z.near, z.height, z.members)
    found = dict(
        stencil=v(4, z.rows, z.cols),
        sea=pltpu.VMEM((z.rows, z.cols), jnp.int32),
        sites=pltpu.VMEM((1, z.sites), jnp.int32),
        data=v(1, z.sites),
        prec=v(1, z.sites),
        few=dma((5,)),
        token=pltpu.SemaphoreType.REGULAR((max(1, z.rounds), 2)),
        pext=v(ext, z.members, z.cols),
        aux=v(ext, 8, z.cols),
        cotf=v(ext, z.total, z.cols),
        chi=b(ext, z.total, z.cols),
        clo=b(ext, z.total, z.cols),
        seen=v(z.members, z.sites),
        beside_seen=v(2, z.n_mem, z.members, z.sites),
        slope=v(z.members, 3 * z.sites),
        fext=v(z.rows + 2, z.members, z.cols),
        state=v(z.rows, z.members, z.cols),
        hot=b(ext, z.cols, z.sites),
        obsf=v(z.n_mem, z.members, z.sites),
        ahi=b(z.total, 3 * z.sites),
        alo=b(z.total, 3 * z.sites),
        innov=v(8, 3 * z.sites),
        sums=v(z.n_mem, 8 * pl.cdiv(z.rows, 8), z.cols),
        dmat=v(z.n_mem, z.members, z.members),
        dx=v(z.n_mem, z.members, z.members),
        vec=v(z.lines, z.members),
        vbuf=v(z.n_space, z.lines, z.members),
        vout=v(z.n_mem, z.lines, z.members),
        f=v(*square),
        g=v(*square),
        fg=v(*square),
        s=v(*square),
        weigh=v(*square),
        fh=b(*square), fl=b(*square),
        f2h=b(*square), f2l=b(*square),
        gh=b(*square), gl=b(*square),
        sh=b(*square), sl=b(*square),
        lh=b(3 * z.members, z.total), ll=b(3 * z.members, z.total),
        vcol=v(z.total, z.lines),
        sbext=v(ext, z.members, z.cols),
        mixed=v(ext, z.members, z.cols),
        picked=v(z.members, 3 * z.sites),
        fbar=v(z.rows + 2, z.members, z.cols),
        cbuf=v(z.n_mem, 4 * z.rows, z.cols),
        own=dma((2, z.rows)),
        halo=dma((2, 2)),
        aux_halo=dma((2, 2)),
        bar_halo=dma((2, 2)),
        far_halo=dma((2, 2)),
        seen_halo=dma((2, 2)),
        cot_sem=dma((2, z.half, z.wide)),
        seen_sem=dma((2, z.half, z.wide)),
        obs_sem=dma((2, z.n_mem)),
        sum_sem=dma((2, z.n_mem)),
        d_sem=dma((2, z.n_mem)),
        v_sem=dma((2, z.n_space)),
        vg_sem=dma((2, z.n_mem)),
        c_sem=dma((2, z.n_mem)),
    )
    for tag in ("gram", "cross"):
        found[tag + "_src"] = v(*half_square)
        found[tag + "_buf"] = v(*half_square)
        found[tag + "_out"] = v(*gathered)
        found[tag + "_rs"] = dma((2, z.n_space))
        found[tag + "_a"] = dma((2, z.far))
        found[tag + "_x"] = dma((2, z.near, z.wide, z.groups))
        found[tag + "_q"] = dma((2, z.half, z.near, z.wide, z.groups))
    return found


class Reduction:
    def __init__(self, g, tag):
        self.g, self.z = g, g.z
        for name in ("src", "buf", "out", "rs", "a", "x", "q"):
            setattr(self, name, getattr(g, tag + "_" + name))
        z = g.z
        self.a_id, self.b_id = g.s_id // z.near, lax.rem(g.s_id, z.near)
        self.p_id, self.q_id = g.m_id // z.half, lax.rem(g.m_id, z.half)

    def scatter(self):
        z, s, m = self.z, self.g.s_id, self.g.m_id
        self.copies = []
        for k in range(1, z.n_space):
            to = lax.rem(s + k, z.n_space)
            self.copies.append(
                remote(self.src.at[to], self.buf.at[s], self.rs.at[0, k], self.rs.at[1, k], to, m)
            )
            self.copies[-1].start()
        self.g.waits += [(copy, None) for copy in self.copies]

    def start(self):
        z, s, m = self.z, self.g.s_id, self.g.m_id
        a, b = self.a_id, self.b_id
        self.buf[s] = self.src[s]
        for copy in self.copies:
            copy.wait_recv()
        total = self.buf[0]
        for k in range(1, z.n_space):
            total = total + self.buf[k]
        self.out[m, a, b] = total
        piece = self.out.at[m, a, b]
        stage = []
        for k in range(1, z.far):
            to = lax.rem(a + k, z.far) * z.near + b
            stage.append(remote(piece, piece, self.a.at[0, k], self.a.at[1, k], to, m))
            stage[-1].start()
        self.g.waits += [(copy, None) for copy in stage]
        if z.group == 1:
            self.steps = [([], a)] + [
                ([stage[k - 1]], lax.rem(a + z.far - k, z.far)) for k in range(1, z.far)
            ]
            self.forward(0)
        else:
            self.steps = [(stage if n == 0 else [], n * z.group) for n in range(z.groups)]

    def forward(self, index):
        z, s, m = self.z, self.g.s_id, self.g.m_id
        needs, start = self.steps[index]
        for copy in needs:
            copy.wait_recv()
        piece = self.out.at[m, pl.ds(start, z.group), self.b_id]
        for kb, kp in self.offsets():
            to_s = self.a_id * z.near + lax.rem(self.b_id + kb, z.near)
            to_m = lax.rem(self.p_id + kp, z.wide) * z.half + self.q_id
            self.send(piece, self.x.at[0, kb, kp, index], self.x.at[1, kb, kp, index], to_s, to_m)
        self.beside(piece, 0, 0, index)

    def forward_all(self):
        for index in range(1 if self.z.group == 1 else 0, self.z.groups):
            self.forward(index)

    def offsets(self):
        z = self.z
        return [(kb, kp) for kb in range(z.near) for kp in range(z.wide) if kb or kp]

    def send(self, piece, *where):
        copy = remote(piece, piece, *where)
        copy.start()
        self.g.waits.append((copy, None))

    def beside(self, piece, kb, kp, index):
        z = self.z
        for kq in range(1, z.half):
            to = self.p_id * z.half + lax.rem(self.q_id + kq, z.half)
            self.send(
                piece, self.q.at[0, kq, kb, kp, index], self.q.at[1, kq, kb, kp, index], self.g.s_id, to
            )

    def piece_of(self, kb, kp, kq, index):
        z = self.z
        which_b = lax.rem(self.b_id + z.near - kb, z.near)
        which_p = lax.rem(self.p_id + z.wide - kp, z.wide)
        which_q = lax.rem(self.q_id + z.half - kq, z.half)
        return self.out.at[which_p * z.half + which_q, pl.ds(self.steps[index][1], z.group), which_b]

    def pass_on(self):
        for index in range(self.z.groups):
            for kb, kp in self.offsets():
                piece = self.piece_of(kb, kp, 0, index)
                self.arrived(piece, self.x.at[0, kb, kp, index], self.x.at[1, kb, kp, index])
                self.beside(piece, kb, kp, index)

    def arrived(self, piece, send, recv):
        remote(piece, piece, send, recv, self.g.s_id, self.g.m_id).wait_recv()

    def finish(self):
        z = self.z
        for index in range(z.groups):
            for kb in range(z.near):
                for kp in range(z.wide):
                    for kq in range(1, z.half):
                        self.arrived(
                            self.piece_of(kb, kp, kq, index),
                            self.q.at[0, kq, kb, kp, index], self.q.at[1, kq, kb, kp, index],
                        )

    def whole(self, i):
        z = self.z
        return self.out[i].reshape(z.n_mem // 2 * z.members, z.members)


class Step:
    def __init__(self, z, refs):
        self.z = z
        self.__dict__.update(refs)
        self.s_id, self.m_id = lax.axis_index("space"), lax.axis_index("mem")
        self.lo = lax.rem(self.m_id, z.n_mem // 2)
        self.hi = self.m_id // (z.n_mem // 2)
        self.waits = []

    def finish_sends(self):
        for copy, when in self.waits:
            if when is None:
                copy.wait_send()
            else:
                pl.when(when)(copy.wait_send)

    def barrier(self):
        z, s, m = self.z, self.s_id, self.m_id
        peers = [(s, lax.rem(m + k, z.n_mem)) for k in range(1, z.n_mem)]
        a, b = s // z.near, lax.rem(s, z.near)
        p, q = m // z.half, lax.rem(m, z.half)
        for kb in range(1, z.near):
            for kp in range(1, z.wide):
                peers.append((
                    a * z.near + lax.rem(b + kb, z.near), lax.rem(p + kp, z.wide) * z.half + q
                ))
        barrier = pltpu.get_barrier_semaphore()
        count = len(peers)
        for peer in peers:
            pl.semaphore_signal(barrier, inc=1, device_id=peer, device_id_type=MESH)
        for step in (1, -1, 2, -2):
            there = self.exists(step)
            count = count + there.astype(jnp.int32)

            @pl.when(there)
            def _():
                pl.semaphore_signal(barrier, inc=1, device_id=(s + step, m), device_id_type=MESH)

        return lambda: pl.semaphore_wait(barrier, count)

    def exists(self, step):
        to = self.s_id + step
        return (to >= 0) & (to < self.z.n_space)

    def vouch(self, round_):
        for side, step in ((0, 2**round_), (1, -(2**round_))):
            @pl.when(self.exists(step))
            def _():
                pl.semaphore_signal(
                    self.token.at[round_ - 1, side], inc=1,
                    device_id=(self.s_id + step, self.m_id), device_id_type=MESH,
                )

    def hear(self, round_):
        for side, step in ((0, -(2**round_)), (1, 2**round_)):
            @pl.when(self.exists(step))
            def _():
                pl.semaphore_wait(self.token.at[round_ - 1, side], 1)

    def between(self, up_src, up_dst, down_src, down_dst, sem):
        z, s, m = self.z, self.s_id, self.m_id
        has_low, has_high = s > 0, s < z.n_space - 1
        up = remote(up_src, up_dst, sem.at[0, 0], sem.at[1, 0], s + 1, m)
        down = remote(down_src, down_dst, sem.at[0, 1], sem.at[1, 1], s - 1, m)
        pl.when(has_high)(up.start)
        pl.when(has_low)(down.start)
        self.waits += [(up, has_high), (down, has_low)]

        def wait():
            pl.when(has_low)(up.wait_recv)
            pl.when(has_high)(down.wait_recv)

        return wait

    def halo_send(self, ref, sem):
        r = self.z.rows
        at = lambda row: ref.at[pl.ds(row, 2)]
        return self.between(at(r), at(0), at(2), at(r + 2), sem)

    def pair_gather(self, part, sem):
        z, s, m = self.z, self.s_id, self.m_id
        p, q = m // z.half, lax.rem(m, z.half)
        across = [lax.rem(p + k, z.wide) * z.half + q for k in range(1, z.wide)]
        beside = [p * z.half + lax.rem(q + k, z.half) for k in range(1, z.half)]
        mine = part(m)
        hops, sides = [], []
        for k, to in enumerate(across):
            hops.append(remote(mine, mine, sem.at[0, 0, k + 1], sem.at[1, 0, k + 1], s, to))
            hops[-1].start()
        for k, to in enumerate(beside):
            sides.append(remote(mine, mine, sem.at[0, k + 1, 0], sem.at[1, k + 1, 0], s, to))
            sides[-1].start()

        def forward():
            for kp, hop in enumerate(hops):
                hop.wait_recv()
                piece = part(lax.rem(p + z.wide - kp - 1, z.wide) * z.half + q)
                for k, to in enumerate(beside):
                    copy = remote(
                        piece, piece, sem.at[0, k + 1, kp + 1], sem.at[1, k + 1, kp + 1], s, to
                    )
                    copy.start()
                    sides.append(copy)

        def wait():
            for copy in sides:
                copy.wait_recv()
            self.waits.extend((copy, None) for copy in hops + sides)

        return forward, wait

    def mem_send(self, ref, sem):
        z, s, m = self.z, self.s_id, self.m_id
        copies = []
        for k in range(1, z.n_mem):
            to = lax.rem(m + k, z.n_mem)
            copies.append(remote(ref.at[m], ref.at[m], sem.at[0, k], sem.at[1, k], s, to))
            copies[-1].start()

        def wait():
            for copy in copies:
                copy.wait_recv()
            self.waits.extend((copy, None) for copy in copies)

        return wait

    def block(self, which):
        size = self.z.members
        return pl.ds(pl.multiple_of(which * size, size), size)


    def coefficients(self, e):
        z = self.z
        c = [self.aux[e, k : k + 1, :] for k in range(4)]
        sea = self.aux[e, 4:5, :]
        lane = lax.broadcasted_iota(jnp.int32, (1, z.cols), 1)
        keep = sea * (1.0 - c[0] - c[1] - c[2] - c[3])
        west = jnp.where(lane == 0, 0.0, c[2])
        east = jnp.where(lane == z.cols - 1, 0.0, c[3])
        return keep, sea * c[0], sea * c[1], sea * west, sea * east

    def chunks(self):
        size = min(32, self.z.members)
        return [pl.ds(k, size) for k in range(0, self.z.members, size)]

    def advance(self, src, first, dst, count):
        z = self.z
        for i in range(count):
            keep, north, south, west, east = self.coefficients(first + i)
            for part in self.chunks():
                v = src[i + 1, part, :]
                dst[i, part, :] = (
                    keep * v
                    + north * src[i, part, :]
                    + south * src[i + 2, part, :]
                    + west * pltpu.roll(v, 1, 1)
                    + east * pltpu.roll(v, z.cols - 1, 1)
                )

    def observe(self):
        z = self.z
        picked = jnp.zeros((z.members, z.sites), F32)
        for r in range(z.rows):
            for piece in split3(self.state[r]):
                picked = picked + plain(piece, self.hot[2 + r])
        self.seen[...] = picked
        tanh = jnp.tanh(picked)
        self.slope[:, : z.sites] = 1.0 + 0.5 * (1.0 - tanh * tanh)
        return picked + 0.5 * tanh

    def observe_beside(self):
        z = self.z
        scale = jnp.sqrt(jnp.float32(z.total - 1))
        for side, e in ((0, 1), (1, z.rows + 2)):
            cols = slice((1 + side) * z.sites, (2 + side) * z.sites)
            prec, data = self.aux[e, 6:7, :], self.aux[e, 7:8, :]
            found, mean = [], jnp.zeros((1, z.sites), F32)
            for k in range(z.n_mem):
                picked = self.beside_seen[side, k]
                found.append(picked + 0.5 * jnp.tanh(picked))
                mean = mean + jnp.sum(found[-1], axis=0, keepdims=True)
            mean = mean / z.total
            for k in range(z.n_mem):
                rows = slice(k * z.members, (k + 1) * z.members)
                self.ahi[rows, cols], self.alo[rows, cols] = split((found[k] - mean) * (prec / scale))
            tanh = jnp.tanh(self.beside_seen[side, self.m_id])
            self.slope[:, cols] = 1.0 + 0.5 * (1.0 - tanh * tanh)
            self.innov[0:1, cols] = prec * (data - mean)

    def mark(self, e, row, sites):
        z = self.z
        cell = lax.broadcasted_iota(jnp.int32, (z.cols, z.sites), 0) + row * z.cols
        self.hot[e] = jnp.where(cell == sites, 1.0, 0.0).astype(BF16)

    def mark_sites(self):
        for r in range(self.z.rows):
            self.mark(2 + r, r, self.sites[...])

    def mark_sites_beside(self):
        r = self.z.rows
        low, high = (self.aux[e, 5:6, :].astype(jnp.int32) for e in (1, r + 2))
        for k in range(2):
            self.mark(k, r - 2 + k, low)
            self.mark(r + 2 + k, k, high)

    def spread(self, slot, rows):
        z = self.z
        hi, lo = split(self.picked[:, slot * z.sites : (slot + 1) * z.sites])
        for e in rows:
            field = self.mixed[e] + plain_t(hi, self.hot[e]) + plain_t(lo, self.hot[e])
            self.sbext[e] = self.aux[e, 4:5, :] * field


    def fold(self, block):
        size = self.z.members
        half = size // 2
        bottom = pltpu.roll(block[half:], half, 1)
        lane = lax.broadcasted_iota(jnp.int32, (half, size), 1)
        line = lax.broadcasted_iota(jnp.int32, (half, size), 0)
        return jnp.where(lane < line, bottom, block[:half])

    def unfold(self, folded, diagonal):
        size = self.z.members
        half = size // 2
        wide = jnp.concatenate([folded, pltpu.roll(folded, half, 1)], axis=0)
        lane = lax.broadcasted_iota(jnp.int32, (size, size), 1)
        line = lax.broadcasted_iota(jnp.int32, (size, size), 0)
        above, below = lane - line, lane - half
        straight = ((line < half) & (above >= 0)) | ((line >= half) & (below >= 0) & (above < 0))
        block = jnp.where(straight, wide, wide.T)
        return jnp.where((line >= half) & (above == 0), diagonal, block)

    def cross_rows(self, dev):
        z, s, m = self.z, self.s_id, self.m_id
        n, size = z.n_mem, z.members
        half = size // 2
        self.d_copies = []
        mean_bar = jnp.zeros((size, 1), F32)
        for k in list(range(n - 1, 0, -1)) + [0]:
            there = lax.rem(m + k, n)
            rows = self.block(there)
            part = mm3_t(dev[0], (self.chi[2, rows, :], self.clo[2, rows, :]))
            for i in range(1, z.rows):
                part = part + mm3_t(dev[i], (self.chi[2 + i, rows, :], self.clo[2 + i, rows, :]))
            mean_bar = mean_bar + jnp.sum(part, axis=1, keepdims=True)
            if 2 * k == n:
                part = jnp.where(self.hi == 0, part, part.T)
            self.dmat[k] = part
            copy = None
            if 2 * k > n:
                copy = remote(
                    self.dmat.at[k], self.dx.at[n - k], self.d_sem.at[0, k], self.d_sem.at[1, k], s, there
                )
            elif 2 * k == n:
                theirs = pl.ds(pl.multiple_of((1 - self.hi) * half, half), half)
                copy = remote(
                    self.dmat.at[k, theirs], self.dx.at[k, pl.ds(0, half)],
                    self.d_sem.at[0, k], self.d_sem.at[1, k], s, there,
                )
            if copy is not None:
                copy.start()
                self.d_copies.append(copy)
        self.waits += [(copy, None) for copy in self.d_copies]
        return mean_bar

    def pack_gram(self, scale):
        z, m = self.z, self.m_id
        n, size = z.n_mem, z.members
        half = size // 2
        mean = jnp.zeros((1, z.sites), F32)
        for k in range(n):
            mean = mean + jnp.sum(self.obsf[k], axis=0, keepdims=True)
        mean = mean / z.total
        prec = self.prec[...]
        for k in range(n):
            rows = slice(k * size, (k + 1) * size)
            self.ahi[rows, : z.sites], self.alo[rows, : z.sites] = split((self.obsf[k] - mean) * (prec / scale))
        anom = lambda rows: (self.ahi[rows, : z.sites], self.alo[rows, : z.sites])
        mine = anom(self.block(m))
        diag = mm3_t(mine, mine)
        parts = [self.fold(diag)]
        base = self.lo * size + self.hi * half
        upper = anom(pl.ds(pl.multiple_of(base, half), half))
        parts.append(mm3_t(upper, anom(self.block(self.lo + n // 2))))
        for k in range(1, n // 2):
            parts.append(mm3_t(mine, anom(self.block(lax.rem(m + k, n)))))
        self.gram_src[...] = jnp.concatenate(parts, axis=0).reshape(z.n_space, z.height, size)
        return mean, diag

    def pack_lines(self, scale, mean_bar, own_sums, mean, diag):
        z, m = self.z, self.m_id
        n, size = z.n_mem, z.members
        prec = self.prec[...]
        innov = prec * (self.data[...] - mean)
        self.innov[0:1, : z.sites] = innov
        exact = (self.obsf[m] - mean) * (prec / scale)
        lane = lax.broadcasted_iota(jnp.int32, (size, size), 1)
        diagonal = lambda x: jnp.sum(jnp.where(eye(size), x, 0.0), axis=1, keepdims=True)
        pull = jnp.sum(exact * innov, axis=1, keepdims=True)
        columns = [pull, mean_bar, diagonal(self.cross_diag), diagonal(diag)]
        stacked = jnp.zeros((size, size), F32)
        for k, column in enumerate(columns):
            stacked = jnp.where(lane == k, column, stacked)
        total = self.sums[0]
        for k in range(1, n):
            total = total + self.sums[k]
        term = None
        for r in range(z.rows):
            lacks = (own_sums[r] / size - total[r : r + 1] / z.total) / scale
            this = mm3_t(split(jnp.broadcast_to(lacks, (8, z.cols))), (self.chi[2 + r], self.clo[2 + r]))
            term = this if term is None else term + this
        lines = [stacked.T[:4]] + [term[:1, k * size : (k + 1) * size] for k in range(n)]
        if z.lines > 4 + n:
            lines.append(jnp.zeros((z.lines - 4 - n, size), F32))
        self.vec[...] = jnp.concatenate(lines, axis=0)

    def pack_cross(self):
        z = self.z
        n, size = z.n_mem, z.members
        half = size // 2
        for copy in self.d_copies:
            copy.wait_recv()
        cross = self.dmat[0]
        self.cross_diag = 0.5 * (cross + cross.T)
        parts = [self.fold(self.cross_diag)]
        ours = pl.ds(pl.multiple_of(self.hi * half, half), half)
        parts.append(0.5 * (self.dmat[n // 2, ours] + self.dx[n // 2, pl.ds(0, half)]))
        for k in range(1, n // 2):
            parts.append(0.5 * (self.dmat[k] + self.dx[k].T))
        self.cross_src[...] = jnp.concatenate(parts, axis=0).reshape(z.n_space, z.height, size)

    def send_lines(self):
        z, s, m = self.z, self.s_id, self.m_id
        self.tiny = []
        for k in range(1, z.n_space):
            to = lax.rem(s + k, z.n_space)
            self.tiny.append(
                remote(self.vec, self.vbuf.at[s], self.v_sem.at[0, k], self.v_sem.at[1, k], to, m)
            )
            self.tiny[-1].start()
        self.waits += [(copy, None) for copy in self.tiny]

    def sum_lines(self):
        self.vbuf[self.s_id] = self.vec[...]
        for copy in self.tiny:
            copy.wait_recv()
        vec = self.vbuf[0]
        for k in range(1, self.z.n_space):
            vec = vec + self.vbuf[k]
        self.vout[self.m_id] = vec
        return self.mem_send(self.vout, self.vg_sem)

    def blocks_of(self, reduction, line):
        z = self.z
        n, size = z.n_mem, z.members
        half = size // 2
        wholes = [reduction.whole(i) for i in range(n)]
        for i in range(n):
            yield i, i, self.unfold(wholes[i][:half], self.vout[i, line : line + 1, :])
        for i in range(n // 2):
            j = i + n // 2
            yield i, j, jnp.concatenate([wholes[i][half:size], wholes[j][half:size]], axis=0)
        for i in range(n):
            for k in range(1, n // 2):
                yield i, (i + k) % n, wholes[i][k * size : (k + 1) * size]


    def transform(self, scale, gram):
        z, m = self.z, self.m_id
        n, size, total = z.n_mem, z.members, z.total
        mine = self.block(m)
        col = lambda k: slice(k * size, (k + 1) * size)
        squares = jnp.zeros((size, size), F32)
        for i, j, block in self.blocks_of(gram, 3):
            if i == j:
                block = block + eye(size).astype(F32)
                squares = squares + block * block
            else:
                self.f[col(j), col(i)] = block.T
                squares = squares + 2.0 * (block * block)
            self.f[col(i), col(j)] = block
        norm = jnp.sqrt(whole_sum(squares))
        root = jnp.sqrt(norm)
        identity = eye(total).astype(F32)
        f = 1.5 * identity - (0.5 / norm) * self.f[...]
        self.f[...] = f
        self.fh[...], self.fl[...] = split(f)
        f_split = (self.fh[...], self.fl[...])
        f2 = mm3(f_split, f_split)
        self.f2h[...], self.f2l[...] = split(f2)
        g = f2 - 1.5 * self.f[...]
        self.g[...] = g
        self.gh[...], self.gl[...] = split(g)
        g_split = (self.gh[...], self.gl[...])
        yield
        p = 1.5 * self.f[...] + mm3((self.f2h[...], self.f2l[...]), g_split)
        self.s[...] = p
        p_split = split(p)
        kind = lax.broadcasted_iota(jnp.int32, (z.lines, size), 0)
        self.lines = []
        for i in range(n):
            lines = self.vout[i]
            lacks = jnp.sum(jnp.sum(lines[4 : 4 + n], axis=0, keepdims=True), axis=1, keepdims=True)
            self.lines.append(jnp.where(kind == 1, lines + lacks, jnp.where(kind == 3, 1.0, lines)))
        rows = jnp.concatenate(self.lines, axis=1)
        self.first = mm3(split(rows), p_split) / root
        second = mm3(split(self.first), p_split) / root
        self.vcol[...] = second.T
        self.pull_bar = second[1:2]
        self.pull_mine = self.vcol[mine, 1:2] - jnp.sum(self.pull_bar, axis=1, keepdims=True) / total
        mix = self.s[mine, :] / root + self.vcol[mine, 0:1] / scale
        row_weights = self.first[3:4] + jnp.sum(second[0:1], axis=1, keepdims=True) / scale
        mix = split(mix + (1.0 - row_weights) / total)
        for e in range(2, z.rows + 2):
            self.mixed[e] = mm3(mix, (self.chi[e], self.clo[e]))
        r = z.rows
        row = lambda e: self.mixed.at[e]
        bar_halo = (
            self.between(row(r + 1), row(1), row(2), row(r + 2), self.bar_halo),
            self.between(row(r), row(0), row(3), row(r + 3), self.far_halo),
        )
        self.fg[...] = mm3((self.fh[...], self.fl[...]), g_split)
        self.weigh[...] = 2.25 * identity + 4.5 * (self.fg[...] + self.f[...] - self.s[...])
        self.norm, self.root = norm, root
        for k, ref in enumerate((self.f, self.g, self.fg)):
            rows = slice(k * size, (k + 1) * size)
            self.lh[rows, :], self.ll[rows, :] = split(self.centred(ref))
        yield bar_halo

    def centred(self, ref):
        return ref[self.block(self.m_id), :] - jnp.sum(ref[...], axis=0, keepdims=True) / self.z.total

    def respond(self, scale, cross):
        z, m = self.z, self.m_id
        n, size, total = z.n_mem, z.members, z.total
        col = lambda k: slice(k * size, (k + 1) * size)
        norm, root = self.norm, self.root
        turned = [x.T for x in self.lines]
        first_t = self.first.T
        for i, j, block in self.blocks_of(cross, 2):
            block = (scale / root) * (
                block + 0.5 * (self.lines[i][4 + j : 5 + j] + turned[j][:, 4 + i : 5 + i])
            ) + (0.5 / root) * (
                turned[i][:, 1:2] * self.first[0:1, col(j)]
                + first_t[col(i), 0:1] * self.lines[j][1:2]
                + first_t[col(i), 1:2] * self.lines[j][0:1]
                + turned[i][:, 0:1] * self.first[1:2, col(j)]
            )
            self.s[col(i), col(j)] = block
            if i != j:
                self.s[col(j), col(i)] = block.T
        scale_bar = whole_sum(self.s[...] * self.weigh[...]) / norm
        self.sh[...], self.sl[...] = split(self.s[...])
        s_split = (self.sh[...], self.sl[...])
        s_mine = self.centred(self.s)
        f_split = (self.fh[...], self.fl[...])
        through = mm3((self.lh[...], self.ll[...]), s_split)
        bar = 1.5 * s_mine + through[2 * size :]
        bar = bar + mm3(split(mm3(split(s_mine), f_split)), (self.gh[...], self.gl[...]))
        bar = bar + mm3(split(through[:size]), (self.f2h[...], self.f2l[...]))
        bar = bar + mm3(split(through[size : 2 * size]), f_split)
        unit = (
            lax.broadcasted_iota(jnp.int32, (size, total), 0) + m * size
            == lax.broadcasted_iota(jnp.int32, (size, total), 1)
        ).astype(F32) - 1.0 / total
        sym = 2.0 * scale_bar * (3.0 * unit - 2.0 * self.centred(self.f)) - bar / norm
        sym = sym - (scale / total) * self.pull_bar
        prec = [self.prec[...], self.aux[1, 6:7, :], self.aux[z.rows + 2, 6:7, :]]
        observed = (jnp.concatenate(prec, axis=1) / scale) * (
            mm3(split(sym), (self.ahi[...], self.alo[...])) + self.pull_mine * self.innov[0:1, :]
        )
        return observed * self.slope[...]


    def pull_back(self, src, first, dst, rows, to_sea):
        z = self.z
        for i in rows:
            e = first + i
            c = [self.aux[e, k : k + 1, :] for k in range(4)]
            lane = lax.broadcasted_iota(jnp.int32, (1, z.cols), 1)
            keep = 1.0 - c[0] - c[1] - c[2] - c[3]
            from_south, from_north = self.aux[e + 1, 0:1, :], self.aux[e - 1, 1:2, :]
            sea = self.aux[e, 4:5, :]
            east = pltpu.roll(jnp.broadcast_to(jnp.where(lane == 0, 0.0, c[2]), (8, z.cols)), z.cols - 1, 1)[:1]
            west = pltpu.roll(jnp.broadcast_to(jnp.where(lane == z.cols - 1, 0.0, c[3]), (8, z.cols)), 1, 1)[:1]
            if to_sea:
                keep, from_south, from_north = sea * keep, sea * from_south, sea * from_north
                east, west = sea * east, sea * west
            for part in self.chunks():
                v = src[i + 1, part, :]
                dst[i, part, :] = (
                    keep * v
                    + from_south * src[i + 2, part, :]
                    + from_north * src[i, part, :]
                    + east * pltpu.roll(v, z.cols - 1, 1)
                    + west * pltpu.roll(v, 1, 1)
                )

    def coefficient_terms(self, weight, w0, field, f0, which):
        z = self.z
        lane = lax.broadcasted_iota(jnp.int32, (1, z.cols), 1)
        rows = {}
        for r in which:
            sums = [0.0] * 5
            for part in self.chunks():
                w = weight[w0 + r, part, :]
                c = field[f0 + r, part, :]
                terms = [
                    w * field[f0 + r - 1, part, :],
                    w * field[f0 + r + 1, part, :],
                    w * pltpu.roll(c, 1, 1),
                    w * pltpu.roll(c, z.cols - 1, 1),
                    w * c,
                ]
                sums = [x + y for x, y in zip(sums, terms)]
            north, south, west, east, own = [jnp.sum(x, axis=0, keepdims=True) for x in sums]
            west = jnp.where(lane == 0, 0.0, west)
            east = jnp.where(lane == z.cols - 1, 0.0, east)
            rows[r] = [north - own, south - own, west - own, east - own]
        return rows


def kernel(z, *refs):
    small = ["stencil", "sea", "sites", "data", "prec"]
    names = ["prior", "cot"] + [name + "_in" for name in small] + ["grad", "coef"]
    names += list(scratch_of(z))
    g = Step(z, dict(zip(names, refs)))
    scale = jnp.sqrt(jnp.float32(z.total - 1))
    s, m = g.s_id, g.m_id
    r, ext = z.rows, z.rows + 4
    mine = g.block(m)

    entered = g.barrier()
    loads = []
    for i in range(r):
        loads.append(pltpu.make_async_copy(g.prior.at[:, i], g.pext.at[2 + i], g.own.at[0, i]))
    for i in range(r):
        loads.append(pltpu.make_async_copy(g.cot.at[:, i], g.cotf.at[2 + i, mine], g.own.at[1, i]))
    few = [
        pltpu.make_async_copy(getattr(g, name + "_in"), getattr(g, name), g.few.at[i])
        for i, name in enumerate(small)
    ]
    for copy in loads[:r] + few + loads[r:]:
        copy.start()
    for copy in few:
        copy.wait()
    for i in range(r):
        g.aux[2 + i, 0:4, :] = g.stencil[:, i, :]
        g.aux[2 + i, 4:5, :] = g.sea[i : i + 1, :].astype(F32)
        g.aux[2 + i, 5:6, :] = g.sites[...].astype(F32)
        g.aux[2 + i, 6:7, :] = g.prec[...]
        g.aux[2 + i, 7:8, :] = g.data[...]
    for e, edge in ((0, 0), (1, 0), (ext - 2, z.n_space - 1), (ext - 1, z.n_space - 1)):
        @pl.when(s == edge)
        def _():
            g.pext[e] = jnp.zeros((z.members, z.cols), F32)
            g.mixed[e] = jnp.zeros((z.members, z.cols), F32)
            g.aux[e] = jnp.zeros((8, z.cols), F32)
            g.beside_seen[0 if e < 2 else 1, m] = jnp.zeros((z.members, z.sites), F32)
    for copy in loads[:r]:
        copy.wait()
    entered()
    halo = g.halo_send(g.pext, g.halo)
    if z.rounds:
        g.vouch(1)
    for copy in loads[r:]:
        copy.wait()
    cot_forward, cot_wait = g.pair_gather(lambda which: g.cotf.at[pl.ds(2, r), g.block(which)], g.cot_sem)
    aux_halo = g.halo_send(g.aux, g.aux_halo)
    g.mark_sites()
    aux_halo()
    g.mark_sites_beside()
    cot_forward()
    for k in range(1, z.rounds):
        g.hear(k)
        g.vouch(k + 1)
    halo()

    g.advance(g.pext, 1, g.fext, r + 2)
    g.advance(g.fext, 2, g.state, r)
    g.obsf[m] = g.observe()
    obs_wait = g.mem_send(g.obsf, g.obs_sem)
    own_sums = [jnp.sum(g.state[i], axis=0, keepdims=True) for i in range(r)]
    padding = [jnp.zeros((-r % 8, z.cols), F32)] * (r % 8 > 0)
    g.sums[m] = jnp.concatenate(own_sums + padding, axis=0)
    sums_wait = g.mem_send(g.sums, g.sum_sem)
    seen_halo = g.between(
        g.seen, g.beside_seen.at[0, m], g.seen, g.beside_seen.at[1, m], g.seen_halo
    )
    cot_wait()
    for e in range(2, r + 2):
        g.chi[e], g.clo[e] = split(g.cotf[e])
    dev = [split((g.state[i] - own_sums[i] / z.members) / scale) for i in range(r)]
    mean_bar = g.cross_rows(dev)
    obs_wait()
    mean, diag = g.pack_gram(scale)
    if z.rounds:
        g.hear(z.rounds)
    gram, cross = Reduction(g, "gram"), Reduction(g, "cross")
    gram.scatter()
    g.pack_cross()
    cross.scatter()
    sums_wait()
    g.pack_lines(scale, mean_bar, own_sums, mean, diag)
    g.send_lines()
    seen_halo()
    extras = [
        g.pair_gather(lambda which: g.beside_seen.at[:, which], g.seen_sem),
    ]
    gram.start()
    cross.start()
    lines_wait = g.sum_lines()
    for forward, _ in extras:
        forward()
    gram.forward_all()
    cross.forward_all()
    for _, wait in extras:
        wait()
    g.observe_beside()
    gram.pass_on()
    lines_wait()
    gram.finish()
    parts = g.transform(scale, gram)
    next(parts)
    cross.pass_on()
    bar_halo = next(parts)
    cross.finish()
    g.picked[...] = g.respond(scale, cross)
    g.spread(0, range(2, r + 2))
    second = g.coefficient_terms(g.sbext, 2, g.fext, 1, range(r))
    g.pull_back(g.sbext, 1, g.fbar, range(2, r), True)
    firsts = g.coefficient_terms(g.fbar, 1, g.pext, 2, range(1, r - 1))
    bar_halo[0]()
    g.spread(1, (1,))
    g.spread(2, (r + 2,))
    outer = (0, r - 1) if r > 1 else (0,)
    g.pull_back(g.sbext, 1, g.fbar, [i + 1 for i in outer], True)
    firsts.update(g.coefficient_terms(g.fbar, 1, g.pext, 2, outer))
    g.cbuf[m] = jnp.concatenate(
        [second[i][k] + firsts[i][k] for k in range(4) for i in range(r)], axis=0
    )
    c_wait = g.mem_send(g.cbuf, g.c_sem)
    bar_halo[1]()
    g.spread(1, (0,))
    g.spread(2, (r + 3,))
    g.pull_back(g.sbext, 1, g.fbar, (0, r + 1), True)
    g.pull_back(g.fbar, 2, g.grad, range(r), False)
    c_wait()
    both = g.cbuf[0]
    for k in range(1, z.n_mem):
        both = both + g.cbuf[k]
    for k in range(4):
        g.coef[k] = both[k * r : (k + 1) * r]
    g.finish_sends()


def place(z, last, sums, grad, coef, scaled, sem):
    stores = [pltpu.make_async_copy(last.at[i], grad.at[:, i], sem.at[i]) for i in range(z.rows)]
    for copy in stores:
        copy.start()
    scaled[...] = sums[...] / jnp.sqrt(jnp.float32(z.total))
    stores.append(pltpu.make_async_copy(scaled, coef, sem.at[z.rows]))
    stores[-1].start()
    for copy in stores:
        copy.wait()


def local(n_space, n_mem, prior, stencil, sea_mask, sites, data, precision, cotangent):
    z = Sizes(n_space, n_mem, prior, sites)
    any_spec = pl.BlockSpec(memory_space=pl.ANY)
    turned = (z.rows, z.members, z.cols)
    factors = (4, z.rows, z.cols)
    inputs = (prior, cotangent, stencil, sea_mask, sites, data[None], precision[None])
    last, sums = pl.pallas_call(
        functools.partial(kernel, z),
        out_shape=(jax.ShapeDtypeStruct(turned, F32), jax.ShapeDtypeStruct(factors, F32)),
        in_specs=[pl.BlockSpec(memory_space=pltpu.HBM)] * 7,
        out_specs=(VMEM_SPEC, VMEM_SPEC),
        scratch_shapes=list(scratch_of(z).values()),
        compiler_params=pltpu.CompilerParams(
            collective_id=1, has_side_effects=True, vmem_limit_bytes=GRANT
        ),
        name="adjoint",
    )(*[pltpu.with_memory_space_constraint(x, pltpu.HBM) for x in inputs])
    return pl.pallas_call(
        functools.partial(place, z),
        out_shape=(jax.ShapeDtypeStruct(prior.shape, F32), jax.ShapeDtypeStruct(factors, F32)),
        in_specs=[VMEM_SPEC, VMEM_SPEC],
        out_specs=(any_spec, any_spec),
        scratch_shapes=[pltpu.VMEM(factors, F32), pltpu.SemaphoreType.DMA((z.rows + 1,))],
        compiler_params=pltpu.CompilerParams(vmem_limit_bytes=4 * 1024 * 1024),
        name="place",
    )(last, sums)


def solution(mesh):
    placed = (
        P("mem", "space", None),
        P(None, "space", None),
        P("space", None),
        P("space", None),
        P("space"),
        P("space"),
        P("mem", "space", None),
    )
    return jax.shard_map(
        functools.partial(local, mesh.shape["space"], mesh.shape["mem"]),
        mesh=mesh,
        in_specs=placed,
        out_specs=(P("mem", "space", None), P(None, "space", None)),
        check_vma=False,
    )
```

```python
import functools
import jax
import jax.numpy as jnp
from jax import lax
from jax.experimental import pallas as pl
from jax.experimental.pallas import tpu as pltpu
from jax.sharding import PartitionSpec as P

MESH = pl.DeviceIdType.MESH
F32 = jnp.float32
GRANT = 48 * 1024 * 1024
BF16 = jnp.bfloat16
VMEM_SPEC = pl.BlockSpec(memory_space=pltpu.VMEM)


def remote(src, dst, send, recv, s, m):
    return pltpu.make_async_remote_copy(
        src_ref=src, dst_ref=dst, send_sem=send, recv_sem=recv, device_id=(s, m), device_id_type=MESH
    )


def split(x):
    lead = x.astype(BF16)
    return lead, (x - lead.astype(F32)).astype(BF16)


def split3(x):
    lead = x.astype(BF16)
    rest = x - lead.astype(F32)
    middle = rest.astype(BF16)
    return lead, middle, (rest - middle.astype(F32)).astype(BF16)


def plain(a, b):
    return jnp.dot(a, b, preferred_element_type=F32)


def plain_t(a, b):
    return lax.dot_general(a, b, (((1,), (1,)), ((), ())), preferred_element_type=F32)


def mm3(a, b):
    left = jnp.concatenate([a[0], a[0], a[1]], axis=1)
    return plain(left, jnp.concatenate([b[0], b[1], b[0]], axis=0))


def mm3_t(a, b):
    left = jnp.concatenate([a[0], a[0], a[1]], axis=1)
    return plain_t(left, jnp.concatenate([b[0], b[1], b[0]], axis=1))


def whole_sum(x):
    return jnp.sum(jnp.sum(x, axis=0, keepdims=True), axis=1, keepdims=True)


def eye(size):
    return lax.broadcasted_iota(jnp.int32, (size, size), 0) == lax.broadcasted_iota(
        jnp.int32, (size, size), 1
    )


class Sizes:
    def __init__(self, n_space, n_mem, prior, sites):
        self.n_space, self.n_mem = n_space, n_mem
        self.members, self.rows, self.cols = prior.shape
        self.total = self.members * n_mem
        self.sites = sites.shape[-1]
        self.near = 2 if n_space % 2 == 0 else 1
        self.far = n_space // self.near
        self.half = 2 if n_mem % 2 == 0 else 1
        self.wide = n_mem // self.half
        self.group = max(1, self.far // 4)
        self.groups = self.far // self.group
        self.height = n_mem // 2 * self.members // n_space
        self.lines = 8 * pl.cdiv(4 + n_mem, 8)
        self.rounds = max(0, (n_space - 1).bit_length() - 1)


def scratch_of(z):
    dma = pltpu.SemaphoreType.DMA
    ext = z.rows + 4
    v = lambda *shape: pltpu.VMEM(shape, F32)
    b = lambda *shape: pltpu.VMEM(shape, BF16)
    square = (z.total, z.total)
    half_square = (z.n_space, z.height, z.members)
    gathered = (z.n_mem, z.far, z.near, z.height, z.members)
    found = dict(
        stencil=v(4, z.rows, z.cols),
        sea=pltpu.VMEM((z.rows, z.cols), jnp.int32),
        sites=pltpu.VMEM((1, z.sites), jnp.int32),
        data=v(1, z.sites),
        prec=v(1, z.sites),
        few=dma((5,)),
        token=pltpu.SemaphoreType.REGULAR((max(1, z.rounds), 2)),
        pext=v(ext, z.members, z.cols),
        aux=v(ext, 8, z.cols),
        cotf=v(ext, z.total, z.cols),
        chi=b(ext, z.total, z.cols),
        clo=b(ext, z.total, z.cols),
        seen=v(z.members, z.sites),
        beside_seen=v(2, z.n_mem, z.members, z.sites),
        slope=v(z.members, 3 * z.sites),
        fext=v(z.rows + 2, z.members, z.cols),
        state=v(z.rows, z.members, z.cols),
        hot=b(ext, z.cols, z.sites),
        obsf=v(z.n_mem, z.members, z.sites),
        ahi=b(z.total, 3 * z.sites),
        alo=b(z.total, 3 * z.sites),
        innov=v(8, 3 * z.sites),
        sums=v(z.n_mem, 8 * pl.cdiv(z.rows, 8), z.cols),
        dmat=v(z.n_mem, z.members, z.members),
        dx=v(z.n_mem, z.members, z.members),
        vec=v(z.lines, z.members),
        vbuf=v(z.n_space, z.lines, z.members),
        vout=v(z.n_mem, z.lines, z.members),
        f=v(*square),
        g=v(*square),
        fg=v(*square),
        s=v(*square),
        weigh=v(*square),
        fh=b(*square), fl=b(*square),
        f2h=b(*square), f2l=b(*square),
        gh=b(*square), gl=b(*square),
        sh=b(*square), sl=b(*square),
        lh=b(3 * z.members, z.total), ll=b(3 * z.members, z.total),
        vcol=v(z.total, z.lines),
        sbext=v(ext, z.members, z.cols),
        mixed=v(ext, z.members, z.cols),
        picked=v(z.members, 3 * z.sites),
        fbar=v(z.rows + 2, z.members, z.cols),
        cbuf=v(z.n_mem, 4 * z.rows, z.cols),
        own=dma((2, z.rows)),
        halo=dma((2, 2)),
        aux_halo=dma((2, 2)),
        bar_halo=dma((2, 2)),
        far_halo=dma((2, 2)),
        seen_halo=dma((2, 2)),
        cot_sem=dma((2, z.half, z.wide)),
        seen_sem=dma((2, z.half, z.wide)),
        obs_sem=dma((2, z.n_mem)),
        sum_sem=dma((2, z.n_mem)),
        d_sem=dma((2, z.n_mem)),
        v_sem=dma((2, z.n_space)),
        vg_sem=dma((2, z.n_mem)),
        c_sem=dma((2, z.n_mem)),
    )
    for tag in ("gram", "cross"):
        found[tag + "_src"] = v(*half_square)
        found[tag + "_buf"] = v(*half_square)
        found[tag + "_out"] = v(*gathered)
        found[tag + "_rs"] = dma((2, z.n_space))
        found[tag + "_a"] = dma((2, z.far))
        found[tag + "_x"] = dma((2, z.near, z.wide, z.groups))
        found[tag + "_q"] = dma((2, z.half, z.near, z.wide, z.groups))
    return found


class Reduction:
    def __init__(self, g, tag):
        self.g, self.z = g, g.z
        for name in ("src", "buf", "out", "rs", "a", "x", "q"):
            setattr(self, name, getattr(g, tag + "_" + name))
        z = g.z
        self.a_id, self.b_id = g.s_id // z.near, lax.rem(g.s_id, z.near)
        self.p_id, self.q_id = g.m_id // z.half, lax.rem(g.m_id, z.half)

    def scatter(self):
        z, s, m = self.z, self.g.s_id, self.g.m_id
        self.copies = []
        for k in range(1, z.n_space):
            to = lax.rem(s + k, z.n_space)
            self.copies.append(
                remote(self.src.at[to], self.buf.at[s], self.rs.at[0, k], self.rs.at[1, k], to, m)
            )
            self.copies[-1].start()
        self.g.waits += [(copy, None) for copy in self.copies]

    def start(self):
        z, s, m = self.z, self.g.s_id, self.g.m_id
        a, b = self.a_id, self.b_id
        self.buf[s] = self.src[s]
        for copy in self.copies:
            copy.wait_recv()
        total = self.buf[0]
        for k in range(1, z.n_space):
            total = total + self.buf[k]
        self.out[m, a, b] = total
        piece = self.out.at[m, a, b]
        stage = []
        for k in range(1, z.far):
            to = lax.rem(a + k, z.far) * z.near + b
            stage.append(remote(piece, piece, self.a.at[0, k], self.a.at[1, k], to, m))
            stage[-1].start()
        self.g.waits += [(copy, None) for copy in stage]
        if z.group == 1:
            self.steps = [([], a)] + [
                ([stage[k - 1]], lax.rem(a + z.far - k, z.far)) for k in range(1, z.far)
            ]
            self.forward(0)
        else:
            self.steps = [(stage if n == 0 else [], n * z.group) for n in range(z.groups)]

    def forward(self, index):
        z, s, m = self.z, self.g.s_id, self.g.m_id
        needs, start = self.steps[index]
        for copy in needs:
            copy.wait_recv()
        piece = self.out.at[m, pl.ds(start, z.group), self.b_id]
        for kb, kp in self.offsets():
            to_s = self.a_id * z.near + lax.rem(self.b_id + kb, z.near)
            to_m = lax.rem(self.p_id + kp, z.wide) * z.half + self.q_id
            self.send(piece, self.x.at[0, kb, kp, index], self.x.at[1, kb, kp, index], to_s, to_m)
        self.beside(piece, 0, 0, index)

    def forward_all(self):
        for index in range(1 if self.z.group == 1 else 0, self.z.groups):
            self.forward(index)

    def offsets(self):
        z = self.z
        return [(kb, kp) for kb in range(z.near) for kp in range(z.wide) if kb or kp]

    def send(self, piece, *where):
        copy = remote(piece, piece, *where)
        copy.start()
        self.g.waits.append((copy, None))

    def beside(self, piece, kb, kp, index):
        z = self.z
        for kq in range(1, z.half):
            to = self.p_id * z.half + lax.rem(self.q_id + kq, z.half)
            self.send(
                piece, self.q.at[0, kq, kb, kp, index], self.q.at[1, kq, kb, kp, index], self.g.s_id, to
            )

    def piece_of(self, kb, kp, kq, index):
        z = self.z
        which_b = lax.rem(self.b_id + z.near - kb, z.near)
        which_p = lax.rem(self.p_id + z.wide - kp, z.wide)
        which_q = lax.rem(self.q_id + z.half - kq, z.half)
        return self.out.at[which_p * z.half + which_q, pl.ds(self.steps[index][1], z.group), which_b]

    def pass_on(self):
        for index in range(self.z.groups):
            for kb, kp in self.offsets():
                piece = self.piece_of(kb, kp, 0, index)
                self.arrived(piece, self.x.at[0, kb, kp, index], self.x.at[1, kb, kp, index])
                self.beside(piece, kb, kp, index)

    def arrived(self, piece, send, recv):
        remote(piece, piece, send, recv, self.g.s_id, self.g.m_id).wait_recv()

    def finish(self):
        z = self.z
        for index in range(z.groups):
            for kb in range(z.near):
                for kp in range(z.wide):
                    for kq in range(1, z.half):
                        self.arrived(
                            self.piece_of(kb, kp, kq, index),
                            self.q.at[0, kq, kb, kp, index], self.q.at[1, kq, kb, kp, index],
                        )

    def whole(self, i):
        z = self.z
        return self.out[i].reshape(z.n_mem // 2 * z.members, z.members)


class Step:
    def __init__(self, z, refs):
        self.z = z
        self.__dict__.update(refs)
        self.s_id, self.m_id = lax.axis_index("space"), lax.axis_index("mem")
        self.lo = lax.rem(self.m_id, z.n_mem // 2)
        self.hi = self.m_id // (z.n_mem // 2)
        self.waits = []

    def finish_sends(self):
        for copy, when in self.waits:
            if when is None:
                copy.wait_send()
            else:
                pl.when(when)(copy.wait_send)

    def barrier(self):
        z, s, m = self.z, self.s_id, self.m_id
        peers = [(s, lax.rem(m + k, z.n_mem)) for k in range(1, z.n_mem)]
        a, b = s // z.near, lax.rem(s, z.near)
        p, q = m // z.half, lax.rem(m, z.half)
        for kb in range(1, z.near):
            for kp in range(1, z.wide):
                peers.append((
                    a * z.near + lax.rem(b + kb, z.near), lax.rem(p + kp, z.wide) * z.half + q
                ))
        barrier = pltpu.get_barrier_semaphore()
        count = len(peers)
        for peer in peers:
            pl.semaphore_signal(barrier, inc=1, device_id=peer, device_id_type=MESH)
        for step in (1, -1, 2, -2):
            there = self.exists(step)
            count = count + there.astype(jnp.int32)

            @pl.when(there)
            def _():
                pl.semaphore_signal(barrier, inc=1, device_id=(s + step, m), device_id_type=MESH)

        return lambda: pl.semaphore_wait(barrier, count)

    def exists(self, step):
        to = self.s_id + step
        return (to >= 0) & (to < self.z.n_space)

    def vouch(self, round_):
        for side, step in ((0, 2**round_), (1, -(2**round_))):
            @pl.when(self.exists(step))
            def _():
                pl.semaphore_signal(
                    self.token.at[round_ - 1, side], inc=1,
                    device_id=(self.s_id + step, self.m_id), device_id_type=MESH,
                )

    def hear(self, round_):
        for side, step in ((0, -(2**round_)), (1, 2**round_)):
            @pl.when(self.exists(step))
            def _():
                pl.semaphore_wait(self.token.at[round_ - 1, side], 1)

    def between(self, up_src, up_dst, down_src, down_dst, sem):
        z, s, m = self.z, self.s_id, self.m_id
        has_low, has_high = s > 0, s < z.n_space - 1
        up = remote(up_src, up_dst, sem.at[0, 0], sem.at[1, 0], s + 1, m)
        down = remote(down_src, down_dst, sem.at[0, 1], sem.at[1, 1], s - 1, m)
        pl.when(has_high)(up.start)
        pl.when(has_low)(down.start)
        self.waits += [(up, has_high), (down, has_low)]

        def wait():
            pl.when(has_low)(up.wait_recv)
            pl.when(has_high)(down.wait_recv)

        return wait

    def halo_send(self, ref, sem):
        r = self.z.rows
        at = lambda row: ref.at[pl.ds(row, 2)]
        return self.between(at(r), at(0), at(2), at(r + 2), sem)

    def pair_gather(self, part, sem):
        z, s, m = self.z, self.s_id, self.m_id
        p, q = m // z.half, lax.rem(m, z.half)
        across = [lax.rem(p + k, z.wide) * z.half + q for k in range(1, z.wide)]
        beside = [p * z.half + lax.rem(q + k, z.half) for k in range(1, z.half)]
        mine = part(m)
        hops, sides = [], []
        for k, to in enumerate(across):
            hops.append(remote(mine, mine, sem.at[0, 0, k + 1], sem.at[1, 0, k + 1], s, to))
            hops[-1].start()
        for k, to in enumerate(beside):
            sides.append(remote(mine, mine, sem.at[0, k + 1, 0], sem.at[1, k + 1, 0], s, to))
            sides[-1].start()

        def forward():
            for kp, hop in enumerate(hops):
                hop.wait_recv()
                piece = part(lax.rem(p + z.wide - kp - 1, z.wide) * z.half + q)
                for k, to in enumerate(beside):
                    copy = remote(
                        piece, piece, sem.at[0, k + 1, kp + 1], sem.at[1, k + 1, kp + 1], s, to
                    )
                    copy.start()
                    sides.append(copy)

        def wait():
            for copy in sides:
                copy.wait_recv()
            self.waits.extend((copy, None) for copy in hops + sides)

        return forward, wait

    def mem_send(self, ref, sem):
        z, s, m = self.z, self.s_id, self.m_id
        copies = []
        for k in range(1, z.n_mem):
            to = lax.rem(m + k, z.n_mem)
            copies.append(remote(ref.at[m], ref.at[m], sem.at[0, k], sem.at[1, k], s, to))
            copies[-1].start()

        def wait():
            for copy in copies:
                copy.wait_recv()
            self.waits.extend((copy, None) for copy in copies)

        return wait

    def block(self, which):
        size = self.z.members
        return pl.ds(pl.multiple_of(which * size, size), size)


    def coefficients(self, e):
        z = self.z
        c = [self.aux[e, k : k + 1, :] for k in range(4)]
        sea = self.aux[e, 4:5, :]
        lane = lax.broadcasted_iota(jnp.int32, (1, z.cols), 1)
        keep = sea * (1.0 - c[0] - c[1] - c[2] - c[3])
        west = jnp.where(lane == 0, 0.0, c[2])
        east = jnp.where(lane == z.cols - 1, 0.0, c[3])
        return keep, sea * c[0], sea * c[1], sea * west, sea * east

    def chunks(self):
        size = min(32, self.z.members)
        return [pl.ds(k, size) for k in range(0, self.z.members, size)]

    def advance(self, src, first, dst, count):
        z = self.z
        for i in range(count):
            keep, north, south, west, east = self.coefficients(first + i)
            for part in self.chunks():
                v = src[i + 1, part, :]
                dst[i, part, :] = (
                    keep * v
                    + north * src[i, part, :]
                    + south * src[i + 2, part, :]
                    + west * pltpu.roll(v, 1, 1)
                    + east * pltpu.roll(v, z.cols - 1, 1)
                )

    def observe(self):
        z = self.z
        pieces = [split3(self.state[r]) for r in range(z.rows)]
        left = jnp.concatenate([pieces[r][k] for k in range(3) for r in range(z.rows)], axis=1)
        hot = jnp.concatenate([self.hot[2 + r] for r in range(z.rows)] * 3, axis=0)
        picked = plain(left, hot)
        self.seen[...] = picked
        tanh = jnp.tanh(picked)
        self.slope[:, : z.sites] = 1.0 + 0.5 * (1.0 - tanh * tanh)
        return picked + 0.5 * tanh

    def observe_beside(self):
        z = self.z
        scale = jnp.sqrt(jnp.float32(z.total - 1))
        for side, e in ((0, 1), (1, z.rows + 2)):
            cols = slice((1 + side) * z.sites, (2 + side) * z.sites)
            prec, data = self.aux[e, 6:7, :], self.aux[e, 7:8, :]
            found, mean = [], jnp.zeros((1, z.sites), F32)
            for k in range(z.n_mem):
                picked = self.beside_seen[side, k]
                found.append(picked + 0.5 * jnp.tanh(picked))
                mean = mean + jnp.sum(found[-1], axis=0, keepdims=True)
            mean = mean / z.total
            for k in range(z.n_mem):
                rows = slice(k * z.members, (k + 1) * z.members)
                self.ahi[rows, cols], self.alo[rows, cols] = split((found[k] - mean) * (prec / scale))
            tanh = jnp.tanh(self.beside_seen[side, self.m_id])
            self.slope[:, cols] = 1.0 + 0.5 * (1.0 - tanh * tanh)
            self.innov[0:1, cols] = prec * (data - mean)

    def mark(self, e, row, sites):
        z = self.z
        cell = lax.broadcasted_iota(jnp.int32, (z.cols, z.sites), 0) + row * z.cols
        self.hot[e] = jnp.where(cell == sites, 1.0, 0.0).astype(BF16)

    def mark_sites(self):
        for r in range(self.z.rows):
            self.mark(2 + r, r, self.sites[...])

    def mark_sites_beside(self):
        r = self.z.rows
        low, high = (self.aux[e, 5:6, :].astype(jnp.int32) for e in (1, r + 2))
        for k in range(2):
            self.mark(k, r - 2 + k, low)
            self.mark(r + 2 + k, k, high)

    def spread(self, slot, rows):
        z = self.z
        hi, lo = split(self.picked[:, slot * z.sites : (slot + 1) * z.sites])
        for e in rows:
            hot = jnp.concatenate([self.hot[e], self.hot[e]], axis=1)
            field = self.mixed[e] + plain_t(jnp.concatenate([hi, lo], axis=1), hot)
            self.sbext[e] = self.aux[e, 4:5, :] * field


    def fold(self, block):
        size = self.z.members
        half = size // 2
        bottom = pltpu.roll(block[half:], half, 1)
        lane = lax.broadcasted_iota(jnp.int32, (half, size), 1)
        line = lax.broadcasted_iota(jnp.int32, (half, size), 0)
        return jnp.where(lane < line, bottom, block[:half])

    def unfold(self, folded, diagonal):
        size = self.z.members
        half = size // 2
        wide = jnp.concatenate([folded, pltpu.roll(folded, half, 1)], axis=0)
        lane = lax.broadcasted_iota(jnp.int32, (size, size), 1)
        line = lax.broadcasted_iota(jnp.int32, (size, size), 0)
        above, below = lane - line, lane - half
        straight = ((line < half) & (above >= 0)) | ((line >= half) & (below >= 0) & (above < 0))
        block = jnp.where(straight, wide, wide.T)
        return jnp.where((line >= half) & (above == 0), diagonal, block)

    def cross_rows(self, dev):
        z, s, m = self.z, self.s_id, self.m_id
        n, size = z.n_mem, z.members
        half = size // 2
        self.d_copies = []
        mean_bar = jnp.zeros((size, 1), F32)
        for k in list(range(n - 1, 0, -1)) + [0]:
            there = lax.rem(m + k, n)
            rows = self.block(there)
            part = mm3_t(
                [jnp.concatenate([d[p] for d in dev], axis=1) for p in range(2)],
                [
                    jnp.concatenate([ref[2 + i, rows, :] for i in range(z.rows)], axis=1)
                    for ref in (self.chi, self.clo)
                ],
            )
            mean_bar = mean_bar + jnp.sum(part, axis=1, keepdims=True)
            if 2 * k == n:
                part = jnp.where(self.hi == 0, part, part.T)
            self.dmat[k] = part
            copy = None
            if 2 * k > n:
                copy = remote(
                    self.dmat.at[k], self.dx.at[n - k], self.d_sem.at[0, k], self.d_sem.at[1, k], s, there
                )
            elif 2 * k == n:
                theirs = pl.ds(pl.multiple_of((1 - self.hi) * half, half), half)
                copy = remote(
                    self.dmat.at[k, theirs], self.dx.at[k, pl.ds(0, half)],
                    self.d_sem.at[0, k], self.d_sem.at[1, k], s, there,
                )
            if copy is not None:
                copy.start()
                self.d_copies.append(copy)
        self.waits += [(copy, None) for copy in self.d_copies]
        return mean_bar

    def pack_gram(self, scale):
        z, m = self.z, self.m_id
        n, size = z.n_mem, z.members
        half = size // 2
        mean = jnp.zeros((1, z.sites), F32)
        for k in range(n):
            mean = mean + jnp.sum(self.obsf[k], axis=0, keepdims=True)
        mean = mean / z.total
        prec = self.prec[...]
        for k in range(n):
            rows = slice(k * size, (k + 1) * size)
            self.ahi[rows, : z.sites], self.alo[rows, : z.sites] = split((self.obsf[k] - mean) * (prec / scale))
        anom = lambda rows: (self.ahi[rows, : z.sites], self.alo[rows, : z.sites])
        mine = anom(self.block(m))
        diag = mm3_t(mine, mine)
        parts = [self.fold(diag)]
        base = self.lo * size + self.hi * half
        upper = anom(pl.ds(pl.multiple_of(base, half), half))
        parts.append(mm3_t(upper, anom(self.block(self.lo + n // 2))))
        for k in range(1, n // 2):
            parts.append(mm3_t(mine, anom(self.block(lax.rem(m + k, n)))))
        self.gram_src[...] = jnp.concatenate(parts, axis=0).reshape(z.n_space, z.height, size)
        return mean, diag

    def pack_lines(self, scale, mean_bar, own_sums, mean, diag):
        z, m = self.z, self.m_id
        n, size = z.n_mem, z.members
        prec = self.prec[...]
        innov = prec * (self.data[...] - mean)
        self.innov[0:1, : z.sites] = innov
        exact = (self.obsf[m] - mean) * (prec / scale)
        lane = lax.broadcasted_iota(jnp.int32, (size, size), 1)
        diagonal = lambda x: jnp.sum(jnp.where(eye(size), x, 0.0), axis=1, keepdims=True)
        pull = jnp.sum(exact * innov, axis=1, keepdims=True)
        columns = [pull, mean_bar, diagonal(self.cross_diag), diagonal(diag)]
        stacked = jnp.zeros((size, size), F32)
        for k, column in enumerate(columns):
            stacked = jnp.where(lane == k, column, stacked)
        total = self.sums[0]
        for k in range(1, n):
            total = total + self.sums[k]
        term = None
        for r in range(z.rows):
            lacks = (own_sums[r] / size - total[r : r + 1] / z.total) / scale
            this = mm3_t(split(jnp.broadcast_to(lacks, (8, z.cols))), (self.chi[2 + r], self.clo[2 + r]))
            term = this if term is None else term + this
        lines = [stacked.T[:4]] + [term[:1, k * size : (k + 1) * size] for k in range(n)]
        if z.lines > 4 + n:
            lines.append(jnp.zeros((z.lines - 4 - n, size), F32))
        self.vec[...] = jnp.concatenate(lines, axis=0)

    def pack_cross(self):
        z = self.z
        n, size = z.n_mem, z.members
        half = size // 2
        for copy in self.d_copies:
            copy.wait_recv()
        cross = self.dmat[0]
        self.cross_diag = 0.5 * (cross + cross.T)
        parts = [self.fold(self.cross_diag)]
        ours = pl.ds(pl.multiple_of(self.hi * half, half), half)
        parts.append(0.5 * (self.dmat[n // 2, ours] + self.dx[n // 2, pl.ds(0, half)]))
        for k in range(1, n // 2):
            parts.append(0.5 * (self.dmat[k] + self.dx[k].T))
        self.cross_src[...] = jnp.concatenate(parts, axis=0).reshape(z.n_space, z.height, size)

    def send_lines(self):
        z, s, m = self.z, self.s_id, self.m_id
        self.tiny = []
        for k in range(1, z.n_space):
            to = lax.rem(s + k, z.n_space)
            self.tiny.append(
                remote(self.vec, self.vbuf.at[s], self.v_sem.at[0, k], self.v_sem.at[1, k], to, m)
            )
            self.tiny[-1].start()
        self.waits += [(copy, None) for copy in self.tiny]

    def sum_lines(self):
        self.vbuf[self.s_id] = self.vec[...]
        for copy in self.tiny:
            copy.wait_recv()
        vec = self.vbuf[0]
        for k in range(1, self.z.n_space):
            vec = vec + self.vbuf[k]
        self.vout[self.m_id] = vec
        return self.mem_send(self.vout, self.vg_sem)

    def blocks_of(self, reduction, line):
        z = self.z
        n, size = z.n_mem, z.members
        half = size // 2
        wholes = [reduction.whole(i) for i in range(n)]
        for i in range(n):
            yield i, i, self.unfold(wholes[i][:half], self.vout[i, line : line + 1, :])
        for i in range(n // 2):
            j = i + n // 2
            yield i, j, jnp.concatenate([wholes[i][half:size], wholes[j][half:size]], axis=0)
        for i in range(n):
            for k in range(1, n // 2):
                yield i, (i + k) % n, wholes[i][k * size : (k + 1) * size]


    def transform(self, scale, gram):
        z, m = self.z, self.m_id
        n, size, total = z.n_mem, z.members, z.total
        mine = self.block(m)
        col = lambda k: slice(k * size, (k + 1) * size)
        squares = jnp.zeros((size, size), F32)
        for i, j, block in self.blocks_of(gram, 3):
            if i == j:
                block = block + eye(size).astype(F32)
                squares = squares + block * block
            else:
                self.f[col(j), col(i)] = block.T
                squares = squares + 2.0 * (block * block)
            self.f[col(i), col(j)] = block
        norm = jnp.sqrt(whole_sum(squares))
        root = jnp.sqrt(norm)
        identity = eye(total).astype(F32)
        f = 1.5 * identity - (0.5 / norm) * self.f[...]
        self.f[...] = f
        self.fh[...], self.fl[...] = split(f)
        f_split = (self.fh[...], self.fl[...])
        f2 = mm3(f_split, f_split)
        self.f2h[...], self.f2l[...] = split(f2)
        g = f2 - 1.5 * self.f[...]
        self.g[...] = g
        self.gh[...], self.gl[...] = split(g)
        g_split = (self.gh[...], self.gl[...])
        yield
        p = 1.5 * self.f[...] + mm3((self.f2h[...], self.f2l[...]), g_split)
        self.s[...] = p
        p_split = split(p)
        kind = lax.broadcasted_iota(jnp.int32, (z.lines, size), 0)
        self.lines = []
        for i in range(n):
            lines = self.vout[i]
            lacks = jnp.sum(jnp.sum(lines[4 : 4 + n], axis=0, keepdims=True), axis=1, keepdims=True)
            self.lines.append(jnp.where(kind == 1, lines + lacks, jnp.where(kind == 3, 1.0, lines)))
        rows = jnp.concatenate(self.lines, axis=1)
        self.first = mm3(split(rows), p_split) / root
        second = mm3(split(self.first), p_split) / root
        self.vcol[...] = second.T
        self.pull_bar = second[1:2]
        self.pull_mine = self.vcol[mine, 1:2] - jnp.sum(self.pull_bar, axis=1, keepdims=True) / total
        mix = self.s[mine, :] / root + self.vcol[mine, 0:1] / scale
        row_weights = self.first[3:4] + jnp.sum(second[0:1], axis=1, keepdims=True) / scale
        mix = split(mix + (1.0 - row_weights) / total)
        for e in range(2, z.rows + 2):
            self.mixed[e] = mm3(mix, (self.chi[e], self.clo[e]))
        r = z.rows
        row = lambda e: self.mixed.at[e]
        bar_halo = (
            self.between(row(r + 1), row(1), row(2), row(r + 2), self.bar_halo),
            self.between(row(r), row(0), row(3), row(r + 3), self.far_halo),
        )
        self.fg[...] = mm3((self.fh[...], self.fl[...]), g_split)
        self.weigh[...] = 2.25 * identity + 4.5 * (self.fg[...] + self.f[...] - self.s[...])
        self.norm, self.root = norm, root
        for k, ref in enumerate((self.f, self.g, self.fg)):
            rows = slice(k * size, (k + 1) * size)
            self.lh[rows, :], self.ll[rows, :] = split(self.centred(ref))
        yield bar_halo

    def centred(self, ref):
        return ref[self.block(self.m_id), :] - jnp.sum(ref[...], axis=0, keepdims=True) / self.z.total

    def respond(self, scale, cross):
        z, m = self.z, self.m_id
        n, size, total = z.n_mem, z.members, z.total
        col = lambda k: slice(k * size, (k + 1) * size)
        norm, root = self.norm, self.root
        turned = [x.T for x in self.lines]
        first_t = self.first.T
        for i, j, block in self.blocks_of(cross, 2):
            block = (scale / root) * (
                block + 0.5 * (self.lines[i][4 + j : 5 + j] + turned[j][:, 4 + i : 5 + i])
            ) + (0.5 / root) * (
                turned[i][:, 1:2] * self.first[0:1, col(j)]
                + first_t[col(i), 0:1] * self.lines[j][1:2]
                + first_t[col(i), 1:2] * self.lines[j][0:1]
                + turned[i][:, 0:1] * self.first[1:2, col(j)]
            )
            self.s[col(i), col(j)] = block
            if i != j:
                self.s[col(j), col(i)] = block.T
        scale_bar = whole_sum(self.s[...] * self.weigh[...]) / norm
        self.sh[...], self.sl[...] = split(self.s[...])
        s_split = (self.sh[...], self.sl[...])
        s_mine = self.centred(self.s)
        f_split = (self.fh[...], self.fl[...])
        through = mm3((self.lh[...], self.ll[...]), s_split)
        bar = 1.5 * s_mine + through[2 * size :]
        lefts = [
            split(mm3(split(s_mine), f_split)), split(through[:size]),
            split(through[size : 2 * size]),
        ]
        rights = [(self.gh, self.gl), (self.f2h, self.f2l), (self.fh, self.fl)]
        bar = bar + mm3(
            [jnp.concatenate([x[p] for x in lefts], axis=1) for p in range(2)],
            [jnp.concatenate([x[p][...] for x in rights], axis=0) for p in range(2)],
        )
        unit = (
            lax.broadcasted_iota(jnp.int32, (size, total), 0) + m * size
            == lax.broadcasted_iota(jnp.int32, (size, total), 1)
        ).astype(F32) - 1.0 / total
        sym = 2.0 * scale_bar * (3.0 * unit - 2.0 * self.centred(self.f)) - bar / norm
        sym = sym - (scale / total) * self.pull_bar
        prec = [self.prec[...], self.aux[1, 6:7, :], self.aux[z.rows + 2, 6:7, :]]
        observed = (jnp.concatenate(prec, axis=1) / scale) * (
            mm3(split(sym), (self.ahi[...], self.alo[...])) + self.pull_mine * self.innov[0:1, :]
        )
        return observed * self.slope[...]


    def pull_back(self, src, first, dst, rows, to_sea):
        z = self.z
        for i in rows:
            e = first + i
            c = [self.aux[e, k : k + 1, :] for k in range(4)]
            lane = lax.broadcasted_iota(jnp.int32, (1, z.cols), 1)
            keep = 1.0 - c[0] - c[1] - c[2] - c[3]
            from_south, from_north = self.aux[e + 1, 0:1, :], self.aux[e - 1, 1:2, :]
            sea = self.aux[e, 4:5, :]
            east = pltpu.roll(jnp.broadcast_to(jnp.where(lane == 0, 0.0, c[2]), (8, z.cols)), z.cols - 1, 1)[:1]
            west = pltpu.roll(jnp.broadcast_to(jnp.where(lane == z.cols - 1, 0.0, c[3]), (8, z.cols)), 1, 1)[:1]
            if to_sea:
                keep, from_south, from_north = sea * keep, sea * from_south, sea * from_north
                east, west = sea * east, sea * west
            for part in self.chunks():
                v = src[i + 1, part, :]
                dst[i, part, :] = (
                    keep * v
                    + from_south * src[i + 2, part, :]
                    + from_north * src[i, part, :]
                    + east * pltpu.roll(v, z.cols - 1, 1)
                    + west * pltpu.roll(v, 1, 1)
                )

    def coefficient_terms(self, weight, w0, field, f0, which):
        z = self.z
        lane = lax.broadcasted_iota(jnp.int32, (1, z.cols), 1)
        rows = {}
        for r in which:
            sums = [0.0] * 5
            for part in self.chunks():
                w = weight[w0 + r, part, :]
                c = field[f0 + r, part, :]
                terms = [
                    w * field[f0 + r - 1, part, :],
                    w * field[f0 + r + 1, part, :],
                    w * pltpu.roll(c, 1, 1),
                    w * pltpu.roll(c, z.cols - 1, 1),
                    w * c,
                ]
                sums = [x + y for x, y in zip(sums, terms)]
            north, south, west, east, own = [jnp.sum(x, axis=0, keepdims=True) for x in sums]
            west = jnp.where(lane == 0, 0.0, west)
            east = jnp.where(lane == z.cols - 1, 0.0, east)
            rows[r] = [north - own, south - own, west - own, east - own]
        return rows


def kernel(z, *refs):
    small = ["stencil", "sea", "sites", "data", "prec"]
    names = ["prior", "cot"] + [name + "_in" for name in small] + ["grad", "coef"]
    names += list(scratch_of(z))
    g = Step(z, dict(zip(names, refs)))
    scale = jnp.sqrt(jnp.float32(z.total - 1))
    s, m = g.s_id, g.m_id
    r, ext = z.rows, z.rows + 4
    mine = g.block(m)

    entered = g.barrier()
    loads = []
    for i in range(r):
        loads.append(pltpu.make_async_copy(g.prior.at[:, i], g.pext.at[2 + i], g.own.at[0, i]))
    for i in range(r):
        loads.append(pltpu.make_async_copy(g.cot.at[:, i], g.cotf.at[2 + i, mine], g.own.at[1, i]))
    few = [
        pltpu.make_async_copy(getattr(g, name + "_in"), getattr(g, name), g.few.at[i])
        for i, name in enumerate(small)
    ]
    for copy in loads[:r] + few + loads[r:]:
        copy.start()
    for copy in few:
        copy.wait()
    for i in range(r):
        g.aux[2 + i, 0:4, :] = g.stencil[:, i, :]
        g.aux[2 + i, 4:5, :] = g.sea[i : i + 1, :].astype(F32)
        g.aux[2 + i, 5:6, :] = g.sites[...].astype(F32)
        g.aux[2 + i, 6:7, :] = g.prec[...]
        g.aux[2 + i, 7:8, :] = g.data[...]
    for e, edge in ((0, 0), (1, 0), (ext - 2, z.n_space - 1), (ext - 1, z.n_space - 1)):
        @pl.when(s == edge)
        def _():
            g.pext[e] = jnp.zeros((z.members, z.cols), F32)
            g.mixed[e] = jnp.zeros((z.members, z.cols), F32)
            g.aux[e] = jnp.zeros((8, z.cols), F32)
            g.beside_seen[0 if e < 2 else 1, m] = jnp.zeros((z.members, z.sites), F32)
    for copy in loads[:r]:
        copy.wait()
    entered()
    halo = g.halo_send(g.pext, g.halo)
    if z.rounds:
        g.vouch(1)
    for copy in loads[r:]:
        copy.wait()
    cot_forward, cot_wait = g.pair_gather(lambda which: g.cotf.at[pl.ds(2, r), g.block(which)], g.cot_sem)
    aux_halo = g.halo_send(g.aux, g.aux_halo)
    g.mark_sites()
    aux_halo()
    g.mark_sites_beside()
    cot_forward()
    for k in range(1, z.rounds):
        g.hear(k)
        g.vouch(k + 1)
    halo()

    g.advance(g.pext, 1, g.fext, r + 2)
    g.advance(g.fext, 2, g.state, r)
    g.obsf[m] = g.observe()
    obs_wait = g.mem_send(g.obsf, g.obs_sem)
    own_sums = [jnp.sum(g.state[i], axis=0, keepdims=True) for i in range(r)]
    padding = [jnp.zeros((-r % 8, z.cols), F32)] * (r % 8 > 0)
    g.sums[m] = jnp.concatenate(own_sums + padding, axis=0)
    sums_wait = g.mem_send(g.sums, g.sum_sem)
    seen_halo = g.between(
        g.seen, g.beside_seen.at[0, m], g.seen, g.beside_seen.at[1, m], g.seen_halo
    )
    cot_wait()
    for e in range(2, r + 2):
        g.chi[e], g.clo[e] = split(g.cotf[e])
    dev = [split((g.state[i] - own_sums[i] / z.members) / scale) for i in range(r)]
    mean_bar = g.cross_rows(dev)
    obs_wait()
    mean, diag = g.pack_gram(scale)
    if z.rounds:
        g.hear(z.rounds)
    gram, cross = Reduction(g, "gram"), Reduction(g, "cross")
    gram.scatter()
    g.pack_cross()
    cross.scatter()
    sums_wait()
    g.pack_lines(scale, mean_bar, own_sums, mean, diag)
    g.send_lines()
    seen_halo()
    extras = [
        g.pair_gather(lambda which: g.beside_seen.at[:, which], g.seen_sem),
    ]
    gram.start()
    cross.start()
    lines_wait = g.sum_lines()
    for forward, _ in extras:
        forward()
    gram.forward_all()
    cross.forward_all()
    for _, wait in extras:
        wait()
    g.observe_beside()
    gram.pass_on()
    lines_wait()
    gram.finish()
    parts = g.transform(scale, gram)
    next(parts)
    cross.pass_on()
    bar_halo = next(parts)
    cross.finish()
    g.picked[...] = g.respond(scale, cross)
    g.spread(0, range(2, r + 2))
    second = g.coefficient_terms(g.sbext, 2, g.fext, 1, range(r))
    g.pull_back(g.sbext, 1, g.fbar, range(2, r), True)
    firsts = g.coefficient_terms(g.fbar, 1, g.pext, 2, range(1, r - 1))
    bar_halo[0]()
    g.spread(1, (1,))
    g.spread(2, (r + 2,))
    outer = (0, r - 1) if r > 1 else (0,)
    g.pull_back(g.sbext, 1, g.fbar, [i + 1 for i in outer], True)
    firsts.update(g.coefficient_terms(g.fbar, 1, g.pext, 2, outer))
    g.cbuf[m] = jnp.concatenate(
        [second[i][k] + firsts[i][k] for k in range(4) for i in range(r)], axis=0
    )
    c_wait = g.mem_send(g.cbuf, g.c_sem)
    bar_halo[1]()
    g.spread(1, (0,))
    g.spread(2, (r + 3,))
    g.pull_back(g.sbext, 1, g.fbar, (0, r + 1), True)
    g.pull_back(g.fbar, 2, g.grad, range(r), False)
    c_wait()
    both = g.cbuf[0]
    for k in range(1, z.n_mem):
        both = both + g.cbuf[k]
    for k in range(4):
        g.coef[k] = both[k * r : (k + 1) * r]
    g.finish_sends()


def place(z, last, sums, grad, coef, scaled, sem):
    stores = [pltpu.make_async_copy(last.at[i], grad.at[:, i], sem.at[i]) for i in range(z.rows)]
    for copy in stores:
        copy.start()
    scaled[...] = sums[...] / jnp.sqrt(jnp.float32(z.total))
    stores.append(pltpu.make_async_copy(scaled, coef, sem.at[z.rows]))
    stores[-1].start()
    for copy in stores:
        copy.wait()


def local(n_space, n_mem, prior, stencil, sea_mask, sites, data, precision, cotangent):
    z = Sizes(n_space, n_mem, prior, sites)
    any_spec = pl.BlockSpec(memory_space=pl.ANY)
    turned = (z.rows, z.members, z.cols)
    factors = (4, z.rows, z.cols)
    inputs = (prior, cotangent, stencil, sea_mask, sites, data[None], precision[None])
    last, sums = pl.pallas_call(
        functools.partial(kernel, z),
        out_shape=(jax.ShapeDtypeStruct(turned, F32), jax.ShapeDtypeStruct(factors, F32)),
        in_specs=[pl.BlockSpec(memory_space=pltpu.HBM)] * 7,
        out_specs=(VMEM_SPEC, VMEM_SPEC),
        scratch_shapes=list(scratch_of(z).values()),
        compiler_params=pltpu.CompilerParams(
            collective_id=1, has_side_effects=True, vmem_limit_bytes=GRANT
        ),
        name="adjoint",
    )(*[pltpu.with_memory_space_constraint(x, pltpu.HBM) for x in inputs])
    return pl.pallas_call(
        functools.partial(place, z),
        out_shape=(jax.ShapeDtypeStruct(prior.shape, F32), jax.ShapeDtypeStruct(factors, F32)),
        in_specs=[VMEM_SPEC, VMEM_SPEC],
        out_specs=(any_spec, any_spec),
        scratch_shapes=[pltpu.VMEM(factors, F32), pltpu.SemaphoreType.DMA((z.rows + 1,))],
        compiler_params=pltpu.CompilerParams(vmem_limit_bytes=4 * 1024 * 1024),
        name="place",
    )(last, sums)


def solution(mesh):
    placed = (
        P("mem", "space", None),
        P(None, "space", None),
        P("space", None),
        P("space", None),
        P("space"),
        P("space"),
        P("mem", "space", None),
    )
    return jax.shard_map(
        functools.partial(local, mesh.shape["space"], mesh.shape["mem"]),
        mesh=mesh,
        in_specs=placed,
        out_specs=(P("mem", "space", None), P(None, "space", None)),
        check_vma=False,
    )
```
